256 devices in a mesh: section: 128 (over z, y, x), attn: 2 (over core).
Axes of the slice: x: 4, y: 4, z: 8, core: 2. Of those that a mesh axis runs over, the one named last changes fastest.
Arguments:
- queries: bfloat16 [65536, 3072], P(('section', 'attn')), may hold values from -120 to 120
- keys: bfloat16 [65536, 1024], P(('section', 'attn')), may hold values from -2.5 to 2.5
- values: bfloat16 [65536, 1024], P(('section', 'attn')), may hold values from -4 to 4
- doc_ids: int32 [65536], replicated, may hold values from 0 to 127, never falling along the last dimension, each value on 1 to 1792 neighbouring positions
Outputs:
- attended: bfloat16 [65536, 3072], P(('section', 'attn'))
The draws below stay inside these ranges and needn't reach their ends.
Inputs may be any that keep to these rules, and one draw needn't show every extreme that they name: `doc_ids`: along the pack the document numbers never fall, and a document holds at most 1792 tokens.
All inputs are finite; a program needn't handle non-finite values.
Results may differ from the reference program's by a relative error of at most 0.0028.
Values may be sent and summed in bfloat16 or wider, within the bound.
A program may use at most 64 MiB of HBM per device.

```python
import math
import jax
import jax.numpy as jnp
import numpy as np
from jax import lax

D = 3072
KV_HEADS = 8
HEAD_DIM = 128
TOK_DEV = 256
GROUP = 3
REACH = 8
TOKENS = 65536
DOC_MOST = 1792
DOCS = 128
DEVICES = 256


def shared_fields(key):
    base = jax.random.fold_in(key, 4242)
    pairs = TOKENS // 2
    key_base = jnp.clip(jax.random.normal(jax.random.fold_in(base, 1), (pairs, 2, KV_HEADS, HEAD_DIM), jnp.float32), -2.5, 2.5)
    query_base = jnp.clip(2.5 * jax.random.normal(jax.random.fold_in(base, 2), (pairs, 2, KV_HEADS, GROUP, HEAD_DIM), jnp.float32), -7.5, 7.5)
    return (key_base, query_base)


def draw_queries(key, part):
    key_base, query_base = shared_fields(key)
    chosen = query_base
    return chosen.reshape(TOKENS, KV_HEADS * GROUP * HEAD_DIM).astype(jnp.bfloat16)


def draw_keys(key, part):
    key_base, query_base = shared_fields(key)
    chosen = key_base
    return chosen.reshape(TOKENS, KV_HEADS * HEAD_DIM).astype(jnp.bfloat16)


def block_levels(key, dims, pieces, low, top_value):
    factor_of, own = 1.0, jax.random.fold_in(key, 6)
    for axis_at, shards_of in pieces:
        heights = jnp.exp(jax.random.uniform(jax.random.fold_in(own, axis_at), (shards_of,), jnp.float32, low / len(pieces), top_value / len(pieces)))
        factor_of = factor_of * jnp.repeat(heights, dims[axis_at] // shards_of).reshape([-1 if axis == axis_at else 1 for axis in range(len(dims))])
    return factor_of


def profile(number_of, total, bound, lean):
    portions = [(1 << 20) // math.isqrt(standing ** lean) + 1 for standing in range(2, number_of + 1)]
    surplus, counts = total - bound - (number_of - 1), [1] * (number_of - 1)
    while surplus > 0:
        free = [i for i in range(number_of - 1) if counts[i] < bound]
        pool, left = sum([portions[i] for i in free]), surplus
        for i in free:
            more = min(bound - counts[i], max(1, left * portions[i] // pool), surplus)
            counts[i] = counts[i] + more
            surplus = surplus - more
    return np.array([bound] + counts)


def uneven(stream_key, count, total, bound, slope):
    if count == 2:
        one = jax.random.randint(stream_key, (), max(1, total - bound), min(bound, total - 1) + 1)
        return jnp.stack([one, total - one])
    lengths = jnp.asarray(profile(count, total, bound, slope), jnp.int32)
    twos = (count - 1) // 2
    giver, sink = lengths[1:1 + 2 * twos:2], lengths[2:2 + 2 * twos:2]
    room = jnp.minimum(giver - 1, bound - sink)
    passed = jax.random.randint(jax.random.fold_in(stream_key, 1), (twos,), 0, 1 << 20) % (room + 1)
    lengths = lengths.at[1:1 + 2 * twos:2].set(giver - passed).at[2:2 + 2 * twos:2].set(sink + passed)
    return lengths[jax.random.permutation(jax.random.fold_in(stream_key, 2), count)]


def centred(key, extent, spread, reach, split=(), held_as=jnp.bfloat16):
    array = spread * jax.random.normal(key, extent, jnp.float32)
    if split:
        array = array * block_levels(key, extent, split, -0.22, 0.18)
    return jnp.clip(array, -reach, reach).astype(held_as)


def setup_inputs(seed: int = 0) -> dict:
    seeds = jax.random.split(jax.random.key(seed), 5)
    queries = draw_queries(jax.random.fold_in(seeds[4], 71), 0)
    keys = draw_keys(jax.random.fold_in(seeds[4], 71), 0)
    values = centred(seeds[2], (TOKENS, KV_HEADS * HEAD_DIM), 1.0, 4.0, ((0, 256),))
    doc_ids = jnp.searchsorted(jnp.cumsum(uneven(seeds[3], DOCS, TOKENS, DOC_MOST, 2)), jnp.arange(TOKENS), side="right").astype(jnp.int32)
    return {"queries": queries, "keys": keys, "values": values, "doc_ids": doc_ids}


def reference(queries, keys, values, doc_ids):
    span = REACH * TOK_DEV
    lead = span - TOK_DEV
    width = KV_HEADS * HEAD_DIM
    query_blocks = queries.reshape(DEVICES, TOK_DEV, KV_HEADS, GROUP, HEAD_DIM)
    padded_keys = jnp.concatenate([jnp.zeros((lead, width), keys.dtype), keys], axis=0).reshape(-1, KV_HEADS, HEAD_DIM)
    padded_values = jnp.concatenate([jnp.zeros((lead, width), values.dtype), values], axis=0).reshape(-1, KV_HEADS, HEAD_DIM)
    all_ids = doc_ids.astype(jnp.int32)
    padded_ids = jnp.concatenate([jnp.full((lead,), -1, jnp.int32), all_ids], axis=0)
    local_rows = jnp.arange(TOK_DEV, dtype=jnp.int32)
    window_rows = jnp.arange(span, dtype=jnp.int32)

    def one_block(operands):
        block_queries, block_index = operands
        first = block_index * TOK_DEV
        window_keys = lax.dynamic_slice_in_dim(padded_keys, first, span, 0)
        window_values = lax.dynamic_slice_in_dim(padded_values, first, span, 0)
        window_ids = lax.dynamic_slice_in_dim(padded_ids, first, span, 0)
        query_ids = lax.dynamic_slice_in_dim(all_ids, first, TOK_DEV, 0)
        query_pos = first + local_rows
        key_pos = first - lead + window_rows
        allowed = (key_pos[None, :] <= query_pos[:, None]) & (window_ids[None, :] == query_ids[:, None])
        scores = jnp.einsum("qgrd,kgd->grqk", block_queries.astype(jnp.float32), window_keys.astype(jnp.float32), precision=lax.Precision.HIGHEST) * (HEAD_DIM ** -0.5)
        scores = jnp.where(allowed[None, None], scores, -1e30)
        weights = jnp.exp(scores - jnp.max(scores, axis=-1, keepdims=True))
        total = jnp.sum(weights, axis=-1)
        rounded = lax.optimization_barrier(weights.astype(jnp.bfloat16)).astype(jnp.float32)
        weighted = jnp.einsum("grqk,kgd->grqd", rounded, window_values.astype(jnp.float32), precision=lax.Precision.HIGHEST)
        return (weighted / total[..., None]).astype(jnp.bfloat16).transpose(2, 0, 1, 3)

    attended = lax.map(one_block, (query_blocks, jnp.arange(DEVICES, dtype=jnp.int32)))
    return attended.reshape(TOKENS, D)
```

```python
import functools
import math

import jax
import jax.numpy as jnp
from jax import lax
from jax.experimental import pallas as pl
from jax.experimental.pallas import tpu as pltpu
from jax.sharding import PartitionSpec as P

MESH = pl.DeviceIdType.MESH
HEAD_DIM = 128
GROUP = 3
RING = 4
LANES = 128
NEG = -1e30

OWN, EXTRA, BACK1, BACK2, BACK3, RELAY = 0, 1, 2, 4, 6, 8
BLOCKS = 9
UP, RIGHT, LEFT, NEXT, PREV, SIDE_EXTRA, SIDE1, SIDE2, SIDE3 = range(9)
KINDS = 9


def attention_kernel(
    sections, rows, heads,
    q_hbm, k_hbm, v_hbm, docs_hbm, out_hbm,
    kv, q, onehot, away, docs, stat_max, acc, out,
    send_sem, recv_sem, q_sem, kv_sem, doc_sem, out_sem,
):
    half = heads // 2
    scale = math.log2(math.e) * HEAD_DIM ** (-0.5)
    s = lax.axis_index("section")
    c = lax.axis_index("attn")
    x = lax.rem(s, RING)
    row_start = s - x
    first, last = x == 0, x == RING - 1
    edge = jnp.logical_or(first, last)

    right = row_start + lax.rem(x + 1, RING)
    left = row_start + lax.rem(x + RING - 1, RING)
    up = lax.rem(s + RING, sections)
    down = lax.rem(s + sections - RING, sections)
    following = lax.rem(s + 1, sections)
    previous = lax.rem(s + sections - 1, sections)
    other = 1 - c
    up_core = jnp.where(first, other, c)

    def load_kv(j):
        at = pl.ds(pl.multiple_of(j * HEAD_DIM, HEAD_DIM), HEAD_DIM)
        return (
            pltpu.make_async_copy(k_hbm.at[:, at], kv.at[OWN, j, 0], kv_sem.at[0, j]),
            pltpu.make_async_copy(v_hbm.at[:, at], kv.at[OWN, j, 1], kv_sem.at[1, j]),
        )

    def load_q(h):
        at = pl.ds(pl.multiple_of(h * HEAD_DIM, HEAD_DIM), HEAD_DIM)
        return pltpu.make_async_copy(q_hbm.at[:, at], q.at[h], q_sem.at[h])

    def load_docs(piece):
        pair = lax.rem(lax.div(s, 2) + sections // 2 - 2 + piece, sections // 2)
        return pltpu.make_async_copy(
            docs_hbm.at[pl.ds(pl.multiple_of(pair * 8, 8), 8), :],
            docs.at[pl.ds(piece * 8, 8), :],
            doc_sem.at[piece],
        )

    @pl.loop(0, heads)
    def _(j):
        for copy in load_kv(j):
            copy.start()

    for piece in range(3):
        load_docs(piece).start()

    barrier = pltpu.get_barrier_semaphore()

    def greet(section, core):
        pl.semaphore_signal(barrier, inc=1, device_id=(section, core), device_id_type=MESH)

    greet(s, other)
    greet(right, c)
    greet(left, c)
    greet(up, up_core)
    greet(down, up_core)

    @pl.when(first)
    def _():
        greet(previous, c)

    @pl.when(last)
    def _():
        greet(following, c)

    @pl.loop(0, heads * GROUP)
    def _(h):
        load_q(h).start()

    def send(kind, j, source, target, section, core):
        return pltpu.make_async_remote_copy(
            src_ref=kv.at[source, j],
            dst_ref=kv.at[target, j],
            send_sem=send_sem.at[kind, j],
            recv_sem=recv_sem.at[target, j],
            device_id=(section, core),
            device_id_type=MESH,
        )

    def arrived(block, j):
        send(UP, j, block, block, s, other).wait_recv()

    up_target = jnp.where(first, EXTRA, RELAY)
    right_source = jnp.where(last, RELAY, OWN)
    left_source = jnp.where(first, OWN, RELAY)

    def send_up(j):
        return send(UP, j, OWN, up_target, up, up_core)

    def send_right(j):
        return send(RIGHT, j, right_source, BACK1 + c, right, c)

    def send_left(j):
        return send(LEFT, j, left_source, BACK3 + c, left, c)

    def send_next(j):
        return send(NEXT, j, BACK1 + c, BACK2 + c, following, c)

    def send_prev(j):
        return send(PREV, j, BACK3 + c, BACK2 + c, previous, c)

    def send_extra(j):
        return send(SIDE_EXTRA, j, jnp.where(c == 0, OWN, RELAY), EXTRA, s, other)

    def send_side(kind, j, block):
        return send(kind, j, block + c, block + c, s, other)

    sends_up = jnp.logical_or(x > 0, c == 1)
    sends_extra = jnp.logical_or(x > 0, c == 0)
    relays = x > 0

    @pl.loop(0, heads)
    def _(j):
        for copy in load_kv(j):
            copy.wait()

    pl.semaphore_wait(barrier, jnp.where(edge, 6, 5))

    @pl.loop(0, heads)
    def _(j):
        @pl.when(sends_up)
        def _():
            send_up(j).start()

        @pl.when(jnp.logical_not(last))
        def _():
            send_right(j).start()

        @pl.when(first)
        def _():
            send_left(j).start()

        @pl.when(c == 0)
        def _():
            send_extra(j).start()

    for piece in range(3):
        load_docs(piece).wait()
    parity = lax.rem(s, 2)
    pieces = rows // LANES
    places = ((0, c), (4 * other, other), (1, 0), (1, 1), (2, 0), (2, 1), (3, 0), (3, 1))
    ids = lax.broadcasted_iota(jnp.int32, (LANES, LANES), 0)
    for block, (back, core) in enumerate(places):
        for piece in range(pieces):
            row = (4 + parity - back) * (2 * pieces) + core * pieces + piece
            same = jnp.where(docs[pl.ds(row, 1), :] == ids, 1.0, 0.0)
            turned = jnp.transpose(same)
            onehot[block, piece * LANES:(piece + 1) * LANES, :] = turned.astype(jnp.bfloat16)
            if block == 0:
                away[piece * LANES:(piece + 1) * LANES, :] = ((1.0 - turned) * NEG).astype(jnp.bfloat16)

    @pl.loop(0, heads * GROUP)
    def _(h):
        load_q(h).wait()

    def scores(query, block, j):
        key = jnp.concatenate([kv[block, j, 0], onehot[block]], axis=1)
        return lax.dot_general(
            query, key, (((1,), (1,)), ((), ())), preferred_element_type=jnp.float32
        )

    def values_of(block, j):
        value = kv[block, j, 1]
        return jnp.concatenate([value, jnp.ones_like(value)], axis=1)

    def query_of(j, r):
        return jnp.concatenate([q[j * GROUP + r], away[...]], axis=1)

    def weigh(parts, top, blocks, j):
        total = None
        for part, block in zip(parts, blocks):
            weights = jnp.exp2((part - top) * scale).astype(jnp.bfloat16)
            product = jnp.dot(weights, values_of(block, j), preferred_element_type=jnp.float32)
            total = product if total is None else total + product
        return total

    early = (OWN, EXTRA, BACK1, BACK1 + 1, BACK3, BACK3 + 1)
    late = (BACK2, BACK2 + 1)

    def fold_early(j):
        causal = lax.broadcasted_iota(jnp.int32, (rows, rows), 1) <= lax.broadcasted_iota(
            jnp.int32, (rows, rows), 0
        )
        for r in range(GROUP):
            query = query_of(j, r)
            parts = [scores(query, block, j) for block in early]
            parts[0] = jnp.where(causal, parts[0], NEG)
            highest = functools.reduce(jnp.maximum, parts)
            top = jnp.max(highest, axis=1, keepdims=True)
            stat_max[j, r] = jnp.broadcast_to(top, (rows, LANES))
            acc[j, r] = weigh(parts, top, early, j)

    def fold_late(j):
        for r in range(GROUP):
            query = query_of(j, r)
            parts = [scores(query, block, j) for block in late]
            old = stat_max[j, r]
            highest = functools.reduce(jnp.maximum, parts)
            top = jnp.maximum(old[:, :1], jnp.max(highest, axis=1, keepdims=True))
            rescale = jnp.exp2((old[:, :1] - top) * scale)
            summed = acc[j, r] * rescale + weigh(parts, top, late, j)
            result = summed[:, :HEAD_DIM] / summed[:, HEAD_DIM:]
            out[j * GROUP + r] = result.astype(jnp.bfloat16)

    def store_out(h):
        at = pl.ds(pl.multiple_of(h * HEAD_DIM, HEAD_DIM), HEAD_DIM)
        return pltpu.make_async_copy(out.at[h], out_hbm.at[:, at], out_sem.at[h])

    shift = jnp.where(edge, 0, half)

    def pass_on(j):
        @pl.when(relays)
        def _():
            arrived(RELAY, j)
            send_left(j).start()

            @pl.when(last)
            def _():
                send_right(j).start()

            @pl.when(c == 1)
            def _():
                send_extra(j).start()

        arrived(BACK1 + c, j)
        send_side(SIDE1, j, BACK1).start()
        arrived(BACK3 + c, j)
        send_side(SIDE3, j, BACK3).start()

        @pl.when(j >= half)
        def _():
            send_next(j - shift).start()
            send_prev(j - shift).start()

    def early_ready(j):
        arrived(EXTRA, j)
        arrived(BACK1 + other, j)
        arrived(BACK3 + other, j)

    @pl.loop(0, heads + 1)
    def _(step):
        @pl.when(step < heads)
        def _():
            pass_on(step)

        @pl.when(step > 0)
        def _():
            early_ready(step - 1)
            fold_early(step - 1)

    @pl.loop(0, half)
    def _(step):
        for j in (step, step + half):
            arrived(BACK2 + c, j)
            send_side(SIDE2, j, BACK2).start()
        for j in (step, step + half):
            arrived(BACK2 + other, j)
            fold_late(j)
            for r in range(GROUP):
                store_out(j * GROUP + r).start()

    @pl.loop(0, heads)
    def _(j):
        for r in range(GROUP):
            store_out(j * GROUP + r).wait()

        @pl.when(sends_up)
        def _():
            send_up(j).wait_send()

        send_right(j).wait_send()
        send_left(j).wait_send()
        send_side(SIDE1, j, BACK1).wait_send()
        send_side(SIDE2, j, BACK2).wait_send()
        send_side(SIDE3, j, BACK3).wait_send()

        @pl.when(sends_extra)
        def _():
            send_extra(j).wait_send()

        @pl.when(j >= half)
        def _():
            send_next(j - shift).wait_send()
            send_prev(j - shift).wait_send()


def shards(sections, queries, keys, values, doc_ids):
    rows, heads = queries.shape[0], keys.shape[1] // HEAD_DIM
    docs = doc_ids.reshape(-1, LANES)
    return pl.pallas_call(
        functools.partial(attention_kernel, sections, rows, heads),
        out_shape=jax.ShapeDtypeStruct(queries.shape, jnp.bfloat16),
        in_specs=[pl.BlockSpec(memory_space=pl.ANY)] * 4,
        out_specs=pl.BlockSpec(memory_space=pl.ANY),
        scratch_shapes=[
            pltpu.VMEM((BLOCKS, heads, 2, rows, HEAD_DIM), jnp.bfloat16),
            pltpu.VMEM((heads * GROUP, rows, HEAD_DIM), jnp.bfloat16),
            pltpu.VMEM((RELAY, rows, LANES), jnp.bfloat16),
            pltpu.VMEM((rows, LANES), jnp.bfloat16),
            pltpu.VMEM((24, LANES), jnp.int32),
            pltpu.VMEM((heads, GROUP, rows, LANES), jnp.float32),
            pltpu.VMEM((heads, GROUP, rows, 2 * HEAD_DIM), jnp.float32),
            pltpu.VMEM((heads * GROUP, rows, HEAD_DIM), jnp.bfloat16),
            pltpu.SemaphoreType.DMA((KINDS, heads)),
            pltpu.SemaphoreType.DMA((BLOCKS, heads)),
            pltpu.SemaphoreType.DMA((heads * GROUP,)),
            pltpu.SemaphoreType.DMA((2, heads)),
            pltpu.SemaphoreType.DMA((3,)),
            pltpu.SemaphoreType.DMA((heads * GROUP,)),
        ],
        compiler_params=pltpu.CompilerParams(
            collective_id=0, has_side_effects=True, vmem_limit_bytes=60 * 1024 * 1024
        ),
    )(queries, keys, values, docs)


def solution(mesh):
    placed = P(("section", "attn"), None)
    return jax.shard_map(
        functools.partial(shards, mesh.shape["section"]),
        mesh=mesh,
        in_specs=(placed, placed, placed, P()),
        out_specs=placed,
        check_vma=False,
    )
```

```python
import functools
import math

import jax
import jax.numpy as jnp
from jax import lax
from jax.experimental import pallas as pl
from jax.experimental.pallas import tpu as pltpu
from jax.sharding import PartitionSpec as P

MESH = pl.DeviceIdType.MESH
HEAD_DIM = 128
GROUP = 3
RING = 4
LANES = 128
NEG = -1e30

OWN, EXTRA, BACK1, BACK2, BACK3, RELAY = 0, 1, 2, 4, 6, 8
BLOCKS = 9
UP, RIGHT, LEFT, NEXT, PREV, SIDE_EXTRA, SIDE1, SIDE2, SIDE3 = range(9)
KINDS = 9


def attention_kernel(
    sections, rows, heads,
    q_hbm, k_hbm, v_hbm, docs_hbm, out_hbm,
    kv, q, onehot, away, docs, stat_max, acc, out,
    send_sem, recv_sem, q_sem, kv_sem, doc_sem, out_sem,
):
    half = heads // 2
    scale = math.log2(math.e) * HEAD_DIM ** (-0.5)
    s = lax.axis_index("section")
    c = lax.axis_index("attn")
    x = lax.rem(s, RING)
    row_start = s - x
    first, last = x == 0, x == RING - 1
    edge = jnp.logical_or(first, last)
    top, bottom = s < RING, s >= sections - RING
    below = jnp.logical_not(top)
    from_left = jnp.where(last, half, half + 1)
    from_right = jnp.where(x == 1, half, half + 1)
    wrapped = half + 1

    right = row_start + lax.rem(x + 1, RING)
    left = row_start + lax.rem(x + RING - 1, RING)
    up = lax.rem(s + RING, sections)
    down = lax.rem(s + sections - RING, sections)
    following = lax.rem(s + 1, sections)
    previous = lax.rem(s + sections - 1, sections)
    other = 1 - c
    up_core = jnp.where(first, other, c)

    def load_kv(j):
        at = pl.ds(pl.multiple_of(j * HEAD_DIM, HEAD_DIM), HEAD_DIM)
        return (
            pltpu.make_async_copy(k_hbm.at[:, at], kv.at[OWN, j, 0], kv_sem.at[0, j]),
            pltpu.make_async_copy(v_hbm.at[:, at], kv.at[OWN, j, 1], kv_sem.at[1, j]),
        )

    def load_q(h):
        at = pl.ds(pl.multiple_of(h * HEAD_DIM, HEAD_DIM), HEAD_DIM)
        return pltpu.make_async_copy(q_hbm.at[:, at], q.at[h], q_sem.at[h])

    def load_docs(piece):
        pair = lax.rem(lax.div(s, 2) + sections // 2 - 2 + piece, sections // 2)
        return pltpu.make_async_copy(
            docs_hbm.at[pl.ds(pl.multiple_of(pair * 8, 8), 8), :],
            docs.at[pl.ds(piece * 8, 8), :],
            doc_sem.at[piece],
        )

    @pl.loop(0, heads)
    def _(j):
        for copy in load_kv(j):
            copy.start()

    for piece in range(3):
        load_docs(piece).start()

    @pl.when(top)
    def _():
        @pl.loop(EXTRA, RELAY)
        def _(block):
            @pl.loop(0, heads)
            def _(j):
                kv[block, j] = jnp.zeros((2, rows, HEAD_DIM), kv.dtype)

    up_open = jnp.logical_or(s < sections - RING, x == 1)
    down_open = jnp.logical_or(s >= RING, x == 1)

    barrier = pltpu.get_barrier_semaphore()

    def greet(section, core):
        pl.semaphore_signal(barrier, inc=1, device_id=(section, core), device_id_type=MESH)

    greet(s, other)
    greet(right, c)
    greet(left, c)
    @pl.when(up_open)
    def _():
        greet(up, up_core)

    @pl.when(down_open)
    def _():
        greet(down, up_core)

    @pl.when(first)
    def _():
        greet(previous, c)

    @pl.when(last)
    def _():
        greet(following, c)

    @pl.loop(0, heads * GROUP)
    def _(h):
        load_q(h).start()

    def send(kind, j, source, target, section, core):
        return pltpu.make_async_remote_copy(
            src_ref=kv.at[source, j],
            dst_ref=kv.at[target, j],
            send_sem=send_sem.at[kind, j],
            recv_sem=recv_sem.at[target, j],
            device_id=(section, core),
            device_id_type=MESH,
        )

    def arrived(block, j):
        send(UP, j, block, block, s, other).wait_recv()

    up_target = jnp.where(first, EXTRA, RELAY)
    right_source = jnp.where(last, RELAY, OWN)
    left_source = jnp.where(first, OWN, RELAY)

    def send_up(j):
        return send(UP, j, OWN, up_target, up, up_core)

    def send_right(j):
        return send(RIGHT, j, right_source, BACK1 + c, right, c)

    def send_left(j):
        return send(LEFT, j, left_source, BACK3 + c, left, c)

    def send_next(j):
        return send(NEXT, j, BACK1 + c, BACK2 + c, following, c)

    def send_prev(j):
        return send(PREV, j, BACK3 + c, BACK2 + c, previous, c)

    def send_extra(j):
        return send(SIDE_EXTRA, j, jnp.where(c == 0, OWN, RELAY), EXTRA, s, other)

    def send_side(kind, j, block):
        return send(kind, j, block + c, block + c, s, other)

    def both(*conditions):
        return functools.reduce(jnp.logical_and, conditions)

    def either(*conditions):
        return functools.reduce(jnp.logical_or, conditions)

    inside = jnp.logical_not(bottom)

    def sends_up(j):
        return either(both(first, c == 1, inside), both(x > 0, inside), both(x == 1, bottom, j >= wrapped))

    def has_relay(j):
        return both(x > 0, either(below, both(x == 1, j >= wrapped)))

    has1 = either(below, x > 0)
    has2 = either(below, x > 1)
    has3 = either(below, last)

    def passes3(j):
        return both(first, top, j >= wrapped)

    def has_extra():
        return either(c == 1, below)

    relays_extra = both(x > 0, below, c == 1)
    sends_next = both(has1, jnp.logical_not(both(bottom, last)))
    sends_prev = either(below, edge)

    @pl.loop(0, heads)
    def _(j):
        for copy in load_kv(j):
            copy.wait()

    pl.semaphore_wait(
        barrier,
        3 + jnp.where(edge, 1, 0) + jnp.where(up_open, 1, 0) + jnp.where(down_open, 1, 0),
    )

    @pl.loop(0, heads)
    def _(j):
        @pl.when(sends_up(j))
        def _():
            send_up(j).start()

        @pl.when(jnp.logical_not(last))
        def _():
            send_right(j).start()

        @pl.when(first)
        def _():
            send_left(j).start()

        @pl.when(c == 0)
        def _():
            send_extra(j).start()

    for piece in range(3):
        load_docs(piece).wait()
    parity = lax.rem(s, 2)
    pieces = rows // LANES
    places = ((0, c), (4 * other, other), (1, 0), (1, 1), (2, 0), (2, 1), (3, 0), (3, 1))
    ids = lax.broadcasted_iota(jnp.int32, (LANES, LANES), 0)
    for block, (back, core) in enumerate(places):
        for piece in range(pieces):
            row = (4 + parity - back) * (2 * pieces) + core * pieces + piece
            same = jnp.where(docs[pl.ds(row, 1), :] == ids, 1.0, 0.0)
            turned = jnp.transpose(same)
            onehot[block, piece * LANES:(piece + 1) * LANES, :] = turned.astype(jnp.bfloat16)
            if block == 0:
                away[piece * LANES:(piece + 1) * LANES, :] = ((1.0 - turned) * NEG).astype(jnp.bfloat16)

    @pl.loop(0, heads * GROUP)
    def _(h):
        load_q(h).wait()

    def scores(query, block, j):
        key = jnp.concatenate([kv[block, j, 0], onehot[block]], axis=1)
        return lax.dot_general(
            query, key, (((1,), (1,)), ((), ())), preferred_element_type=jnp.float32
        )

    def values_of(block, j):
        value = kv[block, j, 1]
        return jnp.concatenate([value, jnp.ones_like(value)], axis=1)

    def query_of(j, r):
        return jnp.concatenate([q[j * GROUP + r], away[...]], axis=1)

    def weigh(parts, top, blocks, j):
        total = None
        for part, block in zip(parts, blocks):
            weights = jnp.exp2((part - top) * scale).astype(jnp.bfloat16)
            product = jnp.dot(weights, values_of(block, j), preferred_element_type=jnp.float32)
            total = product if total is None else total + product
        return total

    early = (OWN, EXTRA, BACK1, BACK1 + 1, BACK3, BACK3 + 1)
    late = (BACK2, BACK2 + 1)

    def fold_early(j):
        causal = lax.broadcasted_iota(jnp.int32, (rows, rows), 1) <= lax.broadcasted_iota(
            jnp.int32, (rows, rows), 0
        )
        for r in range(GROUP):
            query = query_of(j, r)
            parts = [scores(query, block, j) for block in early]
            parts[0] = jnp.where(causal, parts[0], NEG)
            highest = functools.reduce(jnp.maximum, parts)
            top = jnp.max(highest, axis=1, keepdims=True)
            stat_max[j, r] = jnp.broadcast_to(top, (rows, LANES))
            acc[j, r] = weigh(parts, top, early, j)

    def fold_late(j):
        for r in range(GROUP):
            query = query_of(j, r)
            parts = [scores(query, block, j) for block in late]
            old = stat_max[j, r]
            highest = functools.reduce(jnp.maximum, parts)
            top = jnp.maximum(old[:, :1], jnp.max(highest, axis=1, keepdims=True))
            rescale = jnp.exp2((old[:, :1] - top) * scale)
            summed = acc[j, r] * rescale + weigh(parts, top, late, j)
            result = summed[:, :HEAD_DIM] / summed[:, HEAD_DIM:]
            out[j * GROUP + r] = result.astype(jnp.bfloat16)

    def store_out(h):
        at = pl.ds(pl.multiple_of(h * HEAD_DIM, HEAD_DIM), HEAD_DIM)
        return pltpu.make_async_copy(out.at[h], out_hbm.at[:, at], out_sem.at[h])

    def pass_relay(j):
        @pl.when(has_relay(j))
        def _():
            arrived(RELAY, j)
            send_left(j).start()

        @pl.when(both(last, below))
        def _():
            send_right(j).start()

        @pl.when(relays_extra)
        def _():
            send_extra(j).start()

    def pass_aside(j):
        @pl.when(has1)
        def _():
            arrived(BACK1 + c, j)
            send_side(SIDE1, j, BACK1).start()

        @pl.when(has3)
        def _():
            arrived(BACK3 + c, j)
            send_side(SIDE3, j, BACK3).start()

        @pl.when(passes3(j))
        def _():
            arrived(BACK3 + c, j)

    def next_range(step):
        low = jnp.where(last, 0, 2 * (step - (heads - 2)))
        high = jnp.where(last, from_left, jnp.minimum(low + 2, from_left))
        return both(sends_next, step >= jnp.where(last, heads, heads - 2), step <= heads), low, high

    def prev_range(step):
        low = jnp.where(step == heads, from_right, heads - 1)
        high = jnp.where(step == heads, heads - 1, heads)
        return both(sends_prev, step >= heads, step <= heads + 1), low, high

    def early_ready(j):
        @pl.when(has_extra())
        def _():
            arrived(EXTRA, j)

        @pl.when(has1)
        def _():
            arrived(BACK1 + other, j)

        @pl.when(has3)
        def _():
            arrived(BACK3 + other, j)

    @pl.loop(0, heads + 3)
    def _(step):
        @pl.when(step < heads)
        def _():
            pass_relay(step)

        @pl.when(both(step >= 2, step < heads + 2))
        def _():
            pass_aside(step - 2)

        sending, low, high = next_range(step)

        @pl.when(sending)
        def _():
            @pl.loop(low, high)
            def _(j):
                send_next(j).start()

        sending, low, high = prev_range(step)

        @pl.when(sending)
        def _():
            @pl.loop(low, high)
            def _(j):
                send_prev(j).start()

        @pl.when(step >= 3)
        def _():
            early_ready(step - 3)
            fold_early(step - 3)

    def late_head(k):
        odd = lax.rem(k, 2)
        evenly = half * odd + lax.div(k, 2)
        left_first = jnp.where(
            odd == 1, lax.div(k + 1, 2), jnp.where(k == 0, 0, half + lax.div(k, 2))
        )
        return jnp.where(first, evenly, left_first)

    def pass_late(k):
        @pl.when(has2)
        def _():
            j = late_head(k)
            arrived(BACK2 + c, j)
            send_side(SIDE2, j, BACK2).start()

    pass_late(0)

    @pl.loop(0, heads)
    def _(k):
        @pl.when(k + 1 < heads)
        def _():
            pass_late(k + 1)

        j = late_head(k)

        @pl.when(has2)
        def _():
            arrived(BACK2 + other, j)

        fold_late(j)
        for r in range(GROUP):
            store_out(j * GROUP + r).start()

    @pl.loop(0, heads)
    def _(j):
        for r in range(GROUP):
            store_out(j * GROUP + r).wait()

        @pl.when(sends_up(j))
        def _():
            send_up(j).wait_send()

        @pl.when(either(jnp.logical_not(last), below))
        def _():
            send_right(j).wait_send()

        @pl.when(either(first, has_relay(j)))
        def _():
            send_left(j).wait_send()

        @pl.when(has1)
        def _():
            send_side(SIDE1, j, BACK1).wait_send()

        @pl.when(has2)
        def _():
            send_side(SIDE2, j, BACK2).wait_send()

        @pl.when(has3)
        def _():
            send_side(SIDE3, j, BACK3).wait_send()

        @pl.when(either(c == 0, relays_extra))
        def _():
            send_extra(j).wait_send()

        @pl.when(both(sends_next, j < from_left))
        def _():
            send_next(j).wait_send()

        @pl.when(both(sends_prev, j >= from_right))
        def _():
            send_prev(j).wait_send()


def shards(sections, queries, keys, values, doc_ids):
    rows, heads = queries.shape[0], keys.shape[1] // HEAD_DIM
    docs = doc_ids.reshape(-1, LANES)
    return pl.pallas_call(
        functools.partial(attention_kernel, sections, rows, heads),
        out_shape=jax.ShapeDtypeStruct(queries.shape, jnp.bfloat16),
        in_specs=[pl.BlockSpec(memory_space=pltpu.HBM)] * 4,
        out_specs=pl.BlockSpec(memory_space=pl.ANY),
        scratch_shapes=[
            pltpu.VMEM((BLOCKS, heads, 2, rows, HEAD_DIM), jnp.bfloat16),
            pltpu.VMEM((heads * GROUP, rows, HEAD_DIM), jnp.bfloat16),
            pltpu.VMEM((RELAY, rows, LANES), jnp.bfloat16),
            pltpu.VMEM((rows, LANES), jnp.bfloat16),
            pltpu.VMEM((24, LANES), jnp.int32),
            pltpu.VMEM((heads, GROUP, rows, LANES), jnp.float32),
            pltpu.VMEM((heads, GROUP, rows, 2 * HEAD_DIM), jnp.float32),
            pltpu.VMEM((heads * GROUP, rows, HEAD_DIM), jnp.bfloat16),
            pltpu.SemaphoreType.DMA((KINDS, heads)),
            pltpu.SemaphoreType.DMA((BLOCKS, heads)),
            pltpu.SemaphoreType.DMA((heads * GROUP,)),
            pltpu.SemaphoreType.DMA((2, heads)),
            pltpu.SemaphoreType.DMA((3,)),
            pltpu.SemaphoreType.DMA((heads * GROUP,)),
        ],
        compiler_params=pltpu.CompilerParams(
            collective_id=0, has_side_effects=True, vmem_limit_bytes=40 * 1024 * 1024
        ),
    )(queries, keys, values, docs)


def solution(mesh):
    placed = P(("section", "attn"), None)
    return jax.shard_map(
        functools.partial(shards, mesh.shape["section"]),
        mesh=mesh,
        in_specs=(placed, placed, placed, P()),
        out_specs=placed,
        check_vma=False,
    )
```

```python
import functools
import math

import jax
import jax.numpy as jnp
from jax import lax
from jax.experimental import pallas as pl
from jax.experimental.pallas import tpu as pltpu
from jax.sharding import PartitionSpec as P

MESH = pl.DeviceIdType.MESH
HEAD_DIM = 128
GROUP = 3
RING = 4
LANES = 128
NEG = -1e30

OWN, EXTRA, BACK1, BACK2, BACK3, RELAY, RELAY2 = 0, 1, 2, 4, 6, 8, 9
BLOCKS = 10
UP, RIGHT, LEFT, NEXT, PREV, SIDE_EXTRA, SIDE1, SIDE2, SIDE3, ROUND = range(10)
KINDS = 10


def attention_kernel(
    sections, rows, heads,
    q_hbm, k_hbm, v_hbm, docs_hbm, out_hbm,
    kv, q, onehot, away, docs, stat_max, acc, out,
    send_sem, recv_sem, q_sem, kv_sem, doc_sem, out_sem,
):
    half = heads // 2
    scale = math.log2(math.e) * HEAD_DIM ** (-0.5)
    s = lax.axis_index("section")
    c = lax.axis_index("attn")
    x = lax.rem(s, RING)
    row_start = s - x
    first, last = x == 0, x == RING - 1
    edge = jnp.logical_or(first, last)
    top, bottom = s < RING, s >= sections - RING
    below = jnp.logical_not(top)
    from_left = jnp.where(last, half, half + 1)
    from_right = jnp.where(x == 1, half, half + 1)
    wrapped = half + 1

    right = row_start + lax.rem(x + 1, RING)
    left = row_start + lax.rem(x + RING - 1, RING)
    up = lax.rem(s + RING, sections)
    down = lax.rem(s + sections - RING, sections)
    following = lax.rem(s + 1, sections)
    previous = lax.rem(s + sections - 1, sections)
    other = 1 - c
    up_core = jnp.where(first, other, c)

    def load_kv(j):
        at = pl.ds(pl.multiple_of(j * HEAD_DIM, HEAD_DIM), HEAD_DIM)
        return (
            pltpu.make_async_copy(k_hbm.at[:, at], kv.at[OWN, j, 0], kv_sem.at[0, j]),
            pltpu.make_async_copy(v_hbm.at[:, at], kv.at[OWN, j, 1], kv_sem.at[1, j]),
        )

    def load_q(h):
        at = pl.ds(pl.multiple_of(h * HEAD_DIM, HEAD_DIM), HEAD_DIM)
        return pltpu.make_async_copy(q_hbm.at[:, at], q.at[h], q_sem.at[h])

    def load_docs(piece):
        pair = lax.rem(lax.div(s, 2) + sections // 2 - 2 + piece, sections // 2)
        return pltpu.make_async_copy(
            docs_hbm.at[pl.ds(pl.multiple_of(pair * 8, 8), 8), :],
            docs.at[pl.ds(piece * 8, 8), :],
            doc_sem.at[piece],
        )

    @pl.loop(0, heads)
    def _(j):
        for copy in load_kv(j):
            copy.start()

    for piece in range(3):
        load_docs(piece).start()

    @pl.when(top)
    def _():
        @pl.loop(EXTRA, RELAY)
        def _(block):
            @pl.loop(0, heads)
            def _(j):
                kv[block, j] = jnp.zeros((2, rows, HEAD_DIM), kv.dtype)

    up_open = jnp.logical_or(s < sections - RING, x == 1)
    down_open = jnp.logical_or(s >= RING, x == 1)

    barrier = pltpu.get_barrier_semaphore()

    def greet(section, core):
        pl.semaphore_signal(barrier, inc=1, device_id=(section, core), device_id_type=MESH)

    greet(s, other)
    greet(right, c)
    greet(left, c)
    @pl.when(up_open)
    def _():
        greet(up, up_core)

    @pl.when(down_open)
    def _():
        greet(down, up_core)

    @pl.when(first)
    def _():
        greet(previous, c)

    @pl.when(last)
    def _():
        greet(following, c)

    @pl.loop(0, heads * GROUP)
    def _(h):
        load_q(h).start()

    def send(kind, j, source, target, section, core):
        return pltpu.make_async_remote_copy(
            src_ref=kv.at[source, j],
            dst_ref=kv.at[target, j],
            send_sem=send_sem.at[kind, j],
            recv_sem=recv_sem.at[target, j],
            device_id=(section, core),
            device_id_type=MESH,
        )

    def arrived(block, j):
        send(UP, j, block, block, s, other).wait_recv()

    up_target = jnp.where(first, EXTRA, RELAY)
    right_source = jnp.where(last, RELAY, OWN)
    left_source = jnp.where(first, OWN, RELAY)

    def send_up(j):
        return send(UP, j, OWN, up_target, up, up_core)

    def send_right(j):
        return send(RIGHT, j, right_source, BACK1 + c, right, c)

    def send_left(j):
        return send(LEFT, j, left_source, BACK3 + c, left, c)

    def send_next(j):
        target = jnp.where(last, RELAY2, BACK2 + c)
        return send(NEXT, j, BACK1 + c, target, jnp.where(last, up, following), c)

    def send_round(j):
        return send(ROUND, j, RELAY2, BACK2 + c, right, c)

    def send_prev(j):
        return send(PREV, j, BACK3 + c, BACK2 + c, previous, c)

    def send_extra(j):
        return send(SIDE_EXTRA, j, jnp.where(c == 0, OWN, RELAY), EXTRA, s, other)

    def send_side(kind, j, block):
        return send(kind, j, block + c, block + c, s, other)

    def both(*conditions):
        return functools.reduce(jnp.logical_and, conditions)

    def either(*conditions):
        return functools.reduce(jnp.logical_or, conditions)

    inside = jnp.logical_not(bottom)

    def sends_up(j):
        return either(both(first, c == 1, inside), both(x > 0, inside), both(x == 1, bottom, j >= wrapped))

    def has_relay(j):
        return both(x > 0, either(below, both(x == 1, j >= wrapped)))

    has1 = either(below, x > 0)
    has2 = either(below, x > 1)
    has3 = either(below, last)

    def passes3(j):
        return both(first, top, j >= wrapped)

    def has_extra():
        return either(c == 1, below)

    relays_extra = both(x > 0, below, c == 1)
    sends_next = both(has1, jnp.logical_not(both(bottom, last)))
    sends_prev = either(below, edge)

    @pl.loop(0, heads)
    def _(j):
        for copy in load_kv(j):
            copy.wait()

    pl.semaphore_wait(
        barrier,
        3 + jnp.where(edge, 1, 0) + jnp.where(up_open, 1, 0) + jnp.where(down_open, 1, 0),
    )

    @pl.loop(0, heads)
    def _(j):
        @pl.when(sends_up(j))
        def _():
            send_up(j).start()

        @pl.when(jnp.logical_not(last))
        def _():
            send_right(j).start()

        @pl.when(first)
        def _():
            send_left(j).start()

        @pl.when(c == 0)
        def _():
            send_extra(j).start()

    for piece in range(3):
        load_docs(piece).wait()
    parity = lax.rem(s, 2)
    pieces = rows // LANES
    places = ((0, c), (4 * other, other), (1, 0), (1, 1), (2, 0), (2, 1), (3, 0), (3, 1))
    ids = lax.broadcasted_iota(jnp.int32, (LANES, LANES), 0)
    for block, (back, core) in enumerate(places):
        for piece in range(pieces):
            row = (4 + parity - back) * (2 * pieces) + core * pieces + piece
            same = jnp.where(docs[pl.ds(row, 1), :] == ids, 1.0, 0.0)
            span = slice(piece * LANES, (piece + 1) * LANES)
            onehot[block, :, span] = same.astype(jnp.bfloat16)
            if block == OWN:
                away[span, :] = jnp.transpose((1.0 - same) * NEG).astype(jnp.bfloat16)

    @pl.loop(0, heads * GROUP)
    def _(h):
        load_q(h).wait()

    def keys_of(block, j):
        return jnp.concatenate([jnp.transpose(kv[block, j, 0]), onehot[block]], axis=0)

    def scores(query, key):
        return jnp.dot(query, key, preferred_element_type=jnp.float32)

    def wide(column):
        return jnp.concatenate([column] * (rows // LANES), axis=1)

    def values_of(block, j):
        value = kv[block, j, 1]
        return jnp.concatenate([value, jnp.ones_like(value)], axis=1)

    def query_of(j, r):
        return jnp.concatenate([q[j * GROUP + r], away[...]], axis=1)

    def weigh(parts, top, blocks, j):
        total = None
        for part, block in zip(parts, blocks):
            weights = jnp.exp2((part - top) * scale).astype(jnp.bfloat16)
            product = jnp.dot(weights, values_of(block, j), preferred_element_type=jnp.float32)
            total = product if total is None else total + product
        return total

    early = (OWN, EXTRA, BACK1, BACK1 + 1, BACK3, BACK3 + 1)
    late = (BACK2, BACK2 + 1)
    causal = lax.broadcasted_iota(jnp.int32, (rows, rows), 1) <= lax.broadcasted_iota(
        jnp.int32, (rows, rows), 0
    )

    def row_max(parts):
        return jnp.broadcast_to(
            jnp.max(functools.reduce(jnp.maximum, parts), axis=1, keepdims=True), (rows, LANES)
        )

    def finish_late(j, r, parts):
        old = stat_max[j, r]
        top = jnp.maximum(old, row_max(parts))
        rescale = jnp.exp2((old - top) * scale)
        summed = acc[j, r] * wide(rescale) + weigh(parts, wide(top), late, j)
        out[j * GROUP + r] = (summed[:, :HEAD_DIM] / summed[:, HEAD_DIM:]).astype(jnp.bfloat16)

    def finish_early(j, r, parts):
        parts[0] = jnp.where(causal, parts[0], NEG)
        top = row_max(parts)
        stat_max[j, r] = top
        acc[j, r] = weigh(parts, wide(top), early, j)

    def all_scores(blocks, j):
        query = jnp.concatenate([query_of(j, r) for r in range(GROUP)], axis=0)
        whole = [scores(query, key) for key in [keys_of(block, j) for block in blocks]]
        return [[part[r * rows:(r + 1) * rows] for part in whole] for r in range(GROUP)]

    def fold_early(j):
        for r, parts in enumerate(all_scores(early, j)):
            finish_early(j, r, parts)

    def fold_late(j):
        for r, parts in enumerate(all_scores(late, j)):
            finish_late(j, r, parts)

    def store_out(h):
        at = pl.ds(pl.multiple_of(h * HEAD_DIM, HEAD_DIM), HEAD_DIM)
        return pltpu.make_async_copy(out.at[h], out_hbm.at[:, at], out_sem.at[h])

    def pass_relay(j):
        @pl.when(has_relay(j))
        def _():
            arrived(RELAY, j)
            send_left(j).start()

        @pl.when(both(last, below))
        def _():
            send_right(j).start()

        @pl.when(relays_extra)
        def _():
            send_extra(j).start()

    def pass_aside(j):
        @pl.when(has1)
        def _():
            arrived(BACK1 + c, j)
            send_side(SIDE1, j, BACK1).start()

        @pl.when(has3)
        def _():
            arrived(BACK3 + c, j)
            send_side(SIDE3, j, BACK3).start()

        @pl.when(passes3(j))
        def _():
            arrived(BACK3 + c, j)

    def next_range(step):
        low = 2 * (step - (heads - 2))
        high = jnp.minimum(low + 2, from_left)
        return both(sends_next, step >= heads - 2, step <= heads), low, high

    rounds = both(last, below)

    def pass_round(j):
        arrived(RELAY2, j)
        send_round(j).start()

    def prev_range(step):
        low = jnp.where(step == heads, from_right, heads - 1)
        high = jnp.where(step == heads, heads - 1, heads)
        return both(sends_prev, step >= heads, step <= heads + 1), low, high

    def early_ready(j):
        @pl.when(has_extra())
        def _():
            arrived(EXTRA, j)

        @pl.when(has1)
        def _():
            arrived(BACK1 + other, j)

        @pl.when(has3)
        def _():
            arrived(BACK3 + other, j)

    @pl.loop(0, heads + 3)
    def _(step):
        @pl.when(step < heads)
        def _():
            pass_relay(step)

        @pl.when(both(step >= 2, step < heads + 2))
        def _():
            pass_aside(step - 2)

        sending, low, high = next_range(step)

        @pl.when(sending)
        def _():
            @pl.loop(low, high)
            def _(j):
                send_next(j).start()

        sending, low, high = prev_range(step)

        @pl.when(sending)
        def _():
            @pl.loop(low, high)
            def _(j):
                send_prev(j).start()

        @pl.when(both(rounds, step > heads))
        def _():
            pass_round(step - (heads + 1))

        @pl.when(step >= 3)
        def _():
            early_ready(step - 3)
            fold_early(step - 3)

    def late_head(k):
        odd = lax.rem(k, 2)
        evenly = half * odd + lax.div(k, 2)
        left_first = jnp.where(
            odd == 1, lax.div(k + 1, 2), jnp.where(k == 0, 0, half + lax.div(k, 2))
        )
        return jnp.where(first, evenly, left_first)

    def pass_late(k):
        @pl.when(has2)
        def _():
            j = late_head(k)
            arrived(BACK2 + c, j)
            send_side(SIDE2, j, BACK2).start()

    pass_late(0)

    @pl.loop(0, heads)
    def _(k):
        @pl.when(both(rounds, either(k == 0, k == 2)))
        def _():
            pass_round(2 + lax.div(k, 2))

        @pl.when(k + 1 < heads)
        def _():
            pass_late(k + 1)

        j = late_head(k)

        @pl.when(has2)
        def _():
            arrived(BACK2 + other, j)

        fold_late(j)
        for r in range(GROUP):
            store_out(j * GROUP + r).start()

    @pl.loop(0, heads)
    def _(j):
        for r in range(GROUP):
            store_out(j * GROUP + r).wait()

        @pl.when(sends_up(j))
        def _():
            send_up(j).wait_send()

        @pl.when(either(jnp.logical_not(last), below))
        def _():
            send_right(j).wait_send()

        @pl.when(either(first, has_relay(j)))
        def _():
            send_left(j).wait_send()

        @pl.when(has1)
        def _():
            send_side(SIDE1, j, BACK1).wait_send()

        @pl.when(has2)
        def _():
            send_side(SIDE2, j, BACK2).wait_send()

        @pl.when(has3)
        def _():
            send_side(SIDE3, j, BACK3).wait_send()

        @pl.when(either(c == 0, relays_extra))
        def _():
            send_extra(j).wait_send()

        @pl.when(both(sends_next, j < from_left))
        def _():
            send_next(j).wait_send()

        @pl.when(both(rounds, j < half))
        def _():
            send_round(j).wait_send()

        @pl.when(both(sends_prev, j >= from_right))
        def _():
            send_prev(j).wait_send()


def shards(sections, queries, keys, values, doc_ids):
    rows, heads = queries.shape[0], keys.shape[1] // HEAD_DIM
    docs = doc_ids.reshape(-1, LANES)
    return pl.pallas_call(
        functools.partial(attention_kernel, sections, rows, heads),
        out_shape=jax.ShapeDtypeStruct(queries.shape, jnp.bfloat16),
        in_specs=[pl.BlockSpec(memory_space=pltpu.HBM)] * 4,
        out_specs=pl.BlockSpec(memory_space=pl.ANY),
        scratch_shapes=[
            pltpu.VMEM((BLOCKS, heads, 2, rows, HEAD_DIM), jnp.bfloat16),
            pltpu.VMEM((heads * GROUP, rows, HEAD_DIM), jnp.bfloat16),
            pltpu.VMEM((RELAY, LANES, rows), jnp.bfloat16),
            pltpu.VMEM((rows, LANES), jnp.bfloat16),
            pltpu.VMEM((24, LANES), jnp.int32),
            pltpu.VMEM((heads, GROUP, rows, LANES), jnp.float32),
            pltpu.VMEM((heads, GROUP, rows, 2 * HEAD_DIM), jnp.float32),
            pltpu.VMEM((heads * GROUP, rows, HEAD_DIM), jnp.bfloat16),
            pltpu.SemaphoreType.DMA((KINDS, heads)),
            pltpu.SemaphoreType.DMA((BLOCKS, heads)),
            pltpu.SemaphoreType.DMA((heads * GROUP,)),
            pltpu.SemaphoreType.DMA((2, heads)),
            pltpu.SemaphoreType.DMA((3,)),
            pltpu.SemaphoreType.DMA((heads * GROUP,)),
        ],
        compiler_params=pltpu.CompilerParams(
            collective_id=0, has_side_effects=True, vmem_limit_bytes=40 * 1024 * 1024
        ),
    )(*[pltpu.with_memory_space_constraint(a, pltpu.HBM) for a in (queries, keys, values, docs)])


def solution(mesh):
    placed = P(("section", "attn"), None)
    return jax.shard_map(
        functools.partial(shards, mesh.shape["section"]),
        mesh=mesh,
        in_specs=(placed, placed, placed, P()),
        out_specs=placed,
        check_vma=False,
    )
```

```python
import functools
import math

import jax
import jax.numpy as jnp
from jax import lax
from jax.experimental import pallas as pl
from jax.experimental.pallas import tpu as pltpu
from jax.sharding import PartitionSpec as P

MESH = pl.DeviceIdType.MESH
HEAD_DIM = 128
GROUP = 3
RING = 4
LANES = 128
NEG = -1e30

OWN, EXTRA, BACK1, BACK2, BACK3, RELAY, RELAY2 = 0, 1, 2, 4, 6, 8, 9
BLOCKS = 10
UP, RIGHT, LEFT, NEXT, PREV, SIDE_EXTRA, SIDE1, SIDE2, SIDE3, ROUND = range(10)
KINDS = 10


def attention_kernel(
    sections, rows, heads,
    q_hbm, k_hbm, v_hbm, docs_hbm, out_hbm,
    kv, q, onehot, away, docs, stat_max, acc, out,
    send_sem, recv_sem, q_sem, kv_sem, doc_sem, out_sem,
):
    half = heads // 2
    scale = math.log2(math.e) * HEAD_DIM ** (-0.5)
    s = lax.axis_index("section")
    c = lax.axis_index("attn")
    x = lax.rem(s, RING)
    row_start = s - x
    first, last = x == 0, x == RING - 1
    top, bottom = s < RING, s >= sections - RING
    below = jnp.logical_not(top)
    from_left = jnp.where(last, half, jnp.where(jnp.logical_and(bottom, x == 2), heads, half + 1))
    from_right = jnp.where(x == 1, half, half + 1)
    turned_from = half + 1

    right = row_start + lax.rem(x + 1, RING)
    left = row_start + lax.rem(x + RING - 1, RING)
    up = lax.rem(s + RING, sections)
    down = lax.rem(s + sections - RING, sections)
    following = lax.rem(s + 1, sections)
    previous = lax.rem(s + sections - 1, sections)
    other = 1 - c
    up_core = jnp.where(first, other, c)

    def load_kv(j):
        at = pl.ds(pl.multiple_of(j * HEAD_DIM, HEAD_DIM), HEAD_DIM)
        return (
            pltpu.make_async_copy(k_hbm.at[:, at], kv.at[OWN, j, 0], kv_sem.at[0, j]),
            pltpu.make_async_copy(v_hbm.at[:, at], kv.at[OWN, j, 1], kv_sem.at[1, j]),
        )

    def load_q(h):
        at = pl.ds(pl.multiple_of(h * HEAD_DIM, HEAD_DIM), HEAD_DIM)
        return pltpu.make_async_copy(q_hbm.at[:, at], q.at[h], q_sem.at[h])

    def load_docs(piece):
        pair = lax.rem(lax.div(s, 2) + sections // 2 - 2 + piece, sections // 2)
        return pltpu.make_async_copy(
            docs_hbm.at[pl.ds(pl.multiple_of(pair * 8, 8), 8), :],
            docs.at[pl.ds(piece * 8, 8), :],
            doc_sem.at[piece],
        )

    @pl.loop(0, heads)
    def _(j):
        for copy in load_kv(j):
            copy.start()

    for piece in range(3):
        load_docs(piece).start()

    @pl.when(top)
    def _():
        @pl.loop(EXTRA, RELAY)
        def _(block):
            @pl.loop(0, heads)
            def _(j):
                kv[block, j] = jnp.zeros((2, rows, HEAD_DIM), kv.dtype)

    up_open = jnp.logical_not(bottom)
    down_open = below

    barrier = pltpu.get_barrier_semaphore()

    def greet(section, core):
        pl.semaphore_signal(barrier, inc=1, device_id=(section, core), device_id_type=MESH)

    greet(s, other)
    greet(right, c)
    greet(left, c)
    @pl.when(up_open)
    def _():
        greet(up, up_core)

    @pl.when(down_open)
    def _():
        greet(down, up_core)

    from_next = jnp.logical_and(last, up_open)
    to_previous = jnp.logical_and(first, down_open)

    @pl.when(to_previous)
    def _():
        greet(previous, c)

    @pl.when(from_next)
    def _():
        greet(following, c)

    @pl.loop(0, heads * GROUP)
    def _(h):
        load_q(h).start()

    def send(kind, j, source, target, section, core):
        return pltpu.make_async_remote_copy(
            src_ref=kv.at[source, j],
            dst_ref=kv.at[target, j],
            send_sem=send_sem.at[kind, j],
            recv_sem=recv_sem.at[target, j],
            device_id=(section, core),
            device_id_type=MESH,
        )

    def arrived(block, j):
        send(UP, j, block, block, s, other).wait_recv()

    up_target = jnp.where(first, EXTRA, RELAY)
    right_source = jnp.where(last, RELAY, OWN)
    left_source = jnp.where(jnp.logical_or(first, top), OWN, RELAY)
    left_target = jnp.where(jnp.logical_and(top, x == 1), RELAY2, BACK3 + c)

    def send_up(j):
        return send(UP, j, OWN, up_target, up, up_core)

    def send_right(j):
        return send(RIGHT, j, right_source, BACK1 + c, right, c)

    def send_left(j):
        return send(LEFT, j, left_source, left_target, left, c)

    def send_next(j):
        target = jnp.where(last, RELAY2, BACK2 + c)
        return send(NEXT, j, BACK1 + c, target, jnp.where(last, up, following), c)

    def send_round(j):
        return send(ROUND, j, RELAY2, BACK2 + c, jnp.where(first, left, right), c)

    def send_prev(j):
        return send(PREV, j, BACK3 + c, BACK2 + c, previous, c)

    def send_extra(j):
        return send(SIDE_EXTRA, j, jnp.where(c == 0, OWN, RELAY), EXTRA, s, other)

    def send_side(kind, j, block):
        return send(kind, j, block + c, block + c, s, other)

    def both(*conditions):
        return functools.reduce(jnp.logical_and, conditions)

    def either(*conditions):
        return functools.reduce(jnp.logical_or, conditions)

    sends_up = both(either(x > 0, c == 1), up_open)
    has_relay = both(x > 0, below)
    turns = both(top, x == 1)
    turns_on = both(top, first)

    has1 = either(below, x > 0)
    has2 = either(below, x > 1)
    has3 = either(below, last)

    def has_extra():
        return either(c == 1, below)

    relays_extra = both(x > 0, below, c == 1)
    sends_next = both(has1, jnp.logical_not(both(bottom, last)))
    sends_prev = either(both(below, s != RING), last)

    @pl.loop(0, heads)
    def _(j):
        for copy in load_kv(j):
            copy.wait()

    pl.semaphore_wait(
        barrier,
        3 + jnp.where(jnp.logical_or(from_next, to_previous), 1, 0) + jnp.where(up_open, 1, 0) + jnp.where(down_open, 1, 0),
    )

    @pl.loop(0, heads)
    def _(j):
        @pl.when(sends_up)
        def _():
            send_up(j).start()

        @pl.when(jnp.logical_not(last))
        def _():
            send_right(j).start()

        @pl.when(either(first, both(turns, j >= turned_from)))
        def _():
            send_left(j).start()

        @pl.when(c == 0)
        def _():
            send_extra(j).start()

    for piece in range(3):
        load_docs(piece).wait()
    parity = lax.rem(s, 2)
    pieces = rows // LANES
    places = ((0, c), (4 * other, other), (1, 0), (1, 1), (2, 0), (2, 1), (3, 0), (3, 1))
    ids = lax.broadcasted_iota(jnp.int32, (LANES, LANES), 0)
    for block, (back, core) in enumerate(places):
        for piece in range(pieces):
            row = (4 + parity - back) * (2 * pieces) + core * pieces + piece
            same = jnp.where(docs[pl.ds(row, 1), :] == ids, 1.0, 0.0)
            span = slice(piece * LANES, (piece + 1) * LANES)
            onehot[block, :, span] = same.astype(jnp.bfloat16)
            if block == OWN:
                away[span, :] = jnp.transpose((1.0 - same) * NEG).astype(jnp.bfloat16)

    @pl.loop(0, heads * GROUP)
    def _(h):
        load_q(h).wait()

    def keys_of(block, j):
        return jnp.concatenate([jnp.transpose(kv[block, j, 0]), onehot[block]], axis=0)

    def scores(query, key):
        return jnp.dot(query, key, preferred_element_type=jnp.float32)

    def wide(column):
        return jnp.concatenate([column] * (rows // LANES), axis=1)

    def values_of(block, j):
        value = kv[block, j, 1]
        return jnp.concatenate([value, jnp.ones_like(value)], axis=1)

    def query_of(j, r):
        return jnp.concatenate([q[j * GROUP + r], away[...]], axis=1)

    def weigh(parts, top, blocks, j):
        total = None
        for part, block in zip(parts, blocks):
            weights = jnp.exp2((part - top) * scale).astype(jnp.bfloat16)
            product = jnp.dot(weights, values_of(block, j), preferred_element_type=jnp.float32)
            total = product if total is None else total + product
        return total

    early = (OWN, EXTRA, BACK1, BACK1 + 1, BACK3, BACK3 + 1)
    late = (BACK2, BACK2 + 1)
    causal = lax.broadcasted_iota(jnp.int32, (rows, rows), 1) <= lax.broadcasted_iota(
        jnp.int32, (rows, rows), 0
    )

    def row_max(parts):
        return jnp.broadcast_to(
            jnp.max(functools.reduce(jnp.maximum, parts), axis=1, keepdims=True), (rows, LANES)
        )

    def finish_late(j, r, parts):
        old = stat_max[j, r]
        top = jnp.maximum(old, row_max(parts))
        rescale = jnp.exp2((old - top) * scale)
        summed = acc[j, r] * wide(rescale) + weigh(parts, wide(top), late, j)
        out[j * GROUP + r] = (summed[:, :HEAD_DIM] / summed[:, HEAD_DIM:]).astype(jnp.bfloat16)

    def finish_early(j, r, parts):
        parts[0] = jnp.where(causal, parts[0], NEG)
        top = row_max(parts)
        stat_max[j, r] = top
        acc[j, r] = weigh(parts, wide(top), early, j)

    def all_scores(blocks, j):
        query = jnp.concatenate([query_of(j, r) for r in range(GROUP)], axis=0)
        whole = [scores(query, key) for key in [keys_of(block, j) for block in blocks]]
        return [[part[r * rows:(r + 1) * rows] for part in whole] for r in range(GROUP)]

    def fold_early(j):
        for r, parts in enumerate(all_scores(early, j)):
            finish_early(j, r, parts)

    def fold_late(j):
        for r, parts in enumerate(all_scores(late, j)):
            finish_late(j, r, parts)

    def store_out(h):
        at = pl.ds(pl.multiple_of(h * HEAD_DIM, HEAD_DIM), HEAD_DIM)
        return pltpu.make_async_copy(out.at[h], out_hbm.at[:, at], out_sem.at[h])

    def pass_relay(j):
        @pl.when(has_relay)
        def _():
            arrived(RELAY, j)
            send_left(j).start()

        @pl.when(both(last, below))
        def _():
            send_right(j).start()

        @pl.when(relays_extra)
        def _():
            send_extra(j).start()

    def pass_aside(j):
        @pl.when(has1)
        def _():
            arrived(BACK1 + c, j)
            send_side(SIDE1, j, BACK1).start()

        @pl.when(has3)
        def _():
            arrived(BACK3 + c, j)
            send_side(SIDE3, j, BACK3).start()

    def next_range(step):
        low = 2 * (step - (heads - 2))
        high = jnp.minimum(low + 2, from_left)
        return both(sends_next, step >= heads - 2, step <= heads + 1), low, high

    rounds = both(last, below)

    def pass_round(j):
        arrived(RELAY2, j)
        send_round(j).start()

    def prev_range(step):
        low = jnp.where(step == heads, from_right, heads - 1)
        high = jnp.where(step == heads, heads - 1, heads)
        return both(sends_prev, step >= heads, step <= heads + 1), low, high

    def early_ready(j):
        @pl.when(has_extra())
        def _():
            arrived(EXTRA, j)

        @pl.when(has1)
        def _():
            arrived(BACK1 + other, j)

        @pl.when(has3)
        def _():
            arrived(BACK3 + other, j)

    @pl.loop(0, heads + 3)
    def _(step):
        @pl.when(step < heads)
        def _():
            pass_relay(step)

        @pl.when(both(step >= 2, step < heads + 2))
        def _():
            pass_aside(step - 2)

        sending, low, high = next_range(step)

        @pl.when(sending)
        def _():
            @pl.loop(low, high)
            def _(j):
                send_next(j).start()

        sending, low, high = prev_range(step)

        @pl.when(sending)
        def _():
            @pl.loop(low, high)
            def _(j):
                send_prev(j).start()

        @pl.when(both(turns_on, step >= turned_from, step < heads))
        def _():
            pass_round(step)

        @pl.when(both(rounds, step > heads))
        def _():
            pass_round(step - (heads + 1))

        @pl.when(step >= 3)
        def _():
            early_ready(step - 3)
            fold_early(step - 3)

    def late_head(k):
        odd = lax.rem(k, 2)
        evenly = half * odd + lax.div(k, 2)
        left_first = jnp.where(
            odd == 1, lax.div(k + 1, 2), jnp.where(k == 0, 0, half + lax.div(k, 2))
        )
        return jnp.where(first, evenly, left_first)

    def pass_late(k):
        @pl.when(has2)
        def _():
            j = late_head(k)
            arrived(BACK2 + c, j)
            send_side(SIDE2, j, BACK2).start()

    pass_late(0)

    @pl.loop(0, heads)
    def _(k):
        @pl.when(both(rounds, either(k == 0, k == 2)))
        def _():
            pass_round(2 + lax.div(k, 2))

        @pl.when(k + 1 < heads)
        def _():
            pass_late(k + 1)

        j = late_head(k)

        @pl.when(has2)
        def _():
            arrived(BACK2 + other, j)

        fold_late(j)
        for r in range(GROUP):
            store_out(j * GROUP + r).start()

    @pl.loop(0, heads)
    def _(j):
        for r in range(GROUP):
            store_out(j * GROUP + r).wait()

        @pl.when(sends_up)
        def _():
            send_up(j).wait_send()

        @pl.when(either(jnp.logical_not(last), below))
        def _():
            send_right(j).wait_send()

        @pl.when(either(first, has_relay, both(turns, j >= turned_from)))
        def _():
            send_left(j).wait_send()

        @pl.when(has1)
        def _():
            send_side(SIDE1, j, BACK1).wait_send()

        @pl.when(has2)
        def _():
            send_side(SIDE2, j, BACK2).wait_send()

        @pl.when(has3)
        def _():
            send_side(SIDE3, j, BACK3).wait_send()

        @pl.when(either(c == 0, relays_extra))
        def _():
            send_extra(j).wait_send()

        @pl.when(both(sends_next, j < from_left))
        def _():
            send_next(j).wait_send()

        @pl.when(either(both(rounds, j < half), both(turns_on, j >= turned_from)))
        def _():
            send_round(j).wait_send()

        @pl.when(both(sends_prev, j >= from_right))
        def _():
            send_prev(j).wait_send()


def shards(sections, queries, keys, values, doc_ids):
    rows, heads = queries.shape[0], keys.shape[1] // HEAD_DIM
    docs = doc_ids.reshape(-1, LANES)
    return pl.pallas_call(
        functools.partial(attention_kernel, sections, rows, heads),
        out_shape=jax.ShapeDtypeStruct(queries.shape, jnp.bfloat16),
        in_specs=[pl.BlockSpec(memory_space=pltpu.HBM)] * 4,
        out_specs=pl.BlockSpec(memory_space=pl.ANY),
        scratch_shapes=[
            pltpu.VMEM((BLOCKS, heads, 2, rows, HEAD_DIM), jnp.bfloat16),
            pltpu.VMEM((heads * GROUP, rows, HEAD_DIM), jnp.bfloat16),
            pltpu.VMEM((RELAY, LANES, rows), jnp.bfloat16),
            pltpu.VMEM((rows, LANES), jnp.bfloat16),
            pltpu.VMEM((24, LANES), jnp.int32),
            pltpu.VMEM((heads, GROUP, rows, LANES), jnp.float32),
            pltpu.VMEM((heads, GROUP, rows, 2 * HEAD_DIM), jnp.float32),
            pltpu.VMEM((heads * GROUP, rows, HEAD_DIM), jnp.bfloat16),
            pltpu.SemaphoreType.DMA((KINDS, heads)),
            pltpu.SemaphoreType.DMA((BLOCKS, heads)),
            pltpu.SemaphoreType.DMA((heads * GROUP,)),
            pltpu.SemaphoreType.DMA((2, heads)),
            pltpu.SemaphoreType.DMA((3,)),
            pltpu.SemaphoreType.DMA((heads * GROUP,)),
        ],
        compiler_params=pltpu.CompilerParams(
            collective_id=0, has_side_effects=True, vmem_limit_bytes=40 * 1024 * 1024
        ),
    )(*[pltpu.with_memory_space_constraint(a, pltpu.HBM) for a in (queries, keys, values, docs)])


def solution(mesh):
    placed = P(("section", "attn"), None)
    return jax.shard_map(
        functools.partial(shards, mesh.shape["section"]),
        mesh=mesh,
        in_specs=(placed, placed, placed, P()),
        out_specs=placed,
        check_vma=False,
    )
```

```python
import functools
import math

import jax
import jax.numpy as jnp
from jax import lax
from jax.experimental import pallas as pl
from jax.experimental.pallas import tpu as pltpu
from jax.sharding import PartitionSpec as P

MESH = pl.DeviceIdType.MESH
HEAD_DIM = 128
GROUP = 3
RING = 4
LANES = 128
NEG = -1e30

OWN, EXTRA, BACK1, BACK2, BACK3, RELAY, RELAY2 = 0, 1, 2, 4, 6, 8, 9
BLOCKS = 10
UP, RIGHT, LEFT, NEXT, PREV, SIDE_EXTRA, SIDE1, SIDE2, SIDE3, ROUND, CROSS1, CROSS3 = range(12)
KINDS = 12


def attention_kernel(
    sections, rows, heads,
    q_hbm, k_hbm, v_hbm, docs_hbm, out_hbm,
    kv, q, onehot, away, docs, stat_max, acc, out,
    send_sem, recv_sem, q_sem, kv_sem, doc_sem, out_sem,
):
    half = heads // 2
    scale = math.log2(math.e) * HEAD_DIM ** (-0.5)
    s = lax.axis_index("section")
    c = lax.axis_index("attn")
    x = lax.rem(s, RING)
    row_start = s - x
    first, last = x == 0, x == RING - 1
    top, bottom = s < RING, s >= sections - RING
    below = jnp.logical_not(top)
    from_left = jnp.where(jnp.logical_and(bottom, x == 2), heads, half)
    express = heads - 2

    right = row_start + lax.rem(x + 1, RING)
    left = row_start + lax.rem(x + RING - 1, RING)
    up = lax.rem(s + RING, sections)
    down = lax.rem(s + sections - RING, sections)
    following = lax.rem(s + 1, sections)
    previous = lax.rem(s + sections - 1, sections)
    other = 1 - c
    up_core = jnp.where(first, other, c)

    def load_kv(j):
        at = pl.ds(pl.multiple_of(j * HEAD_DIM, HEAD_DIM), HEAD_DIM)
        return (
            pltpu.make_async_copy(k_hbm.at[:, at], kv.at[OWN, j, 0], kv_sem.at[0, j]),
            pltpu.make_async_copy(v_hbm.at[:, at], kv.at[OWN, j, 1], kv_sem.at[1, j]),
        )

    def load_q(h):
        at = pl.ds(pl.multiple_of(h * HEAD_DIM, HEAD_DIM), HEAD_DIM)
        return pltpu.make_async_copy(q_hbm.at[:, at], q.at[h], q_sem.at[h])

    def load_docs(piece):
        pair = lax.rem(lax.div(s, 2) + sections // 2 - 2 + piece, sections // 2)
        return pltpu.make_async_copy(
            docs_hbm.at[pl.ds(pl.multiple_of(pair * 8, 8), 8), :],
            docs.at[pl.ds(piece * 8, 8), :],
            doc_sem.at[piece],
        )

    @pl.loop(0, heads)
    def _(j):
        for copy in load_kv(j):
            copy.start()

    for piece in range(3):
        load_docs(piece).start()

    @pl.when(top)
    def _():
        @pl.loop(EXTRA, RELAY)
        def _(block):
            @pl.loop(0, heads)
            def _(j):
                kv[block, j] = jnp.zeros((2, rows, HEAD_DIM), kv.dtype)

    up_open = jnp.logical_not(bottom)
    down_open = below

    barrier = pltpu.get_barrier_semaphore()

    def greet(section, core):
        pl.semaphore_signal(barrier, inc=1, device_id=(section, core), device_id_type=MESH)

    greet(s, other)
    greet(right, c)
    greet(left, c)
    @pl.when(up_open)
    def _():
        greet(up, up_core)

    @pl.when(down_open)
    def _():
        greet(down, up_core)

    from_next = jnp.logical_and(last, up_open)
    to_previous = jnp.logical_and(first, down_open)

    @pl.when(to_previous)
    def _():
        greet(previous, c)
        greet(down, c)

    @pl.when(jnp.logical_and(first, up_open))
    def _():
        greet(up, c)

    @pl.when(from_next)
    def _():
        greet(following, c)

    @pl.loop(0, heads * GROUP)
    def _(h):
        load_q(h).start()

    def send(kind, j, source, target, section, core):
        return pltpu.make_async_remote_copy(
            src_ref=kv.at[source, j],
            dst_ref=kv.at[target, j],
            send_sem=send_sem.at[kind, j],
            recv_sem=recv_sem.at[target, j],
            device_id=(section, core),
            device_id_type=MESH,
        )

    def arrived(block, j):
        send(UP, j, block, block, s, other).wait_recv()

    up_target = jnp.where(first, EXTRA, RELAY)
    def send_up(j):
        return send(UP, j, OWN, up_target, up, up_core)

    def send_right(j):
        ahead = jnp.logical_and(last, j >= express)
        source = jnp.where(jnp.logical_and(last, j < express), RELAY, OWN)
        return send(RIGHT, j, source, jnp.where(ahead, RELAY, BACK1 + c), right, c)

    def send_left(j):
        own = jnp.logical_or(jnp.logical_or(first, top), j >= express)
        ahead = jnp.logical_and(own, x > 0)
        source = jnp.where(own, OWN, RELAY)
        return send(LEFT, j, source, jnp.where(ahead, RELAY2, BACK3 + c), left, c)

    def send_cross1(j):
        return send(CROSS1, j, RELAY, BACK1 + c, up, c)

    def send_cross3(j):
        return send(CROSS3, j, RELAY2, BACK3 + c, up, c)

    def send_next(j):
        target = jnp.where(last, RELAY2, BACK2 + c)
        return send(NEXT, j, BACK1 + c, target, jnp.where(last, up, following), c)

    def send_round(j):
        return send(ROUND, j, RELAY2, BACK2 + c, jnp.where(first, left, right), c)

    def send_prev(j):
        return send(PREV, j, BACK3 + c, BACK2 + c, previous, c)

    def send_extra(j):
        return send(SIDE_EXTRA, j, jnp.where(c == 0, OWN, RELAY), EXTRA, s, other)

    def send_side(kind, j, block):
        return send(kind, j, block + c, block + c, s, other)

    def both(*conditions):
        return functools.reduce(jnp.logical_and, conditions)

    def either(*conditions):
        return functools.reduce(jnp.logical_or, conditions)

    def sends_up(j):
        return both(up_open, either(c == 1, both(x > 0, j < express)))

    def right_ahead(j):
        return either(jnp.logical_not(last), both(up_open, j >= express))

    def left_ahead(j):
        return either(first, both(x > 0, up_open, j >= express), both(turns, j >= half))

    def relays(j):
        return both(x > 0, below, j < express)

    crosses1 = both(first, up_open)
    crosses3 = both(jnp.logical_not(last), up_open)
    turns = both(top, x == 1)
    turns_on = both(top, first)

    has1 = either(below, x > 0)
    has2 = either(below, x > 1)
    has3 = either(below, last)

    def has_extra():
        return either(c == 1, below)

    relays_extra = both(x > 0, below, c == 1)
    sends_next = both(has1, jnp.logical_not(both(bottom, last)))
    sends_prev = either(both(below, s != RING), last)

    @pl.loop(0, heads)
    def _(j):
        for copy in load_kv(j):
            copy.wait()

    pl.semaphore_wait(
        barrier,
        3
        + jnp.where(from_next, 1, 0)
        + jnp.where(to_previous, 2, 0)
        + jnp.where(jnp.logical_and(first, up_open), 1, 0)
        + jnp.where(up_open, 1, 0) + jnp.where(down_open, 1, 0),
    )

    @pl.loop(0, heads)
    def _(j):
        @pl.when(sends_up(j))
        def _():
            send_up(j).start()

        @pl.when(right_ahead(j))
        def _():
            send_right(j).start()

        @pl.when(left_ahead(j))
        def _():
            send_left(j).start()

        @pl.when(c == 0)
        def _():
            send_extra(j).start()

    for piece in range(3):
        load_docs(piece).wait()
    parity = lax.rem(s, 2)
    pieces = rows // LANES
    places = ((0, c), (4 * other, other), (1, 0), (1, 1), (2, 0), (2, 1), (3, 0), (3, 1))
    ids = lax.broadcasted_iota(jnp.int32, (LANES, LANES), 0)
    for block, (back, core) in enumerate(places):
        for piece in range(pieces):
            row = (4 + parity - back) * (2 * pieces) + core * pieces + piece
            same = jnp.where(docs[pl.ds(row, 1), :] == ids, 1.0, 0.0)
            span = slice(piece * LANES, (piece + 1) * LANES)
            onehot[block, :, span] = same.astype(jnp.bfloat16)
            if block == OWN:
                away[span, :] = jnp.transpose((1.0 - same) * NEG).astype(jnp.bfloat16)

    @pl.loop(0, heads * GROUP)
    def _(h):
        load_q(h).wait()

    def keys_of(block, j):
        return jnp.concatenate([jnp.transpose(kv[block, j, 0]), onehot[block]], axis=0)

    def scores(query, key):
        return jnp.dot(query, key, preferred_element_type=jnp.float32)

    def wide(column):
        return jnp.concatenate([column] * (rows // LANES), axis=1)

    def values_of(block, j):
        value = kv[block, j, 1]
        return jnp.concatenate([value, jnp.ones_like(value)], axis=1)

    def query_of(j, r):
        return jnp.concatenate([q[j * GROUP + r], away[...]], axis=1)

    def weigh(parts, top, blocks, j):
        total = None
        for part, block in zip(parts, blocks):
            weights = jnp.exp2((part - top) * scale).astype(jnp.bfloat16)
            product = jnp.dot(weights, values_of(block, j), preferred_element_type=jnp.float32)
            total = product if total is None else total + product
        return total

    early = (OWN, EXTRA, BACK1, BACK1 + 1, BACK3, BACK3 + 1)
    late = (BACK2, BACK2 + 1)
    causal = lax.broadcasted_iota(jnp.int32, (rows, rows), 1) <= lax.broadcasted_iota(
        jnp.int32, (rows, rows), 0
    )

    def row_max(parts):
        return jnp.broadcast_to(
            jnp.max(functools.reduce(jnp.maximum, parts), axis=1, keepdims=True), (rows, LANES)
        )

    def finish_late(j, r, parts):
        old = stat_max[j, r]
        top = jnp.maximum(old, row_max(parts))
        rescale = jnp.exp2((old - top) * scale)
        summed = acc[j, r] * wide(rescale) + weigh(parts, wide(top), late, j)
        out[j * GROUP + r] = (summed[:, :HEAD_DIM] / summed[:, HEAD_DIM:]).astype(jnp.bfloat16)

    def finish_early(j, r, parts):
        parts[0] = jnp.where(causal, parts[0], NEG)
        top = row_max(parts)
        stat_max[j, r] = top
        acc[j, r] = weigh(parts, wide(top), early, j)

    def all_scores(blocks, j):
        query = jnp.concatenate([query_of(j, r) for r in range(GROUP)], axis=0)
        whole = [scores(query, key) for key in [keys_of(block, j) for block in blocks]]
        return [[part[r * rows:(r + 1) * rows] for part in whole] for r in range(GROUP)]

    def fold_early(j):
        for r, parts in enumerate(all_scores(early, j)):
            finish_early(j, r, parts)

    def fold_late(j):
        for r, parts in enumerate(all_scores(late, j)):
            finish_late(j, r, parts)

    def store_out(h):
        at = pl.ds(pl.multiple_of(h * HEAD_DIM, HEAD_DIM), HEAD_DIM)
        return pltpu.make_async_copy(out.at[h], out_hbm.at[:, at], out_sem.at[h])

    def pass_relay(j):
        @pl.when(relays(j))
        def _():
            arrived(RELAY, j)
            send_left(j).start()

        @pl.when(both(relays_extra, j >= express))
        def _():
            arrived(RELAY, j)

        @pl.when(both(last, relays(j)))
        def _():
            send_right(j).start()

        @pl.when(relays_extra)
        def _():
            send_extra(j).start()

    def pass_across(j):
        @pl.when(crosses3)
        def _():
            arrived(RELAY2, j)
            send_cross3(j).start()

        @pl.when(crosses1)
        def _():
            arrived(RELAY, j)
            send_cross1(j).start()

    def pass_aside(j):
        @pl.when(has1)
        def _():
            arrived(BACK1 + c, j)
            send_side(SIDE1, j, BACK1).start()

        @pl.when(has3)
        def _():
            arrived(BACK3 + c, j)
            send_side(SIDE3, j, BACK3).start()

    def next_range(step):
        in_pairs = step < heads
        low = jnp.where(in_pairs, 2 * (step - (heads - 3)), step - 2)
        high = jnp.minimum(low + jnp.where(in_pairs, 2, 1), from_left)
        return both(sends_next, step >= heads - 3, step <= heads + 1), low, high

    rounds = both(last, below)

    def pass_round(j):
        @pl.when(j < express)
        def _():
            arrived(RELAY2, j)

        send_round(j).start()

    def early_ready(j):
        @pl.when(has_extra())
        def _():
            arrived(EXTRA, j)

        @pl.when(has1)
        def _():
            arrived(BACK1 + other, j)

        @pl.when(has3)
        def _():
            arrived(BACK3 + other, j)

    @pl.loop(0, heads + 3)
    def _(step):
        @pl.when(step < heads)
        def _():
            pass_relay(step)

        @pl.when(both(step >= 2, step < heads + 2))
        def _():
            pass_aside(step - 2)

        sending, low, high = next_range(step)

        @pl.when(sending)
        def _():
            @pl.loop(low, high)
            def _(j):
                send_next(j).start()

        @pl.when(both(sends_prev, step >= half + 2, step < heads + 2))
        def _():
            send_prev(step - 2).start()

        @pl.when(step == 2)
        def _():
            for j in range(express, heads):
                pass_across(j)

        @pl.when(both(turns_on, step >= half, step < heads))
        def _():
            pass_round(step)

        @pl.when(both(rounds, step >= heads))
        def _():
            pass_round(step - heads)

        @pl.when(step >= 3)
        def _():
            early_ready(step - 3)
            fold_early(step - 3)

    def late_head(k):
        odd = lax.rem(k, 2)
        evenly = half * odd + lax.div(k, 2)
        return jnp.where(both(bottom, last), k, evenly)

    def pass_late(k):
        @pl.when(has2)
        def _():
            j = late_head(k)
            arrived(BACK2 + c, j)
            send_side(SIDE2, j, BACK2).start()

    pass_late(0)

    @pl.loop(0, heads)
    def _(k):
        @pl.when(both(rounds, k == 1))
        def _():
            pass_round(half - 1)

        @pl.when(k + 1 < heads)
        def _():
            pass_late(k + 1)

        j = late_head(k)

        @pl.when(has2)
        def _():
            arrived(BACK2 + other, j)

        fold_late(j)
        for r in range(GROUP):
            store_out(j * GROUP + r).start()

    @pl.loop(0, heads)
    def _(j):
        for r in range(GROUP):
            store_out(j * GROUP + r).wait()

        @pl.when(sends_up(j))
        def _():
            send_up(j).wait_send()

        @pl.when(either(right_ahead(j), both(below, j < express)))
        def _():
            send_right(j).wait_send()

        @pl.when(both(crosses1, j >= express))
        def _():
            send_cross1(j).wait_send()

        @pl.when(both(crosses3, j >= express))
        def _():
            send_cross3(j).wait_send()

        @pl.when(either(left_ahead(j), relays(j)))
        def _():
            send_left(j).wait_send()

        @pl.when(has1)
        def _():
            send_side(SIDE1, j, BACK1).wait_send()

        @pl.when(has2)
        def _():
            send_side(SIDE2, j, BACK2).wait_send()

        @pl.when(has3)
        def _():
            send_side(SIDE3, j, BACK3).wait_send()

        @pl.when(either(c == 0, relays_extra))
        def _():
            send_extra(j).wait_send()

        @pl.when(both(sends_next, j < from_left))
        def _():
            send_next(j).wait_send()

        @pl.when(either(both(rounds, j < half), both(turns_on, j >= half)))
        def _():
            send_round(j).wait_send()

        @pl.when(both(sends_prev, j >= half))
        def _():
            send_prev(j).wait_send()


def shards(sections, queries, keys, values, doc_ids):
    rows, heads = queries.shape[0], keys.shape[1] // HEAD_DIM
    docs = doc_ids.reshape(-1, LANES)
    return pl.pallas_call(
        functools.partial(attention_kernel, sections, rows, heads),
        out_shape=jax.ShapeDtypeStruct(queries.shape, jnp.bfloat16),
        in_specs=[pl.BlockSpec(memory_space=pltpu.HBM)] * 4,
        out_specs=pl.BlockSpec(memory_space=pl.ANY),
        scratch_shapes=[
            pltpu.VMEM((BLOCKS, heads, 2, rows, HEAD_DIM), jnp.bfloat16),
            pltpu.VMEM((heads * GROUP, rows, HEAD_DIM), jnp.bfloat16),
            pltpu.VMEM((RELAY, LANES, rows), jnp.bfloat16),
            pltpu.VMEM((rows, LANES), jnp.bfloat16),
            pltpu.VMEM((24, LANES), jnp.int32),
            pltpu.VMEM((heads, GROUP, rows, LANES), jnp.float32),
            pltpu.VMEM((heads, GROUP, rows, 2 * HEAD_DIM), jnp.float32),
            pltpu.VMEM((heads * GROUP, rows, HEAD_DIM), jnp.bfloat16),
            pltpu.SemaphoreType.DMA((KINDS, heads)),
            pltpu.SemaphoreType.DMA((BLOCKS, heads)),
            pltpu.SemaphoreType.DMA((heads * GROUP,)),
            pltpu.SemaphoreType.DMA((2, heads)),
            pltpu.SemaphoreType.DMA((3,)),
            pltpu.SemaphoreType.DMA((heads * GROUP,)),
        ],
        compiler_params=pltpu.CompilerParams(
            collective_id=0, has_side_effects=True, vmem_limit_bytes=40 * 1024 * 1024
        ),
    )(*[pltpu.with_memory_space_constraint(a, pltpu.HBM) for a in (queries, keys, values, docs)])


def solution(mesh):
    placed = P(("section", "attn"), None)
    return jax.shard_map(
        functools.partial(shards, mesh.shape["section"]),
        mesh=mesh,
        in_specs=(placed, placed, placed, P()),
        out_specs=placed,
        check_vma=False,
    )
```

```python
import functools
import math

import jax
import jax.numpy as jnp
from jax import lax
from jax.experimental import pallas as pl
from jax.experimental.pallas import tpu as pltpu
from jax.sharding import PartitionSpec as P

MESH = pl.DeviceIdType.MESH
HEAD_DIM = 128
GROUP = 3
RING = 4
LANES = 128
NEG = -1e30

OWN, EXTRA, BACK1, BACK2, BACK3, RELAY, RELAY2 = 0, 1, 2, 4, 6, 8, 9
BLOCKS = 10
UP, RIGHT, LEFT, NEXT, PREV, SIDE_EXTRA, SIDE1, SIDE2, SIDE3, ROUND, CROSS1, CROSS3, DOWN = range(13)
KINDS = 13


def attention_kernel(
    sections, rows, heads,
    q_hbm, k_hbm, v_hbm, docs_hbm, out_hbm,
    kv, q, onehot, away, docs, stat_max, acc, out,
    send_sem, recv_sem, q_sem, kv_sem, doc_sem, out_sem,
):
    half = heads // 2
    scale = math.log2(math.e) * HEAD_DIM ** (-0.5)
    s = lax.axis_index("section")
    c = lax.axis_index("attn")
    x = lax.rem(s, RING)
    row_start = s - x
    first, last = x == 0, x == RING - 1
    top, bottom = s < RING, s >= sections - RING
    below = jnp.logical_not(top)
    from_left = jnp.where(jnp.logical_and(bottom, x == 2), heads - 2, half)
    crossing = jnp.logical_and(lax.rem(s, RING * RING) < RING, below)
    express = heads - 2

    right = row_start + lax.rem(x + 1, RING)
    left = row_start + lax.rem(x + RING - 1, RING)
    up = lax.rem(s + RING, sections)
    down = lax.rem(s + sections - RING, sections)
    following = lax.rem(s + 1, sections)
    previous = lax.rem(s + sections - 1, sections)
    other = 1 - c
    up_core = jnp.where(first, other, c)

    def load_kv(j):
        at = pl.ds(pl.multiple_of(j * HEAD_DIM, HEAD_DIM), HEAD_DIM)
        return (
            pltpu.make_async_copy(k_hbm.at[:, at], kv.at[OWN, j, 0], kv_sem.at[0, j]),
            pltpu.make_async_copy(v_hbm.at[:, at], kv.at[OWN, j, 1], kv_sem.at[1, j]),
        )

    def load_q(h):
        at = pl.ds(pl.multiple_of(h * HEAD_DIM, HEAD_DIM), HEAD_DIM)
        return pltpu.make_async_copy(q_hbm.at[:, at], q.at[h], q_sem.at[h])

    def load_docs(piece):
        pair = lax.rem(lax.div(s, 2) + sections // 2 - 2 + piece, sections // 2)
        return pltpu.make_async_copy(
            docs_hbm.at[pl.ds(pl.multiple_of(pair * 8, 8), 8), :],
            docs.at[pl.ds(piece * 8, 8), :],
            doc_sem.at[piece],
        )

    @pl.loop(0, heads)
    def _(j):
        for copy in load_kv(j):
            copy.start()

    for piece in range(3):
        load_docs(piece).start()

    @pl.when(top)
    def _():
        @pl.loop(EXTRA, RELAY)
        def _(block):
            @pl.loop(0, heads)
            def _(j):
                kv[block, j] = jnp.zeros((2, rows, HEAD_DIM), kv.dtype)

    up_open = jnp.logical_not(bottom)
    down_open = below

    barrier = pltpu.get_barrier_semaphore()

    def greet(section, core):
        pl.semaphore_signal(barrier, inc=1, device_id=(section, core), device_id_type=MESH)

    greet(s, other)
    greet(right, c)
    greet(left, c)
    @pl.when(up_open)
    def _():
        greet(up, up_core)

    @pl.when(down_open)
    def _():
        greet(down, up_core)

    from_next = jnp.logical_and(last, up_open)
    to_previous = jnp.logical_and(first, down_open)

    @pl.when(to_previous)
    def _():
        greet(previous, c)
        greet(down, c)

    @pl.when(jnp.logical_and(first, up_open))
    def _():
        greet(up, c)

    @pl.when(from_next)
    def _():
        greet(following, c)

    @pl.loop(0, heads * GROUP)
    def _(h):
        load_q(h).start()

    def send(kind, j, source, target, section, core):
        return pltpu.make_async_remote_copy(
            src_ref=kv.at[source, j],
            dst_ref=kv.at[target, j],
            send_sem=send_sem.at[kind, j],
            recv_sem=recv_sem.at[target, j],
            device_id=(section, core),
            device_id_type=MESH,
        )

    def arrived(block, j):
        send(UP, j, block, block, s, other).wait_recv()

    up_target = jnp.where(first, EXTRA, RELAY)
    def send_up(j):
        return send(UP, j, OWN, up_target, up, up_core)

    def send_right(j):
        ahead = jnp.logical_and(last, j >= express)
        source = jnp.where(jnp.logical_and(last, j < express), RELAY, OWN)
        return send(RIGHT, j, source, jnp.where(ahead, RELAY, BACK1 + c), right, c)

    def send_left(j):
        own = jnp.logical_or(jnp.logical_or(first, top), j >= express)
        ahead = jnp.logical_and(own, x > 0)
        source = jnp.where(own, OWN, RELAY)
        return send(LEFT, j, source, jnp.where(ahead, RELAY2, BACK3 + c), left, c)

    def send_cross1(j):
        return send(CROSS1, j, RELAY, BACK1 + c, up, c)

    def send_cross3(j):
        return send(CROSS3, j, RELAY2, BACK3 + c, up, c)

    def send_next(j):
        target = jnp.where(last, RELAY2, BACK2 + c)
        return send(NEXT, j, BACK1 + c, target, jnp.where(last, up, following), c)

    def send_round(j):
        return send(ROUND, j, RELAY2, BACK2 + c, jnp.where(first, left, right), c)

    def send_prev(j):
        around = jnp.logical_and(first, crossing)
        target = jnp.where(around, RELAY2, BACK2 + c)
        return send(PREV, j, BACK3 + c, target, jnp.where(around, left, previous), c)

    def send_down(j):
        return send(DOWN, j, RELAY2, BACK2 + c, down, c)

    def send_extra(j):
        return send(SIDE_EXTRA, j, jnp.where(c == 0, OWN, RELAY), EXTRA, s, other)

    def send_side(kind, j, block):
        return send(kind, j, block + c, block + c, s, other)

    def both(*conditions):
        return functools.reduce(jnp.logical_and, conditions)

    def either(*conditions):
        return functools.reduce(jnp.logical_or, conditions)

    def sends_up(j):
        return both(up_open, either(c == 1, both(x > 0, j < express)))

    def right_ahead(j):
        return either(jnp.logical_not(last), both(up_open, j >= express))

    def left_ahead(j):
        return either(
            first,
            both(x > 0, either(up_open, x == 1), j >= express),
            both(top, x == 1, j >= half),
        )

    def relays(j):
        return both(x > 0, below, j < express)

    crosses1 = both(first, up_open)
    crosses3 = both(jnp.logical_not(last), up_open)
    descends = both(last, crossing)

    def turns_on(j):
        return both(first, either(both(top, j >= half), both(bottom, j >= express)))

    has1 = either(below, x > 0)
    has2 = either(below, x > 1)
    has3 = either(below, last)

    def has_extra():
        return either(c == 1, below)

    relays_extra = both(x > 0, below, c == 1)
    sends_next = both(has1, jnp.logical_not(both(bottom, last)))
    sends_prev = either(both(below, s != RING), last)

    @pl.loop(0, heads)
    def _(j):
        for copy in load_kv(j):
            copy.wait()

    pl.semaphore_wait(
        barrier,
        3
        + jnp.where(from_next, 1, 0)
        + jnp.where(to_previous, 2, 0)
        + jnp.where(jnp.logical_and(first, up_open), 1, 0)
        + jnp.where(up_open, 1, 0) + jnp.where(down_open, 1, 0),
    )

    @pl.loop(0, heads)
    def _(j):
        @pl.when(sends_up(j))
        def _():
            send_up(j).start()

        @pl.when(right_ahead(j))
        def _():
            send_right(j).start()

        @pl.when(left_ahead(j))
        def _():
            send_left(j).start()

        @pl.when(c == 0)
        def _():
            send_extra(j).start()

    for piece in range(3):
        load_docs(piece).wait()
    parity = lax.rem(s, 2)
    pieces = rows // LANES
    places = ((0, c), (4 * other, other), (1, 0), (1, 1), (2, 0), (2, 1), (3, 0), (3, 1))
    ids = lax.broadcasted_iota(jnp.int32, (LANES, LANES), 0)
    for block, (back, core) in enumerate(places):
        for piece in range(pieces):
            row = (4 + parity - back) * (2 * pieces) + core * pieces + piece
            same = jnp.where(docs[pl.ds(row, 1), :] == ids, 1.0, 0.0)
            span = slice(piece * LANES, (piece + 1) * LANES)
            onehot[block, :, span] = same.astype(jnp.bfloat16)
            if block == OWN:
                away[span, :] = jnp.transpose((1.0 - same) * NEG).astype(jnp.bfloat16)

    @pl.loop(0, heads * GROUP)
    def _(h):
        load_q(h).wait()

    def keys_of(block, j):
        return jnp.concatenate([jnp.transpose(kv[block, j, 0]), onehot[block]], axis=0)

    def scores(query, key):
        return jnp.dot(query, key, preferred_element_type=jnp.float32)

    def wide(column):
        return jnp.concatenate([column] * (rows // LANES), axis=1)

    def values_of(block, j):
        value = kv[block, j, 1]
        return jnp.concatenate([value, jnp.ones_like(value)], axis=1)

    def query_of(j, r):
        return jnp.concatenate([q[j * GROUP + r], away[...]], axis=1)

    def weigh(parts, top, blocks, j):
        total = None
        for part, block in zip(parts, blocks):
            weights = jnp.exp2((part - top) * scale).astype(jnp.bfloat16)
            product = jnp.dot(weights, values_of(block, j), preferred_element_type=jnp.float32)
            total = product if total is None else total + product
        return total

    early = (OWN, EXTRA, BACK1, BACK1 + 1, BACK3, BACK3 + 1)
    late = (BACK2, BACK2 + 1)
    causal = lax.broadcasted_iota(jnp.int32, (rows, rows), 1) <= lax.broadcasted_iota(
        jnp.int32, (rows, rows), 0
    )

    def row_max(parts):
        return jnp.broadcast_to(
            jnp.max(functools.reduce(jnp.maximum, parts), axis=1, keepdims=True), (rows, LANES)
        )

    def finish_late(j, r, parts):
        old = stat_max[j, r]
        top = jnp.maximum(old, row_max(parts))
        rescale = jnp.exp2((old - top) * scale)
        summed = acc[j, r] * wide(rescale) + weigh(parts, wide(top), late, j)
        out[j * GROUP + r] = (summed[:, :HEAD_DIM] / summed[:, HEAD_DIM:]).astype(jnp.bfloat16)

    def finish_early(j, r, parts):
        parts[0] = jnp.where(causal, parts[0], NEG)
        top = row_max(parts)
        stat_max[j, r] = top
        acc[j, r] = weigh(parts, wide(top), early, j)

    def all_scores(blocks, j):
        query = jnp.concatenate([query_of(j, r) for r in range(GROUP)], axis=0)
        whole = [scores(query, key) for key in [keys_of(block, j) for block in blocks]]
        return [[part[r * rows:(r + 1) * rows] for part in whole] for r in range(GROUP)]

    def fold_early(j):
        for r, parts in enumerate(all_scores(early, j)):
            finish_early(j, r, parts)

    def fold_late(j):
        for r, parts in enumerate(all_scores(late, j)):
            finish_late(j, r, parts)

    def store_out(h):
        at = pl.ds(pl.multiple_of(h * HEAD_DIM, HEAD_DIM), HEAD_DIM)
        return pltpu.make_async_copy(out.at[h], out_hbm.at[:, at], out_sem.at[h])

    def pass_relay(j):
        @pl.when(relays(j))
        def _():
            arrived(RELAY, j)
            send_left(j).start()

        @pl.when(both(relays_extra, j >= express))
        def _():
            arrived(RELAY, j)

        @pl.when(both(last, relays(j)))
        def _():
            send_right(j).start()

        @pl.when(relays_extra)
        def _():
            send_extra(j).start()

    def pass_across(j):
        @pl.when(crosses3)
        def _():
            arrived(RELAY2, j)
            send_cross3(j).start()

        @pl.when(crosses1)
        def _():
            arrived(RELAY, j)
            send_cross1(j).start()

    def pass_aside(j):
        @pl.when(has1)
        def _():
            arrived(BACK1 + c, j)
            send_side(SIDE1, j, BACK1).start()

        @pl.when(has3)
        def _():
            arrived(BACK3 + c, j)
            send_side(SIDE3, j, BACK3).start()

    def next_range(step):
        in_pairs = step < heads
        low = jnp.where(in_pairs, 2 * (step - (heads - 3)), step - 2)
        high = jnp.minimum(low + jnp.where(in_pairs, 2, 1), from_left)
        return both(sends_next, step >= heads - 3, step <= heads + 1), low, high

    rounds = both(last, below)

    def pass_round(j):
        @pl.when(either(j < express, bottom))
        def _():
            arrived(RELAY2, j)

        send_round(j).start()

    def pass_down(j):
        arrived(RELAY2, j)
        send_down(j).start()

    def early_ready(j):
        @pl.when(has_extra())
        def _():
            arrived(EXTRA, j)

        @pl.when(has1)
        def _():
            arrived(BACK1 + other, j)

        @pl.when(has3)
        def _():
            arrived(BACK3 + other, j)

    @pl.loop(0, heads + 3)
    def _(step):
        @pl.when(step < heads)
        def _():
            pass_relay(step)

        @pl.when(both(step >= 2, step < heads + 2))
        def _():
            pass_aside(step - 2)

        sending, low, high = next_range(step)

        @pl.when(sending)
        def _():
            @pl.loop(low, high)
            def _(j):
                send_next(j).start()

        @pl.when(both(sends_prev, step >= half + 2, step < heads + 2))
        def _():
            send_prev(step - 2).start()

        @pl.when(step == 2)
        def _():
            for j in range(express, heads):
                pass_across(j)

        @pl.when(both(turns_on(step), step < heads))
        def _():
            pass_round(step)

        @pl.when(both(rounds, step >= heads))
        def _():
            pass_round(step - heads)

        @pl.when(both(descends, step > heads))
        def _():
            pass_down(half + step - (heads + 1))

        @pl.when(step >= 3)
        def _():
            early_ready(step - 3)
            fold_early(step - 3)

    def late_head(k):
        odd = lax.rem(k, 2)
        evenly = half * odd + lax.div(k, 2)
        turned = jnp.where(k < 2, k, jnp.where(k < 4, express + k - 2, k - 2))
        return jnp.where(both(bottom, last), turned, evenly)

    def pass_late(k):
        @pl.when(has2)
        def _():
            j = late_head(k)
            arrived(BACK2 + c, j)
            send_side(SIDE2, j, BACK2).start()

    pass_late(0)

    @pl.loop(0, heads)
    def _(k):
        @pl.when(both(rounds, k == 1))
        def _():
            pass_round(half - 1)

        @pl.when(both(descends, either(k == 1, k == 3)))
        def _():
            pass_down(half + 2 + lax.div(k, 2))

        @pl.when(k + 1 < heads)
        def _():
            pass_late(k + 1)

        j = late_head(k)

        @pl.when(has2)
        def _():
            arrived(BACK2 + other, j)

        fold_late(j)
        for r in range(GROUP):
            store_out(j * GROUP + r).start()

    @pl.loop(0, heads)
    def _(j):
        for r in range(GROUP):
            store_out(j * GROUP + r).wait()

        @pl.when(sends_up(j))
        def _():
            send_up(j).wait_send()

        @pl.when(either(right_ahead(j), both(below, j < express)))
        def _():
            send_right(j).wait_send()

        @pl.when(both(crosses1, j >= express))
        def _():
            send_cross1(j).wait_send()

        @pl.when(both(crosses3, j >= express))
        def _():
            send_cross3(j).wait_send()

        @pl.when(either(left_ahead(j), relays(j)))
        def _():
            send_left(j).wait_send()

        @pl.when(has1)
        def _():
            send_side(SIDE1, j, BACK1).wait_send()

        @pl.when(has2)
        def _():
            send_side(SIDE2, j, BACK2).wait_send()

        @pl.when(has3)
        def _():
            send_side(SIDE3, j, BACK3).wait_send()

        @pl.when(either(c == 0, relays_extra))
        def _():
            send_extra(j).wait_send()

        @pl.when(both(sends_next, j < from_left))
        def _():
            send_next(j).wait_send()

        @pl.when(both(descends, j >= half))
        def _():
            send_down(j).wait_send()

        @pl.when(either(both(rounds, j < half), turns_on(j)))
        def _():
            send_round(j).wait_send()

        @pl.when(both(sends_prev, j >= half))
        def _():
            send_prev(j).wait_send()


def shards(sections, queries, keys, values, doc_ids):
    rows, heads = queries.shape[0], keys.shape[1] // HEAD_DIM
    docs = doc_ids.reshape(-1, LANES)
    return pl.pallas_call(
        functools.partial(attention_kernel, sections, rows, heads),
        out_shape=jax.ShapeDtypeStruct(queries.shape, jnp.bfloat16),
        in_specs=[pl.BlockSpec(memory_space=pltpu.HBM)] * 4,
        out_specs=pl.BlockSpec(memory_space=pl.ANY),
        scratch_shapes=[
            pltpu.VMEM((BLOCKS, heads, 2, rows, HEAD_DIM), jnp.bfloat16),
            pltpu.VMEM((heads * GROUP, rows, HEAD_DIM), jnp.bfloat16),
            pltpu.VMEM((RELAY, LANES, rows), jnp.bfloat16),
            pltpu.VMEM((rows, LANES), jnp.bfloat16),
            pltpu.VMEM((24, LANES), jnp.int32),
            pltpu.VMEM((heads, GROUP, rows, LANES), jnp.float32),
            pltpu.VMEM((heads, GROUP, rows, 2 * HEAD_DIM), jnp.float32),
            pltpu.VMEM((heads * GROUP, rows, HEAD_DIM), jnp.bfloat16),
            pltpu.SemaphoreType.DMA((KINDS, heads)),
            pltpu.SemaphoreType.DMA((BLOCKS, heads)),
            pltpu.SemaphoreType.DMA((heads * GROUP,)),
            pltpu.SemaphoreType.DMA((2, heads)),
            pltpu.SemaphoreType.DMA((3,)),
            pltpu.SemaphoreType.DMA((heads * GROUP,)),
        ],
        compiler_params=pltpu.CompilerParams(
            collective_id=0, has_side_effects=True, vmem_limit_bytes=40 * 1024 * 1024
        ),
    )(*[pltpu.with_memory_space_constraint(a, pltpu.HBM) for a in (queries, keys, values, docs)])


def solution(mesh):
    placed = P(("section", "attn"), None)
    return jax.shard_map(
        functools.partial(shards, mesh.shape["section"]),
        mesh=mesh,
        in_specs=(placed, placed, placed, P()),
        out_specs=placed,
        check_vma=False,
    )
```

```python
import functools
import math

import jax
import jax.numpy as jnp
from jax import lax
from jax.experimental import pallas as pl
from jax.experimental.pallas import tpu as pltpu
from jax.sharding import PartitionSpec as P

MESH = pl.DeviceIdType.MESH
HEAD_DIM = 128
GROUP = 3
RING = 4
LANES = 128
NEG = -1e30

OWN, EXTRA, BACK1, BACK2, BACK3, RELAY, RELAY2 = 0, 1, 2, 4, 6, 8, 9
BLOCKS = 10
UP, RIGHT, LEFT, NEXT, PREV, SIDE_EXTRA, SIDE1, SIDE2, SIDE3, ROUND, CROSS1, CROSS3, DOWN = range(13)
KINDS = 13


def attention_kernel(
    sections, rows, heads,
    q_hbm, k_hbm, v_hbm, docs_hbm, out_hbm,
    kv, q, onehot, away, docs, stat_max, acc, out, held0, held1,
    send_sem, recv_sem, q_sem, kv_sem, doc_sem, out_sem,
):
    half = heads // 2
    scale = math.log2(math.e) * HEAD_DIM ** (-0.5)
    s = lax.axis_index("section")
    c = lax.axis_index("attn")
    x = lax.rem(s, RING)
    row_start = s - x
    first, last = x == 0, x == RING - 1
    top, bottom = s < RING, s >= sections - RING
    below = jnp.logical_not(top)
    from_left = jnp.where(jnp.logical_and(bottom, x == 2), heads - 2, half)
    crossing = jnp.logical_and(lax.rem(s, RING * RING) < RING, below)
    express = heads - 2

    right = row_start + lax.rem(x + 1, RING)
    left = row_start + lax.rem(x + RING - 1, RING)
    up = lax.rem(s + RING, sections)
    down = lax.rem(s + sections - RING, sections)
    following = lax.rem(s + 1, sections)
    previous = lax.rem(s + sections - 1, sections)
    other = 1 - c
    up_core = jnp.where(first, other, c)

    def load_kv(j):
        at = pl.ds(pl.multiple_of(j * HEAD_DIM, HEAD_DIM), HEAD_DIM)
        return (
            pltpu.make_async_copy(k_hbm.at[:, at], kv.at[OWN, j, 0], kv_sem.at[0, j]),
            pltpu.make_async_copy(v_hbm.at[:, at], kv.at[OWN, j, 1], kv_sem.at[1, j]),
        )

    def load_q(h):
        at = pl.ds(pl.multiple_of(h * HEAD_DIM, HEAD_DIM), HEAD_DIM)
        return pltpu.make_async_copy(q_hbm.at[:, at], q.at[h], q_sem.at[h])

    def load_docs(piece):
        pair = lax.rem(lax.div(s, 2) + sections // 2 - 2 + piece, sections // 2)
        return pltpu.make_async_copy(
            docs_hbm.at[pl.ds(pl.multiple_of(pair * 8, 8), 8), :],
            docs.at[pl.ds(piece * 8, 8), :],
            doc_sem.at[piece],
        )

    @pl.loop(0, heads)
    def _(j):
        for copy in load_kv(j):
            copy.start()

    for piece in range(3):
        load_docs(piece).start()

    @pl.when(top)
    def _():
        @pl.loop(EXTRA, RELAY)
        def _(block):
            @pl.loop(0, heads)
            def _(j):
                kv[block, j] = jnp.zeros((2, rows, HEAD_DIM), kv.dtype)

    up_open = jnp.logical_not(bottom)
    down_open = below

    barrier = pltpu.get_barrier_semaphore()

    def greet(section, core):
        pl.semaphore_signal(barrier, inc=1, device_id=(section, core), device_id_type=MESH)

    greet(s, other)
    greet(right, c)
    greet(left, c)
    @pl.when(up_open)
    def _():
        greet(up, up_core)

    @pl.when(down_open)
    def _():
        greet(down, up_core)

    from_next = jnp.logical_and(last, up_open)
    to_previous = jnp.logical_and(first, down_open)

    @pl.when(to_previous)
    def _():
        greet(previous, c)
        greet(down, c)

    @pl.when(jnp.logical_and(first, up_open))
    def _():
        greet(up, c)

    @pl.when(from_next)
    def _():
        greet(following, c)

    @pl.loop(0, heads * GROUP)
    def _(h):
        load_q(h).start()

    def send(kind, j, source, target, section, core):
        return pltpu.make_async_remote_copy(
            src_ref=kv.at[source, j],
            dst_ref=kv.at[target, j],
            send_sem=send_sem.at[kind, j],
            recv_sem=recv_sem.at[target, j],
            device_id=(section, core),
            device_id_type=MESH,
        )

    def arrived(block, j):
        send(UP, j, block, block, s, other).wait_recv()

    up_target = jnp.where(first, EXTRA, RELAY)
    def send_up(j):
        return send(UP, j, OWN, up_target, up, up_core)

    def send_right(j):
        ahead = jnp.logical_and(last, j >= express)
        source = jnp.where(jnp.logical_and(last, j < express), RELAY, OWN)
        return send(RIGHT, j, source, jnp.where(ahead, RELAY, BACK1 + c), right, c)

    def send_left(j):
        own = jnp.logical_or(jnp.logical_or(first, top), j >= express)
        ahead = jnp.logical_and(own, x > 0)
        source = jnp.where(own, OWN, RELAY)
        return send(LEFT, j, source, jnp.where(ahead, RELAY2, BACK3 + c), left, c)

    def send_cross1(j):
        return send(CROSS1, j, RELAY, BACK1 + c, up, c)

    def send_cross3(j):
        return send(CROSS3, j, RELAY2, BACK3 + c, up, c)

    def send_next(j):
        target = jnp.where(last, RELAY2, BACK2 + c)
        return send(NEXT, j, BACK1 + c, target, jnp.where(last, up, following), c)

    def send_round(j):
        return send(ROUND, j, RELAY2, BACK2 + c, jnp.where(first, left, right), c)

    def send_prev(j):
        around = jnp.logical_and(first, crossing)
        target = jnp.where(around, RELAY2, BACK2 + c)
        return send(PREV, j, BACK3 + c, target, jnp.where(around, left, previous), c)

    def send_down(j):
        return send(DOWN, j, RELAY2, BACK2 + c, down, c)

    def send_extra(j):
        return send(SIDE_EXTRA, j, jnp.where(c == 0, OWN, RELAY), EXTRA, s, other)

    def send_side(kind, j, block):
        return send(kind, j, block + c, block + c, s, other)

    def both(*conditions):
        return functools.reduce(jnp.logical_and, conditions)

    def either(*conditions):
        return functools.reduce(jnp.logical_or, conditions)

    def sends_up(j):
        return both(up_open, either(c == 1, both(x > 0, j < express)))

    def right_ahead(j):
        return either(jnp.logical_not(last), both(up_open, j >= express))

    def left_ahead(j):
        return either(
            first,
            both(x > 0, either(up_open, x == 1), j >= express),
            both(top, x == 1, j >= half),
        )

    def relays(j):
        return both(x > 0, below, j < express)

    crosses1 = both(first, up_open)
    crosses3 = both(jnp.logical_not(last), up_open)
    descends = both(last, crossing)

    def turns_on(j):
        return both(first, either(both(top, j >= half), both(bottom, j >= express)))

    has1 = either(below, x > 0)
    has2 = either(below, x > 1)
    has3 = either(below, last)

    def has_extra():
        return either(c == 1, below)

    relays_extra = both(x > 0, below, c == 1)
    sends_next = both(has1, jnp.logical_not(both(bottom, last)))
    sends_prev = either(both(below, s != RING), last)

    @pl.loop(0, heads)
    def _(j):
        for copy in load_kv(j):
            copy.wait()

    pl.semaphore_wait(
        barrier,
        3
        + jnp.where(from_next, 1, 0)
        + jnp.where(to_previous, 2, 0)
        + jnp.where(jnp.logical_and(first, up_open), 1, 0)
        + jnp.where(up_open, 1, 0) + jnp.where(down_open, 1, 0),
    )

    @pl.loop(0, heads)
    def _(j):
        @pl.when(sends_up(j))
        def _():
            send_up(j).start()

        @pl.when(right_ahead(j))
        def _():
            send_right(j).start()

        @pl.when(left_ahead(j))
        def _():
            send_left(j).start()

        @pl.when(c == 0)
        def _():
            send_extra(j).start()

    for piece in range(3):
        load_docs(piece).wait()
    parity = lax.rem(s, 2)
    pieces = rows // LANES
    places = ((0, c), (4 * other, other), (1, 0), (1, 1), (2, 0), (2, 1), (3, 0), (3, 1))
    ids = lax.broadcasted_iota(jnp.int32, (LANES, LANES), 0)
    for block, (back, core) in enumerate(places):
        for piece in range(pieces):
            row = (4 + parity - back) * (2 * pieces) + core * pieces + piece
            same = jnp.where(docs[pl.ds(row, 1), :] == ids, 1.0, 0.0)
            span = slice(piece * LANES, (piece + 1) * LANES)
            onehot[block, :, span] = same.astype(jnp.bfloat16)
            if block == OWN:
                away[span, :] = jnp.transpose((1.0 - same) * NEG).astype(jnp.bfloat16)

    @pl.loop(0, heads * GROUP)
    def _(h):
        load_q(h).wait()

    def keys_of(block, j):
        return jnp.concatenate([jnp.transpose(kv[block, j, 0]), onehot[block]], axis=0)

    def scores(query, key):
        return jnp.dot(query, key, preferred_element_type=jnp.float32)

    def wide(column):
        return jnp.concatenate([column] * (rows // LANES), axis=1)

    def values_of(block, j):
        value = kv[block, j, 1]
        return jnp.concatenate([value, jnp.ones_like(value)], axis=1)

    def query_of(j, r):
        return jnp.concatenate([q[j * GROUP + r], away[...]], axis=1)

    def weigh(parts, top, blocks, j):
        total = None
        for part, block in zip(parts, blocks):
            weights = jnp.exp2((part - top) * scale).astype(jnp.bfloat16)
            product = jnp.dot(weights, values_of(block, j), preferred_element_type=jnp.float32)
            total = product if total is None else total + product
        return total

    early = (OWN, EXTRA, BACK1, BACK1 + 1, BACK3, BACK3 + 1)
    late = (BACK2, BACK2 + 1)
    causal = lax.broadcasted_iota(jnp.int32, (rows, rows), 1) <= lax.broadcasted_iota(
        jnp.int32, (rows, rows), 0
    )

    def row_max(parts):
        return jnp.broadcast_to(
            jnp.max(functools.reduce(jnp.maximum, parts), axis=1, keepdims=True), (rows, LANES)
        )

    def finish_late(j, r, parts):
        old = stat_max[j, r]
        top = jnp.maximum(old, row_max(parts))
        rescale = jnp.exp2((old - top) * scale)
        summed = acc[j, r] * wide(rescale) + weigh(parts, wide(top), late, j)
        out[j * GROUP + r] = (summed[:, :HEAD_DIM] / summed[:, HEAD_DIM:]).astype(jnp.bfloat16)

    def finish_early(j, r, parts):
        parts[0] = jnp.where(causal, parts[0], NEG)
        top = row_max(parts)
        stat_max[j, r] = top
        acc[j, r] = weigh(parts, wide(top), early, j)

    def score(blocks, j, held):
        query = jnp.concatenate([query_of(j, r) for r in range(GROUP)], axis=0)
        for at, block in enumerate(blocks):
            held[:, at * rows:(at + 1) * rows] = scores(query, keys_of(block, j))

    def parts_of(blocks, r, held):
        return [
            held[r * rows:(r + 1) * rows, at * rows:(at + 1) * rows] for at in range(len(blocks))
        ]

    def fold_early(j, held):
        for r in range(GROUP):
            finish_early(j, r, parts_of(early, r, held))

    def fold_late(j, held):
        for r in range(GROUP):
            finish_late(j, r, parts_of(late, r, held))

    def store_out(h):
        at = pl.ds(pl.multiple_of(h * HEAD_DIM, HEAD_DIM), HEAD_DIM)
        return pltpu.make_async_copy(out.at[h], out_hbm.at[:, at], out_sem.at[h])

    def pass_relay(j):
        @pl.when(relays(j))
        def _():
            arrived(RELAY, j)
            send_left(j).start()

        @pl.when(both(relays_extra, j >= express))
        def _():
            arrived(RELAY, j)

        @pl.when(both(last, relays(j)))
        def _():
            send_right(j).start()

        @pl.when(relays_extra)
        def _():
            send_extra(j).start()

    def pass_across(j):
        @pl.when(crosses3)
        def _():
            arrived(RELAY2, j)
            send_cross3(j).start()

        @pl.when(crosses1)
        def _():
            arrived(RELAY, j)
            send_cross1(j).start()

    def pass_aside(j):
        @pl.when(has1)
        def _():
            arrived(BACK1 + c, j)
            send_side(SIDE1, j, BACK1).start()

        @pl.when(has3)
        def _():
            arrived(BACK3 + c, j)
            send_side(SIDE3, j, BACK3).start()

    def next_range(step):
        in_pairs = step < heads
        low = jnp.where(in_pairs, 2 * (step - (heads - 3)), step - 2)
        high = jnp.minimum(low + jnp.where(in_pairs, 2, 1), from_left)
        return both(sends_next, step >= heads - 3, step <= heads + 1), low, high

    rounds = both(last, below)

    def pass_round(j):
        @pl.when(either(j < express, bottom))
        def _():
            arrived(RELAY2, j)

        send_round(j).start()

    def pass_down(j):
        arrived(RELAY2, j)
        send_down(j).start()

    def early_ready(j):
        @pl.when(has_extra())
        def _():
            arrived(EXTRA, j)

        @pl.when(has1)
        def _():
            arrived(BACK1 + other, j)

        @pl.when(has3)
        def _():
            arrived(BACK3 + other, j)

    def move(step):
        @pl.when(step < heads)
        def _():
            pass_relay(step)

        @pl.when(both(step >= 2, step < heads + 2))
        def _():
            pass_aside(step - 2)

        sending, low, high = next_range(step)

        @pl.when(sending)
        def _():
            @pl.loop(low, high)
            def _(j):
                send_next(j).start()

        @pl.when(both(sends_prev, step >= half + 2, step < heads + 2))
        def _():
            send_prev(step - 2).start()

        @pl.when(step == 2)
        def _():
            for j in range(express, heads):
                pass_across(j)

        @pl.when(both(turns_on(step), step < heads))
        def _():
            pass_round(step)

        @pl.when(both(rounds, step >= heads))
        def _():
            pass_round(step - heads)

        @pl.when(both(descends, step > heads))
        def _():
            pass_down(half + step - (heads + 1))

    buffers = (held0, held1)

    @pl.loop(0, (heads + 4) // 2)
    def _(pair):
        for side in range(2):
            step = 2 * pair + side
            now, before = buffers[side], buffers[1 - side]
            move(step)

            @pl.when(both(step >= 3, step < heads + 3))
            def _():
                early_ready(step - 3)

            @pl.when(step == 3)
            def _():
                score(early, step - 3, now)

            @pl.when(both(step > 3, step < heads + 3))
            def _():
                score(early, step - 3, now)
                fold_early(step - 4, before)

            @pl.when(step == heads + 3)
            def _():
                fold_early(step - 4, before)

    def late_head(k):
        odd = lax.rem(k, 2)
        evenly = half * odd + lax.div(k, 2)
        turned = jnp.where(k < 2, k, jnp.where(k < 4, express + k - 2, k - 2))
        mixed = jnp.where(odd == 1, lax.div(k + 1, 2), half - 1 + lax.div(k, 2))
        delayed = jnp.where(k == 0, 0, jnp.where(k == heads - 1, k, mixed))
        waits_down = both(last, up_open, lax.rem(s, RING * RING) >= RING * (RING - 1))
        return jnp.where(both(bottom, last), turned, jnp.where(waits_down, delayed, evenly))

    def pass_late(k):
        @pl.when(has2)
        def _():
            j = late_head(k)
            arrived(BACK2 + c, j)
            send_side(SIDE2, j, BACK2).start()

    def late_ready(k):
        @pl.when(has2)
        def _():
            arrived(BACK2 + other, late_head(k))

    def move_late(k):
        @pl.when(both(descends, k == 1))
        def _():
            pass_down(heads - 1)

        @pl.when(k + 1 < heads)
        def _():
            pass_late(k + 1)

    def store_head(j):
        for r in range(GROUP):
            store_out(j * GROUP + r).start()

    pass_late(0)

    @pl.loop(0, heads // 2)
    def _(pair):
        for side in range(2):
            k = 2 * pair + side
            now, before = buffers[side], buffers[1 - side]
            move_late(k)
            late_ready(k)

            if side == 0:
                @pl.when(pair == 0)
                def _():
                    score(late, late_head(k), now)

                @pl.when(pair > 0)
                def _():
                    score(late, late_head(k), now)
                    fold_late(late_head(k - 1), before)
                    store_head(late_head(k - 1))
            else:
                score(late, late_head(k), now)
                fold_late(late_head(k - 1), before)
                store_head(late_head(k - 1))

    fold_late(late_head(heads - 1), buffers[1])
    store_head(late_head(heads - 1))

    @pl.loop(0, heads)
    def _(j):
        for r in range(GROUP):
            store_out(j * GROUP + r).wait()

        @pl.when(sends_up(j))
        def _():
            send_up(j).wait_send()

        @pl.when(either(right_ahead(j), both(below, j < express)))
        def _():
            send_right(j).wait_send()

        @pl.when(both(crosses1, j >= express))
        def _():
            send_cross1(j).wait_send()

        @pl.when(both(crosses3, j >= express))
        def _():
            send_cross3(j).wait_send()

        @pl.when(either(left_ahead(j), relays(j)))
        def _():
            send_left(j).wait_send()

        @pl.when(has1)
        def _():
            send_side(SIDE1, j, BACK1).wait_send()

        @pl.when(has2)
        def _():
            send_side(SIDE2, j, BACK2).wait_send()

        @pl.when(has3)
        def _():
            send_side(SIDE3, j, BACK3).wait_send()

        @pl.when(either(c == 0, relays_extra))
        def _():
            send_extra(j).wait_send()

        @pl.when(both(sends_next, j < from_left))
        def _():
            send_next(j).wait_send()

        @pl.when(both(descends, j >= half))
        def _():
            send_down(j).wait_send()

        @pl.when(either(both(rounds, j < half), turns_on(j)))
        def _():
            send_round(j).wait_send()

        @pl.when(both(sends_prev, j >= half))
        def _():
            send_prev(j).wait_send()


def shards(sections, queries, keys, values, doc_ids):
    rows, heads = queries.shape[0], keys.shape[1] // HEAD_DIM
    docs = doc_ids.reshape(-1, LANES)
    return pl.pallas_call(
        functools.partial(attention_kernel, sections, rows, heads),
        out_shape=jax.ShapeDtypeStruct(queries.shape, jnp.bfloat16),
        in_specs=[pl.BlockSpec(memory_space=pltpu.HBM)] * 4,
        out_specs=pl.BlockSpec(memory_space=pl.ANY),
        scratch_shapes=[
            pltpu.VMEM((BLOCKS, heads, 2, rows, HEAD_DIM), jnp.bfloat16),
            pltpu.VMEM((heads * GROUP, rows, HEAD_DIM), jnp.bfloat16),
            pltpu.VMEM((RELAY, LANES, rows), jnp.bfloat16),
            pltpu.VMEM((rows, LANES), jnp.bfloat16),
            pltpu.VMEM((24, LANES), jnp.int32),
            pltpu.VMEM((heads, GROUP, rows, LANES), jnp.float32),
            pltpu.VMEM((heads, GROUP, rows, 2 * HEAD_DIM), jnp.float32),
            pltpu.VMEM((heads * GROUP, rows, HEAD_DIM), jnp.bfloat16),
            pltpu.VMEM((GROUP * rows, 6 * rows), jnp.float32),
            pltpu.VMEM((GROUP * rows, 6 * rows), jnp.float32),
            pltpu.SemaphoreType.DMA((KINDS, heads)),
            pltpu.SemaphoreType.DMA((BLOCKS, heads)),
            pltpu.SemaphoreType.DMA((heads * GROUP,)),
            pltpu.SemaphoreType.DMA((2, heads)),
            pltpu.SemaphoreType.DMA((3,)),
            pltpu.SemaphoreType.DMA((heads * GROUP,)),
        ],
        compiler_params=pltpu.CompilerParams(
            collective_id=0, has_side_effects=True, vmem_limit_bytes=40 * 1024 * 1024
        ),
    )(*[pltpu.with_memory_space_constraint(a, pltpu.HBM) for a in (queries, keys, values, docs)])


def solution(mesh):
    placed = P(("section", "attn"), None)
    return jax.shard_map(
        functools.partial(shards, mesh.shape["section"]),
        mesh=mesh,
        in_specs=(placed, placed, placed, P()),
        out_specs=placed,
        check_vma=False,
    )
```

```python
import functools
import math

import jax
import jax.numpy as jnp
from jax import lax
from jax.experimental import pallas as pl
from jax.experimental.pallas import tpu as pltpu
from jax.sharding import PartitionSpec as P

MESH = pl.DeviceIdType.MESH
HEAD_DIM = 128
GROUP = 3
RING = 4
LANES = 128
NEG = -1e30

OWN, EXTRA, BACK1, BACK2, BACK3, RELAY, RELAY2 = 0, 1, 2, 4, 6, 8, 9
BLOCKS = 10
UP, RIGHT, LEFT, NEXT, PREV, SIDE_EXTRA, SIDE1, SIDE2, SIDE3, ROUND, CROSS1, CROSS3, DOWN = range(13)
KINDS = 13


def attention_kernel(
    sections, rows, heads,
    q_hbm, k_hbm, v_hbm, docs_hbm, out_hbm,
    kv, q, onehot, away, docs, stat_max, acc, out, held0, held1,
    send_sem, recv_sem, q_sem, kv_sem, doc_sem, out_sem,
):
    half = heads // 2
    scale = math.log2(math.e) * HEAD_DIM ** (-0.5)
    s = lax.axis_index("section")
    c = lax.axis_index("attn")
    x = lax.rem(s, RING)
    row_start = s - x
    first, last = x == 0, x == RING - 1
    top, bottom = s < RING, s >= sections - RING
    below = jnp.logical_not(top)
    from_left = jnp.where(jnp.logical_and(bottom, x == 2), heads - 2, half)
    crossing = jnp.logical_and(lax.rem(s, RING * RING) < RING, below)
    express = heads - 2

    right = row_start + lax.rem(x + 1, RING)
    left = row_start + lax.rem(x + RING - 1, RING)
    up = lax.rem(s + RING, sections)
    down = lax.rem(s + sections - RING, sections)
    following = lax.rem(s + 1, sections)
    previous = lax.rem(s + sections - 1, sections)
    other = 1 - c
    up_core = jnp.where(first, other, c)

    def load_kv(j):
        at = pl.ds(pl.multiple_of(j * HEAD_DIM, HEAD_DIM), HEAD_DIM)
        return (
            pltpu.make_async_copy(k_hbm.at[:, at], kv.at[OWN, j, 0], kv_sem.at[0, j]),
            pltpu.make_async_copy(v_hbm.at[:, at], kv.at[OWN, j, 1], kv_sem.at[1, j]),
        )

    def load_q(h):
        at = pl.ds(pl.multiple_of(h * HEAD_DIM, HEAD_DIM), HEAD_DIM)
        return pltpu.make_async_copy(q_hbm.at[:, at], q.at[h], q_sem.at[h])

    def load_docs(piece):
        pair = lax.rem(lax.div(s, 2) + sections // 2 - 2 + piece, sections // 2)
        return pltpu.make_async_copy(
            docs_hbm.at[pl.ds(pl.multiple_of(pair * 8, 8), 8), :],
            docs.at[pl.ds(piece * 8, 8), :],
            doc_sem.at[piece],
        )

    @pl.loop(0, heads)
    def _(j):
        for copy in load_kv(j):
            copy.start()

    for piece in range(3):
        load_docs(piece).start()

    @pl.when(top)
    def _():
        @pl.loop(EXTRA, RELAY)
        def _(block):
            @pl.loop(0, heads)
            def _(j):
                kv[block, j] = jnp.zeros((2, rows, HEAD_DIM), kv.dtype)

    up_open = jnp.logical_not(bottom)
    down_open = below

    barrier = pltpu.get_barrier_semaphore()

    def greet(section, core):
        pl.semaphore_signal(barrier, inc=1, device_id=(section, core), device_id_type=MESH)

    greet(s, other)
    greet(right, c)
    greet(left, c)
    @pl.when(up_open)
    def _():
        greet(up, up_core)

    @pl.when(down_open)
    def _():
        greet(down, up_core)

    from_next = jnp.logical_and(last, up_open)
    to_previous = jnp.logical_and(first, down_open)

    @pl.when(to_previous)
    def _():
        greet(previous, c)
        greet(down, c)

    @pl.when(jnp.logical_and(first, up_open))
    def _():
        greet(up, c)

    @pl.when(from_next)
    def _():
        greet(following, c)

    @pl.loop(0, heads * GROUP)
    def _(h):
        load_q(h).start()

    def send(kind, j, source, target, section, core):
        return pltpu.make_async_remote_copy(
            src_ref=kv.at[source, j],
            dst_ref=kv.at[target, j],
            send_sem=send_sem.at[kind, j],
            recv_sem=recv_sem.at[target, j],
            device_id=(section, core),
            device_id_type=MESH,
        )

    def arrived(block, j):
        send(UP, j, block, block, s, other).wait_recv()

    up_target = jnp.where(first, EXTRA, RELAY)
    def send_up(j):
        return send(UP, j, OWN, up_target, up, up_core)

    def send_right(j):
        ahead = jnp.logical_and(last, j >= express)
        source = jnp.where(jnp.logical_and(last, j < express), RELAY, OWN)
        return send(RIGHT, j, source, jnp.where(ahead, RELAY, BACK1 + c), right, c)

    def send_left(j):
        own = jnp.logical_or(jnp.logical_or(first, top), j >= express)
        ahead = jnp.logical_and(own, x > 0)
        source = jnp.where(own, OWN, RELAY)
        return send(LEFT, j, source, jnp.where(ahead, RELAY2, BACK3 + c), left, c)

    def send_cross1(j):
        return send(CROSS1, j, RELAY, BACK1 + c, up, c)

    def send_cross3(j):
        return send(CROSS3, j, RELAY2, BACK3 + c, up, c)

    def send_next(j):
        target = jnp.where(last, RELAY2, BACK2 + c)
        return send(NEXT, j, BACK1 + c, target, jnp.where(last, up, following), c)

    def send_round(j):
        return send(ROUND, j, RELAY2, BACK2 + c, jnp.where(first, left, right), c)

    def send_prev(j):
        around = jnp.logical_and(first, crossing)
        target = jnp.where(around, RELAY2, BACK2 + c)
        return send(PREV, j, BACK3 + c, target, jnp.where(around, left, previous), c)

    def send_down(j):
        return send(DOWN, j, RELAY2, BACK2 + c, down, c)

    def send_extra(j):
        return send(SIDE_EXTRA, j, jnp.where(c == 0, OWN, RELAY), EXTRA, s, other)

    def send_side(kind, j, block):
        return send(kind, j, block + c, block + c, s, other)

    def both(*conditions):
        return functools.reduce(jnp.logical_and, conditions)

    def either(*conditions):
        return functools.reduce(jnp.logical_or, conditions)

    def sends_up(j):
        return both(up_open, either(c == 1, both(x > 0, j < express)))

    def right_ahead(j):
        return either(jnp.logical_not(last), both(up_open, j >= express))

    def left_ahead(j):
        return either(
            first,
            both(x > 0, either(up_open, x == 1), j >= express),
            both(top, x == 1, j >= half),
        )

    def relays(j):
        return both(x > 0, below, j < express)

    crosses1 = both(first, up_open)
    crosses3 = both(jnp.logical_not(last), up_open)
    descends = both(last, crossing)

    def turns_on(j):
        return both(first, either(both(top, j >= half), both(bottom, j >= express)))

    has1 = either(below, x > 0)
    has2 = either(below, x > 1)
    has3 = either(below, last)

    def has_extra():
        return either(c == 1, below)

    relays_extra = both(x > 0, below, c == 1)
    sends_next = both(has1, jnp.logical_not(both(bottom, last)))
    sends_prev = either(both(below, s != RING), last)

    @pl.loop(0, heads)
    def _(j):
        for copy in load_kv(j):
            copy.wait()

    pl.semaphore_wait(
        barrier,
        3
        + jnp.where(from_next, 1, 0)
        + jnp.where(to_previous, 2, 0)
        + jnp.where(jnp.logical_and(first, up_open), 1, 0)
        + jnp.where(up_open, 1, 0) + jnp.where(down_open, 1, 0),
    )

    @pl.loop(0, heads)
    def _(j):
        @pl.when(sends_up(j))
        def _():
            send_up(j).start()

        @pl.when(right_ahead(j))
        def _():
            send_right(j).start()

        @pl.when(left_ahead(j))
        def _():
            send_left(j).start()

        @pl.when(c == 0)
        def _():
            send_extra(j).start()

    for piece in range(3):
        load_docs(piece).wait()
    parity = lax.rem(s, 2)
    pieces = rows // LANES
    places = ((0, c), (4 * other, other), (1, 0), (1, 1), (2, 0), (2, 1), (3, 0), (3, 1))
    ids = lax.broadcasted_iota(jnp.int32, (LANES, LANES), 0)
    for block, (back, core) in enumerate(places):
        for piece in range(pieces):
            row = (4 + parity - back) * (2 * pieces) + core * pieces + piece
            same = jnp.where(docs[pl.ds(row, 1), :] == ids, 1.0, 0.0)
            span = slice(piece * LANES, (piece + 1) * LANES)
            onehot[block, :, span] = same.astype(jnp.bfloat16)
            if block == OWN:
                away[span, :] = jnp.transpose((1.0 - same) * NEG).astype(jnp.bfloat16)

    @pl.loop(0, heads * GROUP)
    def _(h):
        load_q(h).wait()

    def keys_of(block, j):
        return jnp.concatenate([jnp.transpose(kv[block, j, 0]), onehot[block]], axis=0)

    def scores(query, key):
        return jnp.dot(query, key, preferred_element_type=jnp.float32)

    def wide(column):
        return jnp.concatenate([column] * (rows // LANES), axis=1)

    def values_of(block, j):
        value = kv[block, j, 1]
        return jnp.concatenate([value, jnp.ones_like(value)], axis=1)

    def query_of(j, r):
        return jnp.concatenate([q[j * GROUP + r], away[...]], axis=1)

    def weigh(parts, top, blocks, j):
        total = None
        for part, block in zip(parts, blocks):
            weights = jnp.exp2((part - top) * scale).astype(jnp.bfloat16)
            product = jnp.dot(weights, values_of(block, j), preferred_element_type=jnp.float32)
            total = product if total is None else total + product
        return total

    early = (OWN, EXTRA, BACK1, BACK1 + 1, BACK3, BACK3 + 1)
    late = (BACK2, BACK2 + 1)
    causal = lax.broadcasted_iota(jnp.int32, (rows, rows), 1) <= lax.broadcasted_iota(
        jnp.int32, (rows, rows), 0
    )

    def row_max(parts):
        return jnp.broadcast_to(
            jnp.max(functools.reduce(jnp.maximum, parts), axis=1, keepdims=True), (rows, LANES)
        )

    def finish_late(j, r, parts):
        old = stat_max[j, r]
        top = jnp.maximum(old, row_max(parts))
        rescale = jnp.exp2((old - top) * scale)
        summed = acc[j, r] * wide(rescale) + weigh(parts, wide(top), late, j)
        out[j * GROUP + r] = (summed[:, :HEAD_DIM] / summed[:, HEAD_DIM:]).astype(jnp.bfloat16)

    def finish_early(j, r, parts):
        parts[0] = jnp.where(causal, parts[0], NEG)
        top = row_max(parts)
        stat_max[j, r] = top
        acc[j, r] = weigh(parts, wide(top), early, j)

    def score(blocks, j, held):
        query = jnp.concatenate([query_of(j, r) for r in range(GROUP)], axis=0)
        for at, block in enumerate(blocks):
            held[:, at * rows:(at + 1) * rows] = scores(query, keys_of(block, j))

    def parts_of(blocks, r, held):
        return [
            held[r * rows:(r + 1) * rows, at * rows:(at + 1) * rows] for at in range(len(blocks))
        ]

    def fold_early(j, held):
        for r in range(GROUP):
            finish_early(j, r, parts_of(early, r, held))

    def fold_late(j, held):
        for r in range(GROUP):
            finish_late(j, r, parts_of(late, r, held))

    def store_out(h):
        at = pl.ds(pl.multiple_of(h * HEAD_DIM, HEAD_DIM), HEAD_DIM)
        return pltpu.make_async_copy(out.at[h], out_hbm.at[:, at], out_sem.at[h])

    def pass_relay(j):
        @pl.when(relays(j))
        def _():
            arrived(RELAY, j)
            send_left(j).start()

        @pl.when(both(relays_extra, j >= express))
        def _():
            arrived(RELAY, j)

        @pl.when(both(last, relays(j)))
        def _():
            send_right(j).start()

        @pl.when(relays_extra)
        def _():
            send_extra(j).start()

    def pass_across(j):
        @pl.when(crosses3)
        def _():
            arrived(RELAY2, j)
            send_cross3(j).start()

        @pl.when(crosses1)
        def _():
            arrived(RELAY, j)
            send_cross1(j).start()

    def pass_aside(j):
        @pl.when(has1)
        def _():
            arrived(BACK1 + c, j)
            send_side(SIDE1, j, BACK1).start()

        @pl.when(has3)
        def _():
            arrived(BACK3 + c, j)
            send_side(SIDE3, j, BACK3).start()

    def next_range(step):
        in_pairs = step < heads
        low = jnp.where(in_pairs, 2 * (step - (heads - 3)), step - 2)
        high = jnp.minimum(low + jnp.where(in_pairs, 2, 1), from_left)
        return both(sends_next, step >= heads - 3, step <= heads + 1), low, high

    rounds = both(last, below)

    def pass_round(j):
        @pl.when(either(j < express, bottom))
        def _():
            arrived(RELAY2, j)

        send_round(j).start()

    def pass_down(j):
        arrived(RELAY2, j)
        send_down(j).start()

    def early_ready(j):
        @pl.when(has_extra())
        def _():
            arrived(EXTRA, j)

        @pl.when(has1)
        def _():
            arrived(BACK1 + other, j)

        @pl.when(has3)
        def _():
            arrived(BACK3 + other, j)

    def move(step):
        @pl.when(step < heads)
        def _():
            pass_relay(step)

        sending, low, high = next_range(step)

        @pl.when(sending)
        def _():
            @pl.loop(low, high)
            def _(j):
                send_next(j).start()

        @pl.when(both(sends_prev, step >= half + 2, step < heads + 2))
        def _():
            send_prev(step - 2).start()

        @pl.when(step == 2)
        def _():
            for j in range(express, heads):
                pass_across(j)

        @pl.when(both(turns_on(step), step < heads))
        def _():
            pass_round(step)

        @pl.when(both(rounds, step >= heads, step < heads + 3))
        def _():
            pass_round(step - heads)

        @pl.when(both(descends, step > heads, step < heads + 3))
        def _():
            pass_down(half + step - (heads + 1))

    buffers = (held0, held1)

    @pl.loop(0, (heads + 4) // 2)
    def _(pair):
        for side in range(2):
            step = 2 * pair + side
            now, before = buffers[side], buffers[1 - side]
            move(step)

            @pl.when(both(step >= 2, step < heads + 2))
            def _():
                early_ready(step - 2)

            @pl.when(step == 2)
            def _():
                score(early, step - 2, now)

            @pl.when(both(step > 2, step < heads + 2))
            def _():
                score(early, step - 2, now)
                fold_early(step - 3, before)

            @pl.when(step == heads + 2)
            def _():
                fold_early(step - 3, before)

            @pl.when(both(step >= 1, step <= heads))
            def _():
                pass_aside(step - 1)

    def late_head(k):
        odd = lax.rem(k, 2)
        evenly = half * odd + lax.div(k, 2)
        turned = jnp.where(k < 2, k, jnp.where(k < 4, express + k - 2, k - 2))
        mixed = jnp.where(odd == 1, lax.div(k + 1, 2), half - 1 + lax.div(k, 2))
        delayed = jnp.where(k == 0, 0, jnp.where(k == heads - 1, k, mixed))
        waits_down = both(last, up_open, lax.rem(s, RING * RING) >= RING * (RING - 1))
        return jnp.where(both(bottom, last), turned, jnp.where(waits_down, delayed, evenly))

    def pass_late(k):
        @pl.when(has2)
        def _():
            j = late_head(k)
            arrived(BACK2 + c, j)
            send_side(SIDE2, j, BACK2).start()

    def late_ready(k):
        @pl.when(has2)
        def _():
            arrived(BACK2 + other, late_head(k))

    def move_late(k):
        @pl.when(both(rounds, k == 1))
        def _():
            pass_round(half - 1)

        @pl.when(both(descends, either(k == 2, k == 4)))
        def _():
            pass_down(half + 1 + lax.div(k, 2))

        @pl.when(k + 1 < heads)
        def _():
            pass_late(k + 1)

    def store_head(j):
        for r in range(GROUP):
            store_out(j * GROUP + r).start()

    pass_late(0)

    @pl.loop(0, heads // 2)
    def _(pair):
        for side in range(2):
            k = 2 * pair + side
            now, before = buffers[side], buffers[1 - side]
            move_late(k)
            late_ready(k)

            if side == 0:
                @pl.when(pair == 0)
                def _():
                    score(late, late_head(k), now)

                @pl.when(pair > 0)
                def _():
                    score(late, late_head(k), now)
                    fold_late(late_head(k - 1), before)
                    store_head(late_head(k - 1))
            else:
                score(late, late_head(k), now)
                fold_late(late_head(k - 1), before)
                store_head(late_head(k - 1))

    fold_late(late_head(heads - 1), buffers[1])
    store_head(late_head(heads - 1))

    @pl.loop(0, heads)
    def _(j):
        for r in range(GROUP):
            store_out(j * GROUP + r).wait()

        @pl.when(sends_up(j))
        def _():
            send_up(j).wait_send()

        @pl.when(either(right_ahead(j), both(below, j < express)))
        def _():
            send_right(j).wait_send()

        @pl.when(both(crosses1, j >= express))
        def _():
            send_cross1(j).wait_send()

        @pl.when(both(crosses3, j >= express))
        def _():
            send_cross3(j).wait_send()

        @pl.when(either(left_ahead(j), relays(j)))
        def _():
            send_left(j).wait_send()

        @pl.when(has1)
        def _():
            send_side(SIDE1, j, BACK1).wait_send()

        @pl.when(has2)
        def _():
            send_side(SIDE2, j, BACK2).wait_send()

        @pl.when(has3)
        def _():
            send_side(SIDE3, j, BACK3).wait_send()

        @pl.when(either(c == 0, relays_extra))
        def _():
            send_extra(j).wait_send()

        @pl.when(both(sends_next, j < from_left))
        def _():
            send_next(j).wait_send()

        @pl.when(both(descends, j >= half))
        def _():
            send_down(j).wait_send()

        @pl.when(either(both(rounds, j < half), turns_on(j)))
        def _():
            send_round(j).wait_send()

        @pl.when(both(sends_prev, j >= half))
        def _():
            send_prev(j).wait_send()


def shards(sections, queries, keys, values, doc_ids):
    rows, heads = queries.shape[0], keys.shape[1] // HEAD_DIM
    docs = doc_ids.reshape(-1, LANES)
    return pl.pallas_call(
        functools.partial(attention_kernel, sections, rows, heads),
        out_shape=jax.ShapeDtypeStruct(queries.shape, jnp.bfloat16),
        in_specs=[pl.BlockSpec(memory_space=pltpu.HBM)] * 4,
        out_specs=pl.BlockSpec(memory_space=pl.ANY),
        scratch_shapes=[
            pltpu.VMEM((BLOCKS, heads, 2, rows, HEAD_DIM), jnp.bfloat16),
            pltpu.VMEM((heads * GROUP, rows, HEAD_DIM), jnp.bfloat16),
            pltpu.VMEM((RELAY, LANES, rows), jnp.bfloat16),
            pltpu.VMEM((rows, LANES), jnp.bfloat16),
            pltpu.VMEM((24, LANES), jnp.int32),
            pltpu.VMEM((heads, GROUP, rows, LANES), jnp.float32),
            pltpu.VMEM((heads, GROUP, rows, 2 * HEAD_DIM), jnp.float32),
            pltpu.VMEM((heads * GROUP, rows, HEAD_DIM), jnp.bfloat16),
            pltpu.VMEM((GROUP * rows, 6 * rows), jnp.float32),
            pltpu.VMEM((GROUP * rows, 6 * rows), jnp.float32),
            pltpu.SemaphoreType.DMA((KINDS, heads)),
            pltpu.SemaphoreType.DMA((BLOCKS, heads)),
            pltpu.SemaphoreType.DMA((heads * GROUP,)),
            pltpu.SemaphoreType.DMA((2, heads)),
            pltpu.SemaphoreType.DMA((3,)),
            pltpu.SemaphoreType.DMA((heads * GROUP,)),
        ],
        compiler_params=pltpu.CompilerParams(
            collective_id=0, has_side_effects=True, vmem_limit_bytes=40 * 1024 * 1024
        ),
    )(*[pltpu.with_memory_space_constraint(a, pltpu.HBM) for a in (queries, keys, values, docs)])


def solution(mesh):
    placed = P(("section", "attn"), None)
    return jax.shard_map(
        functools.partial(shards, mesh.shape["section"]),
        mesh=mesh,
        in_specs=(placed, placed, placed, P()),
        out_specs=placed,
        check_vma=False,
    )
```

```python
import functools
import math

import jax
import jax.numpy as jnp
from jax import lax
from jax.experimental import pallas as pl
from jax.experimental.pallas import tpu as pltpu
from jax.sharding import PartitionSpec as P

MESH = pl.DeviceIdType.MESH
HEAD_DIM = 128
GROUP = 3
RING = 4
LANES = 128
NEG = -1e30

OWN, EXTRA, BACK1, BACK2, BACK3, RELAY, RELAY2 = 0, 1, 2, 4, 6, 8, 9
BLOCKS = 10
UP, RIGHT, LEFT, NEXT, PREV, SIDE_EXTRA, SIDE1, SIDE2, SIDE3, ROUND, CROSS1, CROSS3, DOWN = range(13)
KINDS = 13


def attention_kernel(
    sections, rows, heads,
    q_hbm, k_hbm, v_hbm, docs_hbm, out_hbm,
    kv, q, onehot, away, docs, stat_max, acc, out, held0, held1,
    send_sem, recv_sem, q_sem, kv_sem, doc_sem, out_sem,
):
    half = heads // 2
    scale = math.log2(math.e) * HEAD_DIM ** (-0.5)
    s = lax.axis_index("section")
    c = lax.axis_index("attn")
    x = lax.rem(s, RING)
    row_start = s - x
    first, last = x == 0, x == RING - 1
    top, bottom = s < RING, s >= sections - RING
    below = jnp.logical_not(top)
    crossing = jnp.logical_and(lax.rem(s, RING * RING) < RING, below)
    before_crossing = lax.rem(s, RING * RING) >= RING * (RING - 1)
    from_left = jnp.where(
        x == 2, jnp.where(bottom, heads - 2, jnp.where(before_crossing, half + 1, half)), half
    )
    from_right = jnp.where(jnp.logical_and(first, crossing), half + 1, half)
    express = heads - 2

    right = row_start + lax.rem(x + 1, RING)
    left = row_start + lax.rem(x + RING - 1, RING)
    up = lax.rem(s + RING, sections)
    down = lax.rem(s + sections - RING, sections)
    following = lax.rem(s + 1, sections)
    previous = lax.rem(s + sections - 1, sections)
    other = 1 - c
    up_core = jnp.where(first, other, c)

    def load_kv(j):
        at = pl.ds(pl.multiple_of(j * HEAD_DIM, HEAD_DIM), HEAD_DIM)
        return (
            pltpu.make_async_copy(k_hbm.at[:, at], kv.at[OWN, j, 0], kv_sem.at[0, j]),
            pltpu.make_async_copy(v_hbm.at[:, at], kv.at[OWN, j, 1], kv_sem.at[1, j]),
        )

    def load_q(h):
        at = pl.ds(pl.multiple_of(h * HEAD_DIM, HEAD_DIM), HEAD_DIM)
        return pltpu.make_async_copy(q_hbm.at[:, at], q.at[h], q_sem.at[h])

    def load_docs(piece):
        pair = lax.rem(lax.div(s, 2) + sections // 2 - 2 + piece, sections // 2)
        return pltpu.make_async_copy(
            docs_hbm.at[pl.ds(pl.multiple_of(pair * 8, 8), 8), :],
            docs.at[pl.ds(piece * 8, 8), :],
            doc_sem.at[piece],
        )

    @pl.loop(0, heads)
    def _(j):
        for copy in load_kv(j):
            copy.start()

    for piece in range(3):
        load_docs(piece).start()

    @pl.when(top)
    def _():
        @pl.loop(EXTRA, RELAY)
        def _(block):
            @pl.loop(0, heads)
            def _(j):
                kv[block, j] = jnp.zeros((2, rows, HEAD_DIM), kv.dtype)

    up_open = jnp.logical_not(bottom)
    down_open = below

    barrier = pltpu.get_barrier_semaphore()

    def greet(section, core):
        pl.semaphore_signal(barrier, inc=1, device_id=(section, core), device_id_type=MESH)

    greet(s, other)
    greet(right, c)
    greet(left, c)
    @pl.when(up_open)
    def _():
        greet(up, up_core)

    @pl.when(down_open)
    def _():
        greet(down, up_core)

    from_next = jnp.logical_and(last, up_open)
    to_previous = jnp.logical_and(first, down_open)

    @pl.when(to_previous)
    def _():
        greet(previous, c)
        greet(down, c)

    @pl.when(jnp.logical_and(first, up_open))
    def _():
        greet(up, c)

    @pl.when(from_next)
    def _():
        greet(following, c)

    @pl.loop(0, heads * GROUP)
    def _(h):
        load_q(h).start()

    def send(kind, j, source, target, section, core):
        return pltpu.make_async_remote_copy(
            src_ref=kv.at[source, j],
            dst_ref=kv.at[target, j],
            send_sem=send_sem.at[kind, j],
            recv_sem=recv_sem.at[target, j],
            device_id=(section, core),
            device_id_type=MESH,
        )

    def arrived(block, j):
        send(UP, j, block, block, s, other).wait_recv()

    up_target = jnp.where(first, EXTRA, RELAY)
    def send_up(j):
        return send(UP, j, OWN, up_target, up, up_core)

    def send_right(j):
        ahead = jnp.logical_and(last, j >= express)
        source = jnp.where(jnp.logical_and(last, j < express), RELAY, OWN)
        return send(RIGHT, j, source, jnp.where(ahead, RELAY, BACK1 + c), right, c)

    def send_left(j):
        own = jnp.logical_or(jnp.logical_or(first, top), j >= express)
        ahead = jnp.logical_and(own, x > 0)
        source = jnp.where(own, OWN, RELAY)
        return send(LEFT, j, source, jnp.where(ahead, RELAY2, BACK3 + c), left, c)

    def send_cross1(j):
        return send(CROSS1, j, RELAY, BACK1 + c, up, c)

    def send_cross3(j):
        return send(CROSS3, j, RELAY2, BACK3 + c, up, c)

    def send_next(j):
        target = jnp.where(last, RELAY2, BACK2 + c)
        return send(NEXT, j, BACK1 + c, target, jnp.where(last, up, following), c)

    def send_round(j):
        return send(ROUND, j, RELAY2, BACK2 + c, jnp.where(first, left, right), c)

    def send_prev(j):
        around = jnp.logical_and(first, crossing)
        target = jnp.where(around, RELAY2, BACK2 + c)
        return send(PREV, j, BACK3 + c, target, jnp.where(around, left, previous), c)

    def send_down(j):
        return send(DOWN, j, RELAY2, BACK2 + c, down, c)

    def send_extra(j):
        return send(SIDE_EXTRA, j, jnp.where(c == 0, OWN, RELAY), EXTRA, s, other)

    def send_side(kind, j, block):
        return send(kind, j, block + c, block + c, s, other)

    def both(*conditions):
        return functools.reduce(jnp.logical_and, conditions)

    def either(*conditions):
        return functools.reduce(jnp.logical_or, conditions)

    def sends_up(j):
        return both(up_open, either(c == 1, both(x > 0, j < express)))

    def right_ahead(j):
        return either(jnp.logical_not(last), both(up_open, j >= express))

    def left_ahead(j):
        return either(
            first,
            both(x > 0, either(up_open, x == 1), j >= express),
            both(top, x == 1, j >= half),
        )

    def relays(j):
        return both(x > 0, below, j < express)

    crosses1 = both(first, up_open)
    crosses3 = both(jnp.logical_not(last), up_open)
    descends = both(last, crossing)

    def turns_on(j):
        return both(first, either(both(top, j >= half), both(bottom, j >= express)))

    has1 = either(below, x > 0)
    has2 = either(below, x > 1)
    has3 = either(below, last)

    def has_extra():
        return either(c == 1, below)

    relays_extra = both(x > 0, below, c == 1)
    sends_next = both(has1, jnp.logical_not(both(bottom, last)))
    sends_prev = either(both(below, s != RING), last)

    @pl.loop(0, heads)
    def _(j):
        for copy in load_kv(j):
            copy.wait()

    pl.semaphore_wait(
        barrier,
        3
        + jnp.where(from_next, 1, 0)
        + jnp.where(to_previous, 2, 0)
        + jnp.where(jnp.logical_and(first, up_open), 1, 0)
        + jnp.where(up_open, 1, 0) + jnp.where(down_open, 1, 0),
    )

    @pl.loop(0, heads)
    def _(j):
        @pl.when(sends_up(j))
        def _():
            send_up(j).start()

        @pl.when(right_ahead(j))
        def _():
            send_right(j).start()

        @pl.when(left_ahead(j))
        def _():
            send_left(j).start()

        @pl.when(c == 0)
        def _():
            send_extra(j).start()

    for piece in range(3):
        load_docs(piece).wait()
    parity = lax.rem(s, 2)
    pieces = rows // LANES
    places = ((0, c), (4 * other, other), (1, 0), (1, 1), (2, 0), (2, 1), (3, 0), (3, 1))
    ids = lax.broadcasted_iota(jnp.int32, (LANES, LANES), 0)
    for block, (back, core) in enumerate(places):
        for piece in range(pieces):
            row = (4 + parity - back) * (2 * pieces) + core * pieces + piece
            same = jnp.where(docs[pl.ds(row, 1), :] == ids, 1.0, 0.0)
            span = slice(piece * LANES, (piece + 1) * LANES)
            onehot[block, :, span] = same.astype(jnp.bfloat16)
            if block == OWN:
                away[span, :] = jnp.transpose((1.0 - same) * NEG).astype(jnp.bfloat16)

    @pl.loop(0, heads * GROUP)
    def _(h):
        load_q(h).wait()

    def keys_of(block, j):
        return jnp.concatenate([jnp.transpose(kv[block, j, 0]), onehot[block]], axis=0)

    def scores(query, key):
        return jnp.dot(query, key, preferred_element_type=jnp.float32)

    def wide(column):
        return jnp.concatenate([column] * (rows // LANES), axis=1)

    def values_of(block, j):
        value = kv[block, j, 1]
        return jnp.concatenate([value, jnp.ones_like(value)], axis=1)

    def query_of(j, r):
        return jnp.concatenate([q[j * GROUP + r], away[...]], axis=1)

    def weigh(parts, top, blocks, j):
        total = None
        for part, block in zip(parts, blocks):
            weights = jnp.exp2((part - top) * scale).astype(jnp.bfloat16)
            product = jnp.dot(weights, values_of(block, j), preferred_element_type=jnp.float32)
            total = product if total is None else total + product
        return total

    early = (OWN, EXTRA, BACK1, BACK1 + 1, BACK3, BACK3 + 1)
    late = (BACK2, BACK2 + 1)
    causal = lax.broadcasted_iota(jnp.int32, (rows, rows), 1) <= lax.broadcasted_iota(
        jnp.int32, (rows, rows), 0
    )

    def row_max(parts):
        return jnp.broadcast_to(
            jnp.max(functools.reduce(jnp.maximum, parts), axis=1, keepdims=True), (rows, LANES)
        )

    def finish_late(j, r, parts):
        old = stat_max[j, r]
        top = jnp.maximum(old, row_max(parts))
        rescale = jnp.exp2((old - top) * scale)
        summed = acc[j, r] * wide(rescale) + weigh(parts, wide(top), late, j)
        out[j * GROUP + r] = (summed[:, :HEAD_DIM] / summed[:, HEAD_DIM:]).astype(jnp.bfloat16)

    def finish_early(j, r, parts):
        parts[0] = jnp.where(causal, parts[0], NEG)
        top = row_max(parts)
        stat_max[j, r] = top
        acc[j, r] = weigh(parts, wide(top), early, j)

    def score(blocks, j, held):
        query = jnp.concatenate([query_of(j, r) for r in range(GROUP)], axis=0)
        for at, block in enumerate(blocks):
            held[:, at * rows:(at + 1) * rows] = scores(query, keys_of(block, j))

    def parts_of(blocks, r, held):
        return [
            held[r * rows:(r + 1) * rows, at * rows:(at + 1) * rows] for at in range(len(blocks))
        ]

    def fold_early(j, held):
        for r in range(GROUP):
            finish_early(j, r, parts_of(early, r, held))

    def fold_late(j, held):
        for r in range(GROUP):
            finish_late(j, r, parts_of(late, r, held))

    def store_out(h):
        at = pl.ds(pl.multiple_of(h * HEAD_DIM, HEAD_DIM), HEAD_DIM)
        return pltpu.make_async_copy(out.at[h], out_hbm.at[:, at], out_sem.at[h])

    def pass_relay(j):
        @pl.when(relays(j))
        def _():
            arrived(RELAY, j)
            send_left(j).start()

        @pl.when(both(relays_extra, j >= express))
        def _():
            arrived(RELAY, j)

        @pl.when(both(last, relays(j)))
        def _():
            send_right(j).start()

        @pl.when(relays_extra)
        def _():
            send_extra(j).start()

    def pass_across(j):
        @pl.when(crosses3)
        def _():
            arrived(RELAY2, j)
            send_cross3(j).start()

        @pl.when(crosses1)
        def _():
            arrived(RELAY, j)
            send_cross1(j).start()

    def pass_aside(j):
        @pl.when(has1)
        def _():
            arrived(BACK1 + c, j)
            send_side(SIDE1, j, BACK1).start()

        @pl.when(has3)
        def _():
            arrived(BACK3 + c, j)
            send_side(SIDE3, j, BACK3).start()

    def next_range(step):
        in_pairs = step < heads
        low = jnp.where(in_pairs, 2 * (step - (heads - 3)), step - 2)
        high = jnp.minimum(low + jnp.where(in_pairs, 2, 1), from_left)
        return both(sends_next, step >= heads - 3, step <= heads + 1), low, high

    rounds = both(last, below)

    def pass_round(j):
        @pl.when(either(j < express, bottom))
        def _():
            arrived(RELAY2, j)

        send_round(j).start()

    def pass_down(j):
        arrived(RELAY2, j)
        send_down(j).start()

    def early_ready(j):
        @pl.when(has_extra())
        def _():
            arrived(EXTRA, j)

        @pl.when(has1)
        def _():
            arrived(BACK1 + other, j)

        @pl.when(has3)
        def _():
            arrived(BACK3 + other, j)

    def move(step):
        @pl.when(step < heads)
        def _():
            pass_relay(step)

        @pl.when(both(step >= 2, step < heads + 2))
        def _():
            pass_aside(step - 2)

        sending, low, high = next_range(step)

        @pl.when(sending)
        def _():
            @pl.loop(low, high)
            def _(j):
                send_next(j).start()

        @pl.when(both(sends_prev, step >= from_right + 2, step < heads + 2))
        def _():
            send_prev(step - 2).start()

        @pl.when(step == 2)
        def _():
            for j in range(express, heads):
                pass_across(j)

        @pl.when(both(turns_on(step), step < heads))
        def _():
            pass_round(step)

        @pl.when(both(rounds, step >= heads))
        def _():
            pass_round(step - heads)

        @pl.when(both(descends, step > heads))
        def _():
            pass_down(half + step - heads)

    buffers = (held0, held1)

    @pl.loop(0, (heads + 4) // 2)
    def _(pair):
        for side in range(2):
            step = 2 * pair + side
            now, before = buffers[side], buffers[1 - side]
            move(step)

            @pl.when(both(step >= 3, step < heads + 3))
            def _():
                early_ready(step - 3)

            @pl.when(step == 3)
            def _():
                score(early, step - 3, now)

            @pl.when(both(step > 3, step < heads + 3))
            def _():
                score(early, step - 3, now)
                fold_early(step - 4, before)

            @pl.when(step == heads + 3)
            def _():
                fold_early(step - 4, before)

    def late_head(k):
        odd = lax.rem(k, 2)
        evenly = half * odd + lax.div(k, 2)
        turned = jnp.where(k < 2, k, jnp.where(k < 4, express + k - 2, k - 2))
        mixed = jnp.where(odd == 1, half + 1 + lax.div(k - 3, 2), lax.div(k, 2) + 1)
        delayed = jnp.where(k < 3, k, mixed)
        waits_down = both(last, up_open, before_crossing)
        return jnp.where(both(bottom, last), turned, jnp.where(waits_down, delayed, evenly))

    def pass_late(k):
        @pl.when(has2)
        def _():
            j = late_head(k)
            arrived(BACK2 + c, j)
            send_side(SIDE2, j, BACK2).start()

    def late_ready(k):
        @pl.when(has2)
        def _():
            arrived(BACK2 + other, late_head(k))

    def move_late(k):
        @pl.when(k + 1 < heads)
        def _():
            pass_late(k + 1)

    def store_head(j):
        for r in range(GROUP):
            store_out(j * GROUP + r).start()

    pass_late(0)

    @pl.loop(0, heads // 2)
    def _(pair):
        for side in range(2):
            k = 2 * pair + side
            now, before = buffers[side], buffers[1 - side]
            move_late(k)
            late_ready(k)

            if side == 0:
                @pl.when(pair == 0)
                def _():
                    score(late, late_head(k), now)

                @pl.when(pair > 0)
                def _():
                    score(late, late_head(k), now)
                    fold_late(late_head(k - 1), before)
                    store_head(late_head(k - 1))
            else:
                score(late, late_head(k), now)
                fold_late(late_head(k - 1), before)
                store_head(late_head(k - 1))

    fold_late(late_head(heads - 1), buffers[1])
    store_head(late_head(heads - 1))

    @pl.loop(0, heads)
    def _(j):
        for r in range(GROUP):
            store_out(j * GROUP + r).wait()

        @pl.when(sends_up(j))
        def _():
            send_up(j).wait_send()

        @pl.when(either(right_ahead(j), both(below, j < express)))
        def _():
            send_right(j).wait_send()

        @pl.when(both(crosses1, j >= express))
        def _():
            send_cross1(j).wait_send()

        @pl.when(both(crosses3, j >= express))
        def _():
            send_cross3(j).wait_send()

        @pl.when(either(left_ahead(j), relays(j)))
        def _():
            send_left(j).wait_send()

        @pl.when(has1)
        def _():
            send_side(SIDE1, j, BACK1).wait_send()

        @pl.when(has2)
        def _():
            send_side(SIDE2, j, BACK2).wait_send()

        @pl.when(has3)
        def _():
            send_side(SIDE3, j, BACK3).wait_send()

        @pl.when(either(c == 0, relays_extra))
        def _():
            send_extra(j).wait_send()

        @pl.when(both(sends_next, j < from_left))
        def _():
            send_next(j).wait_send()

        @pl.when(both(descends, j > half))
        def _():
            send_down(j).wait_send()

        @pl.when(either(both(rounds, j < half), turns_on(j)))
        def _():
            send_round(j).wait_send()

        @pl.when(both(sends_prev, j >= from_right))
        def _():
            send_prev(j).wait_send()


def shards(sections, queries, keys, values, doc_ids):
    rows, heads = queries.shape[0], keys.shape[1] // HEAD_DIM
    docs = doc_ids.reshape(-1, LANES)
    return pl.pallas_call(
        functools.partial(attention_kernel, sections, rows, heads),
        out_shape=jax.ShapeDtypeStruct(queries.shape, jnp.bfloat16),
        in_specs=[pl.BlockSpec(memory_space=pltpu.HBM)] * 4,
        out_specs=pl.BlockSpec(memory_space=pl.ANY),
        scratch_shapes=[
            pltpu.VMEM((BLOCKS, heads, 2, rows, HEAD_DIM), jnp.bfloat16),
            pltpu.VMEM((heads * GROUP, rows, HEAD_DIM), jnp.bfloat16),
            pltpu.VMEM((RELAY, LANES, rows), jnp.bfloat16),
            pltpu.VMEM((rows, LANES), jnp.bfloat16),
            pltpu.VMEM((24, LANES), jnp.int32),
            pltpu.VMEM((heads, GROUP, rows, LANES), jnp.float32),
            pltpu.VMEM((heads, GROUP, rows, 2 * HEAD_DIM), jnp.float32),
            pltpu.VMEM((heads * GROUP, rows, HEAD_DIM), jnp.bfloat16),
            pltpu.VMEM((GROUP * rows, 6 * rows), jnp.float32),
            pltpu.VMEM((GROUP * rows, 6 * rows), jnp.float32),
            pltpu.SemaphoreType.DMA((KINDS, heads)),
            pltpu.SemaphoreType.DMA((BLOCKS, heads)),
            pltpu.SemaphoreType.DMA((heads * GROUP,)),
            pltpu.SemaphoreType.DMA((2, heads)),
            pltpu.SemaphoreType.DMA((3,)),
            pltpu.SemaphoreType.DMA((heads * GROUP,)),
        ],
        compiler_params=pltpu.CompilerParams(
            collective_id=0, has_side_effects=True, vmem_limit_bytes=40 * 1024 * 1024
        ),
    )(*[pltpu.with_memory_space_constraint(a, pltpu.HBM) for a in (queries, keys, values, docs)])


def solution(mesh):
    placed = P(("section", "attn"), None)
    return jax.shard_map(
        functools.partial(shards, mesh.shape["section"]),
        mesh=mesh,
        in_specs=(placed, placed, placed, P()),
        out_specs=placed,
        check_vma=False,
    )
```

```python
import functools
import math

import jax
import jax.numpy as jnp
from jax import lax
from jax.experimental import pallas as pl
from jax.experimental.pallas import tpu as pltpu
from jax.sharding import PartitionSpec as P

MESH = pl.DeviceIdType.MESH
HEAD_DIM = 128
GROUP = 3
RING = 4
LANES = 128
NEG = -1e30

OWN, EXTRA, BACK1, BACK2, BACK3, RELAY, RELAY2 = 0, 1, 2, 4, 6, 8, 9
BLOCKS = 10
UP, RIGHT, LEFT, NEXT, PREV, SIDE_EXTRA, SIDE1, SIDE2, SIDE3, ROUND, CROSS1, CROSS3, DOWN = range(13)
KINDS = 13


def attention_kernel(
    sections, rows, heads,
    q_hbm, k_hbm, v_hbm, docs_hbm, out_hbm,
    kv, q, onehot, away, docs, stat_max, acc, out, held0, held1,
    send_sem, recv_sem, q_sem, kv_sem, doc_sem, out_sem,
):
    half = heads // 2
    scale = math.log2(math.e) * HEAD_DIM ** (-0.5)
    s = lax.axis_index("section")
    c = lax.axis_index("attn")
    x = lax.rem(s, RING)
    row_start = s - x
    first, last = x == 0, x == RING - 1
    top, bottom = s < RING, s >= sections - RING
    below = jnp.logical_not(top)
    crossing = jnp.logical_and(lax.rem(s, RING * RING) < RING, below)
    before_crossing = lax.rem(s, RING * RING) >= RING * (RING - 1)
    from_left = jnp.where(
        x == 2, jnp.where(bottom, heads - 2, jnp.where(before_crossing, half + 1, half)), half
    )
    from_right = jnp.where(jnp.logical_and(first, crossing), half + 1, half)
    express = heads - 2

    right = row_start + lax.rem(x + 1, RING)
    left = row_start + lax.rem(x + RING - 1, RING)
    up = lax.rem(s + RING, sections)
    down = lax.rem(s + sections - RING, sections)
    following = lax.rem(s + 1, sections)
    previous = lax.rem(s + sections - 1, sections)
    other = 1 - c
    up_core = jnp.where(first, other, c)

    def load_kv(j):
        at = pl.ds(pl.multiple_of(j * HEAD_DIM, HEAD_DIM), HEAD_DIM)
        return (
            pltpu.make_async_copy(k_hbm.at[:, at], kv.at[OWN, j, 0], kv_sem.at[0, j]),
            pltpu.make_async_copy(v_hbm.at[:, at], kv.at[OWN, j, 1], kv_sem.at[1, j]),
        )

    def load_q(h):
        at = pl.ds(pl.multiple_of(h * HEAD_DIM, HEAD_DIM), HEAD_DIM)
        return pltpu.make_async_copy(q_hbm.at[:, at], q.at[h], q_sem.at[h])

    def load_docs(piece):
        pair = lax.rem(lax.div(s, 2) + sections // 2 - 2 + piece, sections // 2)
        return pltpu.make_async_copy(
            docs_hbm.at[pl.ds(pl.multiple_of(pair * 8, 8), 8), :],
            docs.at[pl.ds(piece * 8, 8), :],
            doc_sem.at[piece],
        )

    @pl.loop(0, heads)
    def _(j):
        for copy in load_kv(j):
            copy.start()

    for piece in range(3):
        load_docs(piece).start()

    @pl.when(top)
    def _():
        @pl.loop(EXTRA, RELAY)
        def _(block):
            @pl.loop(0, heads)
            def _(j):
                kv[block, j] = jnp.zeros((2, rows, HEAD_DIM), kv.dtype)

    up_open = jnp.logical_not(bottom)
    down_open = below

    barrier = pltpu.get_barrier_semaphore()

    def greet(section, core):
        pl.semaphore_signal(barrier, inc=1, device_id=(section, core), device_id_type=MESH)

    greet(s, other)
    greet(right, c)
    greet(left, c)
    @pl.when(up_open)
    def _():
        greet(up, up_core)

    @pl.when(down_open)
    def _():
        greet(down, up_core)

    from_next = jnp.logical_and(last, up_open)
    to_previous = jnp.logical_and(first, down_open)

    @pl.when(to_previous)
    def _():
        greet(previous, c)
        greet(down, c)

    @pl.when(jnp.logical_and(first, up_open))
    def _():
        greet(up, c)

    @pl.when(from_next)
    def _():
        greet(following, c)

    @pl.loop(0, heads * GROUP)
    def _(h):
        load_q(h).start()

    def send(kind, j, source, target, section, core):
        return pltpu.make_async_remote_copy(
            src_ref=kv.at[source, j],
            dst_ref=kv.at[target, j],
            send_sem=send_sem.at[kind, j],
            recv_sem=recv_sem.at[target, j],
            device_id=(section, core),
            device_id_type=MESH,
        )

    def arrived(block, j):
        send(UP, j, block, block, s, other).wait_recv()

    up_target = jnp.where(first, EXTRA, RELAY)
    def send_up(j):
        return send(UP, j, OWN, up_target, up, up_core)

    def send_right(j):
        ahead = jnp.logical_and(last, j >= express)
        source = jnp.where(jnp.logical_and(last, j < express), RELAY, OWN)
        return send(RIGHT, j, source, jnp.where(ahead, RELAY, BACK1 + c), right, c)

    def send_left(j):
        own = jnp.logical_or(jnp.logical_or(first, top), j >= express)
        ahead = jnp.logical_and(own, x > 0)
        source = jnp.where(own, OWN, RELAY)
        return send(LEFT, j, source, jnp.where(ahead, RELAY2, BACK3 + c), left, c)

    def send_cross1(j):
        return send(CROSS1, j, RELAY, BACK1 + c, up, c)

    def send_cross3(j):
        return send(CROSS3, j, RELAY2, BACK3 + c, up, c)

    def send_next(j):
        target = jnp.where(last, RELAY2, BACK2 + c)
        return send(NEXT, j, BACK1 + c, target, jnp.where(last, up, following), c)

    def send_round(j):
        return send(ROUND, j, RELAY2, BACK2 + c, jnp.where(first, left, right), c)

    def send_prev(j):
        around = jnp.logical_and(first, crossing)
        target = jnp.where(around, RELAY2, BACK2 + c)
        return send(PREV, j, BACK3 + c, target, jnp.where(around, left, previous), c)

    def send_down(j):
        return send(DOWN, j, RELAY2, BACK2 + c, down, c)

    def send_extra(j):
        return send(SIDE_EXTRA, j, jnp.where(c == 0, OWN, RELAY), EXTRA, s, other)

    def send_side(kind, j, block):
        return send(kind, j, block + c, block + c, s, other)

    def both(*conditions):
        return functools.reduce(jnp.logical_and, conditions)

    def either(*conditions):
        return functools.reduce(jnp.logical_or, conditions)

    def sends_up(j):
        return both(up_open, either(c == 1, both(x > 0, j < express)))

    def right_ahead(j):
        return either(jnp.logical_not(last), both(up_open, j >= express))

    def left_ahead(j):
        return either(
            first,
            both(x > 0, either(up_open, x == 1), j >= express),
            both(top, x == 1, j >= half),
        )

    def relays(j):
        return both(x > 0, below, j < express)

    crosses1 = both(first, up_open)
    crosses3 = both(jnp.logical_not(last), up_open)
    descends = both(last, crossing)

    def turns_on(j):
        return both(first, either(both(top, j >= half), both(bottom, j >= express)))

    has1 = either(below, x > 0)
    has2 = either(below, x > 1)
    has3 = either(below, last)

    def has_extra():
        return either(c == 1, below)

    relays_extra = both(x > 0, below, c == 1)
    sends_next = both(has1, jnp.logical_not(both(bottom, last)))
    sends_prev = either(both(below, s != RING), last)

    @pl.loop(0, heads)
    def _(j):
        for copy in load_kv(j):
            copy.wait()

    pl.semaphore_wait(
        barrier,
        3
        + jnp.where(from_next, 1, 0)
        + jnp.where(to_previous, 2, 0)
        + jnp.where(jnp.logical_and(first, up_open), 1, 0)
        + jnp.where(up_open, 1, 0) + jnp.where(down_open, 1, 0),
    )

    @pl.loop(0, heads)
    def _(j):
        @pl.when(sends_up(j))
        def _():
            send_up(j).start()

        @pl.when(right_ahead(j))
        def _():
            send_right(j).start()

        @pl.when(left_ahead(j))
        def _():
            send_left(j).start()

        @pl.when(c == 0)
        def _():
            send_extra(j).start()

    for piece in range(3):
        load_docs(piece).wait()
    parity = lax.rem(s, 2)
    pieces = rows // LANES
    places = ((0, c), (4 * other, other), (1, 0), (1, 1), (2, 0), (2, 1), (3, 0), (3, 1))
    ids = lax.broadcasted_iota(jnp.int32, (LANES, LANES), 0)
    for block, (back, core) in enumerate(places):
        for piece in range(pieces):
            row = (4 + parity - back) * (2 * pieces) + core * pieces + piece
            same = jnp.where(docs[pl.ds(row, 1), :] == ids, 1.0, 0.0)
            span = slice(piece * LANES, (piece + 1) * LANES)
            onehot[block, :, span] = same.astype(jnp.bfloat16)
            if block == OWN:
                away[span, :] = jnp.transpose((1.0 - same) * NEG).astype(jnp.bfloat16)

    @pl.loop(0, heads * GROUP)
    def _(h):
        load_q(h).wait()

    def keys_of(block, j):
        return jnp.concatenate([jnp.transpose(kv[block, j, 0]), onehot[block]], axis=0)

    def scores(query, key):
        return jnp.dot(query, key, preferred_element_type=jnp.float32)

    def wide(column):
        return jnp.concatenate([column] * (rows // LANES), axis=1)

    def values_of(block, j):
        value = kv[block, j, 1]
        return jnp.concatenate([value, jnp.ones_like(value)], axis=1)

    def query_of(j, r):
        return jnp.concatenate([q[j * GROUP + r], away[...]], axis=1)

    def weigh(parts, top, blocks, j):
        total = None
        for part, block in zip(parts, blocks):
            weights = jnp.exp2((part - top) * scale).astype(jnp.bfloat16)
            product = jnp.dot(weights, values_of(block, j), preferred_element_type=jnp.float32)
            total = product if total is None else total + product
        return total

    early = (OWN, EXTRA, BACK1, BACK1 + 1, BACK3, BACK3 + 1)
    late = (BACK2, BACK2 + 1)
    causal = lax.broadcasted_iota(jnp.int32, (rows, rows), 1) <= lax.broadcasted_iota(
        jnp.int32, (rows, rows), 0
    )

    def row_max(parts):
        return jnp.broadcast_to(
            jnp.max(functools.reduce(jnp.maximum, parts), axis=1, keepdims=True), (rows, LANES)
        )

    def finish_late(j, r, parts):
        old = stat_max[j, r]
        top = jnp.maximum(old, row_max(parts))
        rescale = jnp.exp2((old - top) * scale)
        summed = acc[j, r] * wide(rescale) + weigh(parts, wide(top), late, j)
        out[j * GROUP + r] = (summed[:, :HEAD_DIM] / summed[:, HEAD_DIM:]).astype(jnp.bfloat16)

    def finish_early(j, r, parts):
        parts[0] = jnp.where(causal, parts[0], NEG)
        top = row_max(parts)
        stat_max[j, r] = top
        acc[j, r] = weigh(parts, wide(top), early, j)

    def score(blocks, j, held):
        query = jnp.concatenate([query_of(j, r) for r in range(GROUP)], axis=0)
        for at, block in enumerate(blocks):
            held[:, at * rows:(at + 1) * rows] = scores(query, keys_of(block, j))

    def parts_of(blocks, r, held):
        return [
            held[r * rows:(r + 1) * rows, at * rows:(at + 1) * rows] for at in range(len(blocks))
        ]

    def fold_early(j, held):
        for r in range(GROUP):
            finish_early(j, r, parts_of(early, r, held))

    def fold_late(j, held):
        for r in range(GROUP):
            finish_late(j, r, parts_of(late, r, held))

    def store_out(h):
        at = pl.ds(pl.multiple_of(h * HEAD_DIM, HEAD_DIM), HEAD_DIM)
        return pltpu.make_async_copy(out.at[h], out_hbm.at[:, at], out_sem.at[h])

    def pass_relay(j):
        @pl.when(relays(j))
        def _():
            arrived(RELAY, j)
            send_left(j).start()

        @pl.when(both(relays_extra, j >= express))
        def _():
            arrived(RELAY, j)

        @pl.when(both(last, relays(j)))
        def _():
            send_right(j).start()

        @pl.when(relays_extra)
        def _():
            send_extra(j).start()

    def pass_across(j):
        @pl.when(crosses3)
        def _():
            arrived(RELAY2, j)
            send_cross3(j).start()

        @pl.when(crosses1)
        def _():
            arrived(RELAY, j)
            send_cross1(j).start()

    def pass_aside(j):
        @pl.when(has1)
        def _():
            arrived(BACK1 + c, j)
            send_side(SIDE1, j, BACK1).start()

        @pl.when(has3)
        def _():
            arrived(BACK3 + c, j)
            send_side(SIDE3, j, BACK3).start()

    def next_range(step):
        in_pairs = step < heads
        low = jnp.where(in_pairs, 2 * (step - (heads - 3)), step - 2)
        high = jnp.minimum(low + jnp.where(in_pairs, 2, 1), from_left)
        return both(sends_next, step >= heads - 3, step <= heads + 1), low, high

    rounds = both(last, below)

    def pass_round(j):
        @pl.when(either(j < express, bottom))
        def _():
            arrived(RELAY2, j)

        send_round(j).start()

    def pass_down(j):
        arrived(RELAY2, j)
        send_down(j).start()

    def early_ready(j):
        @pl.when(has_extra())
        def _():
            arrived(EXTRA, j)

        @pl.when(has1)
        def _():
            arrived(BACK1 + other, j)

        @pl.when(has3)
        def _():
            arrived(BACK3 + other, j)

    def move(step):
        @pl.when(step < heads)
        def _():
            pass_relay(step)

        @pl.when(both(step >= 2, step < heads + 2))
        def _():
            pass_aside(step - 2)

        sending, low, high = next_range(step)

        @pl.when(sending)
        def _():
            @pl.loop(low, high)
            def _(j):
                send_next(j).start()

        @pl.when(both(sends_prev, step >= from_right + 2, step < heads + 2))
        def _():
            send_prev(step - 2).start()

        @pl.when(step == 2)
        def _():
            for j in range(express, heads):
                pass_across(j)

        @pl.when(both(turns_on(step), step < heads))
        def _():
            pass_round(step)

        @pl.when(both(rounds, step >= heads))
        def _():
            pass_round(step - heads)

        @pl.when(both(descends, step > heads + 1))
        def _():
            pass_down(half + step - (heads + 1))

    buffers = (held0, held1)

    @pl.loop(0, (heads + 4) // 2)
    def _(pair):
        for side in range(2):
            step = 2 * pair + side
            now, before = buffers[side], buffers[1 - side]
            move(step)

            @pl.when(both(step >= 3, step < heads + 3))
            def _():
                early_ready(step - 3)

            @pl.when(step == 3)
            def _():
                score(early, step - 3, now)

            @pl.when(both(step > 3, step < heads + 3))
            def _():
                score(early, step - 3, now)
                fold_early(step - 4, before)

            @pl.when(step == heads + 3)
            def _():
                fold_early(step - 4, before)

    def late_head(k):
        odd = lax.rem(k, 2)
        evenly = half * odd + lax.div(k, 2)
        turned = jnp.where(k < 2, k, jnp.where(k < 4, express + k - 2, k - 2))
        mixed = jnp.where(odd == 1, half + 1 + lax.div(k - 3, 2), lax.div(k, 2) + 1)
        delayed = jnp.where(k < 3, k, mixed)
        waits_down = both(last, up_open, before_crossing)
        return jnp.where(both(bottom, last), turned, jnp.where(waits_down, delayed, evenly))

    def pass_late(k):
        @pl.when(has2)
        def _():
            j = late_head(k)
            arrived(BACK2 + c, j)
            send_side(SIDE2, j, BACK2).start()

    def late_ready(k):
        @pl.when(has2)
        def _():
            arrived(BACK2 + other, late_head(k))

    def move_late(k):
        @pl.when(both(descends, k == 0))
        def _():
            pass_down(heads - 1)

        @pl.when(k + 1 < heads)
        def _():
            pass_late(k + 1)

    def store_head(j):
        for r in range(GROUP):
            store_out(j * GROUP + r).start()

    pass_late(0)

    @pl.loop(0, heads // 2)
    def _(pair):
        for side in range(2):
            k = 2 * pair + side
            now, before = buffers[side], buffers[1 - side]
            move_late(k)
            late_ready(k)

            if side == 0:
                @pl.when(pair == 0)
                def _():
                    score(late, late_head(k), now)

                @pl.when(pair > 0)
                def _():
                    score(late, late_head(k), now)
                    fold_late(late_head(k - 1), before)
                    store_head(late_head(k - 1))
            else:
                score(late, late_head(k), now)
                fold_late(late_head(k - 1), before)
                store_head(late_head(k - 1))

    fold_late(late_head(heads - 1), buffers[1])
    store_head(late_head(heads - 1))

    @pl.loop(0, heads)
    def _(j):
        for r in range(GROUP):
            store_out(j * GROUP + r).wait()

        @pl.when(sends_up(j))
        def _():
            send_up(j).wait_send()

        @pl.when(either(right_ahead(j), both(below, j < express)))
        def _():
            send_right(j).wait_send()

        @pl.when(both(crosses1, j >= express))
        def _():
            send_cross1(j).wait_send()

        @pl.when(both(crosses3, j >= express))
        def _():
            send_cross3(j).wait_send()

        @pl.when(either(left_ahead(j), relays(j)))
        def _():
            send_left(j).wait_send()

        @pl.when(has1)
        def _():
            send_side(SIDE1, j, BACK1).wait_send()

        @pl.when(has2)
        def _():
            send_side(SIDE2, j, BACK2).wait_send()

        @pl.when(has3)
        def _():
            send_side(SIDE3, j, BACK3).wait_send()

        @pl.when(either(c == 0, relays_extra))
        def _():
            send_extra(j).wait_send()

        @pl.when(both(sends_next, j < from_left))
        def _():
            send_next(j).wait_send()

        @pl.when(both(descends, j > half))
        def _():
            send_down(j).wait_send()

        @pl.when(either(both(rounds, j < half), turns_on(j)))
        def _():
            send_round(j).wait_send()

        @pl.when(both(sends_prev, j >= from_right))
        def _():
            send_prev(j).wait_send()


def shards(sections, queries, keys, values, doc_ids):
    rows, heads = queries.shape[0], keys.shape[1] // HEAD_DIM
    docs = doc_ids.reshape(-1, LANES)
    return pl.pallas_call(
        functools.partial(attention_kernel, sections, rows, heads),
        out_shape=jax.ShapeDtypeStruct(queries.shape, jnp.bfloat16),
        in_specs=[pl.BlockSpec(memory_space=pltpu.HBM)] * 4,
        out_specs=pl.BlockSpec(memory_space=pl.ANY),
        scratch_shapes=[
            pltpu.VMEM((BLOCKS, heads, 2, rows, HEAD_DIM), jnp.bfloat16),
            pltpu.VMEM((heads * GROUP, rows, HEAD_DIM), jnp.bfloat16),
            pltpu.VMEM((RELAY, LANES, rows), jnp.bfloat16),
            pltpu.VMEM((rows, LANES), jnp.bfloat16),
            pltpu.VMEM((24, LANES), jnp.int32),
            pltpu.VMEM((heads, GROUP, rows, LANES), jnp.float32),
            pltpu.VMEM((heads, GROUP, rows, 2 * HEAD_DIM), jnp.float32),
            pltpu.VMEM((heads * GROUP, rows, HEAD_DIM), jnp.bfloat16),
            pltpu.VMEM((GROUP * rows, 6 * rows), jnp.float32),
            pltpu.VMEM((GROUP * rows, 6 * rows), jnp.float32),
            pltpu.SemaphoreType.DMA((KINDS, heads)),
            pltpu.SemaphoreType.DMA((BLOCKS, heads)),
            pltpu.SemaphoreType.DMA((heads * GROUP,)),
            pltpu.SemaphoreType.DMA((2, heads)),
            pltpu.SemaphoreType.DMA((3,)),
            pltpu.SemaphoreType.DMA((heads * GROUP,)),
        ],
        compiler_params=pltpu.CompilerParams(
            collective_id=0, has_side_effects=True, vmem_limit_bytes=40 * 1024 * 1024
        ),
    )(*[pltpu.with_memory_space_constraint(a, pltpu.HBM) for a in (queries, keys, values, docs)])


def solution(mesh):
    placed = P(("section", "attn"), None)
    return jax.shard_map(
        functools.partial(shards, mesh.shape["section"]),
        mesh=mesh,
        in_specs=(placed, placed, placed, P()),
        out_specs=placed,
        check_vma=False,
    )
```

```python
import functools
import math

import jax
import jax.numpy as jnp
from jax import lax
from jax.experimental import pallas as pl
from jax.experimental.pallas import tpu as pltpu
from jax.sharding import PartitionSpec as P

MESH = pl.DeviceIdType.MESH
HEAD_DIM = 128
GROUP = 3
RING = 4
LANES = 128
NEG = -1e30

OWN, EXTRA, BACK1, BACK2, BACK3, RELAY, RELAY2 = 0, 1, 2, 4, 6, 8, 9
BLOCKS = 10
UP, RIGHT, LEFT, NEXT, PREV, SIDE_EXTRA, SIDE1, SIDE2, SIDE3, ROUND, CROSS1, CROSS3, DOWN = range(13)
KINDS = 13


def attention_kernel(
    sections, rows, heads,
    q_hbm, k_hbm, v_hbm, docs_hbm, out_hbm,
    kv, q, onehot, away, docs, stat_max, acc, out, held0, held1,
    send_sem, recv_sem, q_sem, kv_sem, doc_sem, out_sem,
):
    half = heads // 2
    scale = math.log2(math.e) * HEAD_DIM ** (-0.5)
    s = lax.axis_index("section")
    c = lax.axis_index("attn")
    x = lax.rem(s, RING)
    row_start = s - x
    first, last = x == 0, x == RING - 1
    top, bottom = s < RING, s >= sections - RING
    below = jnp.logical_not(top)
    crossing = jnp.logical_and(lax.rem(s, RING * RING) < RING, below)
    before_crossing = lax.rem(s, RING * RING) >= RING * (RING - 1)
    from_left = jnp.where(
        x == 2, jnp.where(bottom, heads - 2, jnp.where(before_crossing, half + 1, half)), half
    )
    from_right = jnp.where(jnp.logical_and(first, crossing), half + 1, half)
    express = heads - 2

    right = row_start + lax.rem(x + 1, RING)
    left = row_start + lax.rem(x + RING - 1, RING)
    up = lax.rem(s + RING, sections)
    down = lax.rem(s + sections - RING, sections)
    following = lax.rem(s + 1, sections)
    previous = lax.rem(s + sections - 1, sections)
    other = 1 - c
    up_core = jnp.where(first, other, c)

    def load_kv(j):
        at = pl.ds(pl.multiple_of(j * HEAD_DIM, HEAD_DIM), HEAD_DIM)
        return (
            pltpu.make_async_copy(k_hbm.at[:, at], kv.at[OWN, j, 0], kv_sem.at[0, j]),
            pltpu.make_async_copy(v_hbm.at[:, at], kv.at[OWN, j, 1], kv_sem.at[1, j]),
        )

    def load_q(h):
        at = pl.ds(pl.multiple_of(h * HEAD_DIM, HEAD_DIM), HEAD_DIM)
        return pltpu.make_async_copy(q_hbm.at[:, at], q.at[h], q_sem.at[h])

    def load_docs(piece):
        pair = lax.rem(lax.div(s, 2) + sections // 2 - 2 + piece, sections // 2)
        return pltpu.make_async_copy(
            docs_hbm.at[pl.ds(pl.multiple_of(pair * 8, 8), 8), :],
            docs.at[pl.ds(piece * 8, 8), :],
            doc_sem.at[piece],
        )

    @pl.loop(0, heads)
    def _(j):
        for copy in load_kv(j):
            copy.start()

    for piece in range(3):
        load_docs(piece).start()

    @pl.when(top)
    def _():
        @pl.loop(EXTRA, RELAY)
        def _(block):
            @pl.loop(0, heads)
            def _(j):
                kv[block, j] = jnp.zeros((2, rows, HEAD_DIM), kv.dtype)

    up_open = jnp.logical_not(bottom)
    down_open = below

    barrier = pltpu.get_barrier_semaphore()

    def greet(section, core):
        pl.semaphore_signal(barrier, inc=1, device_id=(section, core), device_id_type=MESH)

    greet(s, other)
    greet(right, c)
    greet(left, c)
    @pl.when(up_open)
    def _():
        greet(up, up_core)

    @pl.when(down_open)
    def _():
        greet(down, up_core)

    from_next = jnp.logical_and(last, up_open)
    to_previous = jnp.logical_and(first, down_open)

    @pl.when(to_previous)
    def _():
        greet(previous, c)
        greet(down, c)

    @pl.when(jnp.logical_and(first, up_open))
    def _():
        greet(up, c)

    @pl.when(from_next)
    def _():
        greet(following, c)

    @pl.loop(0, heads * GROUP)
    def _(h):
        load_q(h).start()

    def send(kind, j, source, target, section, core):
        return pltpu.make_async_remote_copy(
            src_ref=kv.at[source, j],
            dst_ref=kv.at[target, j],
            send_sem=send_sem.at[kind, j],
            recv_sem=recv_sem.at[target, j],
            device_id=(section, core),
            device_id_type=MESH,
        )

    def arrived(block, j):
        send(UP, j, block, block, s, other).wait_recv()

    up_target = jnp.where(first, EXTRA, RELAY)
    def send_up(j):
        return send(UP, j, OWN, up_target, up, up_core)

    def send_right(j):
        ahead = jnp.logical_and(last, j >= express)
        source = jnp.where(jnp.logical_and(last, j < express), RELAY, OWN)
        return send(RIGHT, j, source, jnp.where(ahead, RELAY, BACK1 + c), right, c)

    def send_left(j):
        own = jnp.logical_or(jnp.logical_or(first, top), j >= express)
        ahead = jnp.logical_and(own, x > 0)
        source = jnp.where(own, OWN, RELAY)
        return send(LEFT, j, source, jnp.where(ahead, RELAY2, BACK3 + c), left, c)

    def send_cross1(j):
        return send(CROSS1, j, RELAY, BACK1 + c, up, c)

    def send_cross3(j):
        return send(CROSS3, j, RELAY2, BACK3 + c, up, c)

    def send_next(j):
        target = jnp.where(last, RELAY2, BACK2 + c)
        return send(NEXT, j, BACK1 + c, target, jnp.where(last, up, following), c)

    def send_round(j):
        return send(ROUND, j, RELAY2, BACK2 + c, jnp.where(first, left, right), c)

    def send_prev(j):
        around = jnp.logical_and(first, crossing)
        target = jnp.where(around, RELAY2, BACK2 + c)
        return send(PREV, j, BACK3 + c, target, jnp.where(around, left, previous), c)

    def send_down(j):
        return send(DOWN, j, RELAY2, BACK2 + c, down, c)

    def send_extra(j):
        return send(SIDE_EXTRA, j, jnp.where(c == 0, OWN, RELAY), EXTRA, s, other)

    def send_side(kind, j, block):
        return send(kind, j, block + c, block + c, s, other)

    def both(*conditions):
        return functools.reduce(jnp.logical_and, conditions)

    def either(*conditions):
        return functools.reduce(jnp.logical_or, conditions)

    def sends_up(j):
        return both(up_open, either(c == 1, both(x > 0, j < express)))

    def right_ahead(j):
        return either(jnp.logical_not(last), both(up_open, j >= express))

    def left_ahead(j):
        return either(
            first,
            both(x > 0, either(up_open, x == 1), j >= express),
            both(top, x == 1, j >= half),
        )

    def relays(j):
        return both(x > 0, below, j < express)

    crosses1 = both(first, up_open)
    crosses3 = both(jnp.logical_not(last), up_open)
    descends = both(last, crossing)

    def turns_on(j):
        return both(first, either(both(top, j >= half), both(bottom, j >= express)))

    has1 = either(below, x > 0)
    has2 = either(below, x > 1)
    has3 = either(below, last)

    def has_extra():
        return either(c == 1, below)

    relays_extra = both(x > 0, below, c == 1)
    sends_next = both(has1, jnp.logical_not(both(bottom, last)))
    sends_prev = either(both(below, s != RING), last)

    @pl.loop(0, heads)
    def _(j):
        for copy in load_kv(j):
            copy.wait()

    pl.semaphore_wait(
        barrier,
        3
        + jnp.where(from_next, 1, 0)
        + jnp.where(to_previous, 2, 0)
        + jnp.where(jnp.logical_and(first, up_open), 1, 0)
        + jnp.where(up_open, 1, 0) + jnp.where(down_open, 1, 0),
    )

    @pl.loop(0, heads)
    def _(j):
        @pl.when(sends_up(j))
        def _():
            send_up(j).start()

        @pl.when(right_ahead(j))
        def _():
            send_right(j).start()

        @pl.when(left_ahead(j))
        def _():
            send_left(j).start()

        @pl.when(c == 0)
        def _():
            send_extra(j).start()

    for piece in range(3):
        load_docs(piece).wait()
    parity = lax.rem(s, 2)
    pieces = rows // LANES
    places = ((0, c), (4 * other, other), (1, 0), (1, 1), (2, 0), (2, 1), (3, 0), (3, 1))
    ids = lax.broadcasted_iota(jnp.int32, (LANES, LANES), 0)
    for block, (back, core) in enumerate(places):
        for piece in range(pieces):
            row = (4 + parity - back) * (2 * pieces) + core * pieces + piece
            same = jnp.where(docs[pl.ds(row, 1), :] == ids, 1.0, 0.0)
            span = slice(piece * LANES, (piece + 1) * LANES)
            onehot[block, :, span] = same.astype(jnp.bfloat16)
            if block == OWN:
                away[span, :] = jnp.transpose((1.0 - same) * NEG).astype(jnp.bfloat16)

    @pl.loop(0, heads * GROUP)
    def _(h):
        load_q(h).wait()

    def keys_of(block, j):
        return jnp.concatenate([jnp.transpose(kv[block, j, 0]), onehot[block]], axis=0)

    def scores(query, key):
        return jnp.dot(query, key, preferred_element_type=jnp.float32)

    def wide(column):
        return jnp.concatenate([column] * (rows // LANES), axis=1)

    def values_of(block, j):
        value = kv[block, j, 1]
        return jnp.concatenate([value, jnp.ones_like(value)], axis=1)

    def query_of(j, r):
        return jnp.concatenate([q[j * GROUP + r], away[...]], axis=1)

    def weigh(parts, top, blocks, j):
        total = None
        for part, block in zip(parts, blocks):
            weights = jnp.exp2((part - top) * scale).astype(jnp.bfloat16)
            product = jnp.dot(weights, values_of(block, j), preferred_element_type=jnp.float32)
            total = product if total is None else total + product
        return total

    early = (OWN, EXTRA, BACK1, BACK1 + 1, BACK3, BACK3 + 1)
    late = (BACK2, BACK2 + 1)
    causal = lax.broadcasted_iota(jnp.int32, (rows, rows), 1) <= lax.broadcasted_iota(
        jnp.int32, (rows, rows), 0
    )

    def row_max(parts):
        return jnp.broadcast_to(
            jnp.max(functools.reduce(jnp.maximum, parts), axis=1, keepdims=True), (rows, LANES)
        )

    def finish_late(j, r, parts):
        old = stat_max[j, r]
        top = jnp.maximum(old, row_max(parts))
        rescale = jnp.exp2((old - top) * scale)
        summed = acc[j, r] * wide(rescale) + weigh(parts, wide(top), late, j)
        out[j * GROUP + r] = (summed[:, :HEAD_DIM] / summed[:, HEAD_DIM:]).astype(jnp.bfloat16)

    def finish_early(j, r, parts):
        parts[0] = jnp.where(causal, parts[0], NEG)
        top = row_max(parts)
        stat_max[j, r] = top
        acc[j, r] = weigh(parts, wide(top), early, j)

    def score(blocks, j, held):
        query = jnp.concatenate([query_of(j, r) for r in range(GROUP)], axis=0)
        for at, block in enumerate(blocks):
            held[:, at * rows:(at + 1) * rows] = scores(query, keys_of(block, j))

    def parts_of(blocks, r, held):
        return [
            held[r * rows:(r + 1) * rows, at * rows:(at + 1) * rows] for at in range(len(blocks))
        ]

    def fold_early(j, held):
        for r in range(GROUP):
            finish_early(j, r, parts_of(early, r, held))

    def fold_late(j, held):
        for r in range(GROUP):
            finish_late(j, r, parts_of(late, r, held))

    def store_out(h):
        at = pl.ds(pl.multiple_of(h * HEAD_DIM, HEAD_DIM), HEAD_DIM)
        return pltpu.make_async_copy(out.at[h], out_hbm.at[:, at], out_sem.at[h])

    def pass_relay(j):
        @pl.when(relays(j))
        def _():
            arrived(RELAY, j)
            send_left(j).start()

        @pl.when(both(relays_extra, j >= express))
        def _():
            arrived(RELAY, j)

        @pl.when(both(last, relays(j)))
        def _():
            send_right(j).start()

        @pl.when(relays_extra)
        def _():
            send_extra(j).start()

    def pass_across(j):
        @pl.when(crosses3)
        def _():
            arrived(RELAY2, j)
            send_cross3(j).start()

        @pl.when(crosses1)
        def _():
            arrived(RELAY, j)
            send_cross1(j).start()

    def pass_aside(j):
        @pl.when(has1)
        def _():
            arrived(BACK1 + c, j)
            send_side(SIDE1, j, BACK1).start()

        @pl.when(has3)
        def _():
            arrived(BACK3 + c, j)
            send_side(SIDE3, j, BACK3).start()

    def next_range(step):
        in_pairs = step < heads
        low = jnp.where(in_pairs, 2 * (step - (heads - 3)), step - 2)
        high = jnp.minimum(low + jnp.where(in_pairs, 2, 1), from_left)
        return both(sends_next, step >= heads - 3, step <= heads + 1), low, high

    rounds = both(last, below)

    def pass_round(j):
        @pl.when(either(j < express, bottom))
        def _():
            arrived(RELAY2, j)

        send_round(j).start()

    def pass_down(j):
        arrived(RELAY2, j)
        send_down(j).start()

    def early_ready(j):
        @pl.when(has_extra())
        def _():
            arrived(EXTRA, j)

        @pl.when(has1)
        def _():
            arrived(BACK1 + other, j)

        @pl.when(has3)
        def _():
            arrived(BACK3 + other, j)

    def move(step):
        @pl.when(step < heads)
        def _():
            pass_relay(step)

        @pl.when(both(step >= 2, step < heads + 2))
        def _():
            pass_aside(step - 2)

        sending, low, high = next_range(step)

        @pl.when(sending)
        def _():
            @pl.loop(low, high)
            def _(j):
                send_next(j).start()

        @pl.when(both(sends_prev, step >= from_right + 2, step < heads + 2))
        def _():
            send_prev(step - 2).start()

        @pl.when(step == 2)
        def _():
            for j in range(express, heads):
                pass_across(j)

        @pl.when(both(turns_on(step), step < heads))
        def _():
            pass_round(step)

        @pl.when(both(rounds, step >= heads))
        def _():
            pass_round(step - heads)

        @pl.when(both(descends, step > heads, step < heads + 3))
        def _():
            pass_down(half + step - heads)

    buffers = (held0, held1)

    @pl.loop(0, (heads + 4) // 2)
    def _(pair):
        for side in range(2):
            step = 2 * pair + side
            now, before = buffers[side], buffers[1 - side]
            move(step)

            @pl.when(both(step >= 3, step < heads + 3))
            def _():
                early_ready(step - 3)

            @pl.when(step == 3)
            def _():
                score(early, step - 3, now)

            @pl.when(both(step > 3, step < heads + 3))
            def _():
                score(early, step - 3, now)
                fold_early(step - 4, before)

            @pl.when(step == heads + 3)
            def _():
                fold_early(step - 4, before)

    def late_head(k):
        odd = lax.rem(k, 2)
        evenly = half * odd + lax.div(k, 2)
        turned = jnp.where(k < 2, k, jnp.where(k < 4, express + k - 2, k - 2))
        mixed = jnp.where(odd == 1, half + 1 + lax.div(k - 3, 2), lax.div(k, 2) + 1)
        delayed = jnp.where(k < 3, k, mixed)
        waits_down = both(last, up_open, before_crossing)
        return jnp.where(both(bottom, last), turned, jnp.where(waits_down, delayed, evenly))

    def pass_late(k):
        @pl.when(has2)
        def _():
            j = late_head(k)
            arrived(BACK2 + c, j)
            send_side(SIDE2, j, BACK2).start()

    def late_ready(k):
        @pl.when(has2)
        def _():
            arrived(BACK2 + other, late_head(k))

    def move_late(k):
        @pl.when(both(descends, k == 0))
        def _():
            pass_down(heads - 1)

        @pl.when(k + 1 < heads)
        def _():
            pass_late(k + 1)

    def store_head(j):
        for r in range(GROUP):
            store_out(j * GROUP + r).start()

    pass_late(0)

    @pl.loop(0, heads // 2)
    def _(pair):
        for side in range(2):
            k = 2 * pair + side
            now, before = buffers[side], buffers[1 - side]
            move_late(k)
            late_ready(k)

            if side == 0:
                @pl.when(pair == 0)
                def _():
                    score(late, late_head(k), now)

                @pl.when(pair > 0)
                def _():
                    score(late, late_head(k), now)
                    fold_late(late_head(k - 1), before)
                    store_head(late_head(k - 1))
            else:
                score(late, late_head(k), now)
                fold_late(late_head(k - 1), before)
                store_head(late_head(k - 1))

    fold_late(late_head(heads - 1), buffers[1])
    store_head(late_head(heads - 1))

    @pl.loop(0, heads)
    def _(j):
        for r in range(GROUP):
            store_out(j * GROUP + r).wait()

        @pl.when(sends_up(j))
        def _():
            send_up(j).wait_send()

        @pl.when(either(right_ahead(j), both(below, j < express)))
        def _():
            send_right(j).wait_send()

        @pl.when(both(crosses1, j >= express))
        def _():
            send_cross1(j).wait_send()

        @pl.when(both(crosses3, j >= express))
        def _():
            send_cross3(j).wait_send()

        @pl.when(either(left_ahead(j), relays(j)))
        def _():
            send_left(j).wait_send()

        @pl.when(has1)
        def _():
            send_side(SIDE1, j, BACK1).wait_send()

        @pl.when(has2)
        def _():
            send_side(SIDE2, j, BACK2).wait_send()

        @pl.when(has3)
        def _():
            send_side(SIDE3, j, BACK3).wait_send()

        @pl.when(either(c == 0, relays_extra))
        def _():
            send_extra(j).wait_send()

        @pl.when(both(sends_next, j < from_left))
        def _():
            send_next(j).wait_send()

        @pl.when(both(descends, j > half))
        def _():
            send_down(j).wait_send()

        @pl.when(either(both(rounds, j < half), turns_on(j)))
        def _():
            send_round(j).wait_send()

        @pl.when(both(sends_prev, j >= from_right))
        def _():
            send_prev(j).wait_send()


def shards(sections, queries, keys, values, doc_ids):
    rows, heads = queries.shape[0], keys.shape[1] // HEAD_DIM
    docs = doc_ids.reshape(-1, LANES)
    return pl.pallas_call(
        functools.partial(attention_kernel, sections, rows, heads),
        out_shape=jax.ShapeDtypeStruct(queries.shape, jnp.bfloat16),
        in_specs=[pl.BlockSpec(memory_space=pltpu.HBM)] * 4,
        out_specs=pl.BlockSpec(memory_space=pl.ANY),
        scratch_shapes=[
            pltpu.VMEM((BLOCKS, heads, 2, rows, HEAD_DIM), jnp.bfloat16),
            pltpu.VMEM((heads * GROUP, rows, HEAD_DIM), jnp.bfloat16),
            pltpu.VMEM((RELAY, LANES, rows), jnp.bfloat16),
            pltpu.VMEM((rows, LANES), jnp.bfloat16),
            pltpu.VMEM((24, LANES), jnp.int32),
            pltpu.VMEM((heads, GROUP, rows, LANES), jnp.float32),
            pltpu.VMEM((heads, GROUP, rows, 2 * HEAD_DIM), jnp.float32),
            pltpu.VMEM((heads * GROUP, rows, HEAD_DIM), jnp.bfloat16),
            pltpu.VMEM((GROUP * rows, 6 * rows), jnp.float32),
            pltpu.VMEM((GROUP * rows, 6 * rows), jnp.float32),
            pltpu.SemaphoreType.DMA((KINDS, heads)),
            pltpu.SemaphoreType.DMA((BLOCKS, heads)),
            pltpu.SemaphoreType.DMA((heads * GROUP,)),
            pltpu.SemaphoreType.DMA((2, heads)),
            pltpu.SemaphoreType.DMA((3,)),
            pltpu.SemaphoreType.DMA((heads * GROUP,)),
        ],
        compiler_params=pltpu.CompilerParams(
            collective_id=0, has_side_effects=True, vmem_limit_bytes=40 * 1024 * 1024
        ),
    )(*[pltpu.with_memory_space_constraint(a, pltpu.HBM) for a in (queries, keys, values, docs)])


def solution(mesh):
    placed = P(("section", "attn"), None)
    return jax.shard_map(
        functools.partial(shards, mesh.shape["section"]),
        mesh=mesh,
        in_specs=(placed, placed, placed, P()),
        out_specs=placed,
        check_vma=False,
    )
```
